32 devices in a mesh: dp: 8 (over z, x), expert: 4 (over y, core).
Axes of the slice: x: 2, y: 2, z: 4, core: 2. Of those that a mesh axis runs over, the one named last changes fastest.
Arguments:
- patches: bfloat16 [16384, 768], P(('dp', 'expert')), may hold values from -6 to 6
- time_embed: bfloat16 [64, 768], P(('dp', 'expert')), may hold values from -6 to 6
- ada_weight: bfloat16 [768, 4608], replicated, may hold values from -0.21875 to 0.21875
- ada_bias: float32 [4608], replicated, may hold values from -3 to 3
- qkv_weight: bfloat16 [768, 2304], replicated, may hold values from -0.21875 to 0.21875
- out_weight: bfloat16 [768, 768], replicated, may hold values from -0.875 to 0.875
- up_weight: bfloat16 [768, 3072], replicated, may hold values from -0.21875 to 0.21875
- down_weight: bfloat16 [3072, 768], replicated, may hold values from -0.109375 to 0.109375
- expert_up: bfloat16 [4, 768, 3072], P('expert'), may hold values from -0.21875 to 0.21875
- expert_down: bfloat16 [4, 3072, 768], P('expert'), may hold values from -0.109375 to 0.109375
- routes: int32 [16384, 2], P(('dp', 'expert')), may hold values from 0 to 3, as said below
- gate_weights: float32 [16384, 2], P(('dp', 'expert')), may hold values from 0.2 to 0.8
- cotangent: bfloat16 [16384, 768], P(('dp', 'expert')), may hold values from -21 to 21
Outputs:
- block_out: bfloat16 [16384, 768], P(('dp', 'expert'))
- grad_input: float32 [16384, 768], P(('dp', 'expert'))
- grad_ada: float32 [768, 4608], P('dp')
- grad_ada_bias: float32 [4608], P('dp')
- grad_qkv: float32 [768, 2304], P('dp')
- grad_out_proj: float32 [768, 768], P('dp')
- grad_up: float32 [768, 3072], P('dp')
- grad_down: float32 [3072, 768], P('dp')
- grad_expert_up: float32 [4, 768, 3072], P('expert', 'dp')
- grad_expert_down: float32 [4, 3072, 768], P('expert', 'dp')
- counts: int32 [4], replicated
The draws below stay inside these ranges and needn't reach their ends.
Inputs may be any that keep to these rules, and one draw needn't show every extreme that they name: `routes`: each patch names two different experts.
All inputs are finite; a program needn't handle non-finite values.
Results may differ from the reference program's by a relative error of at most 0.019.
The reference program's roundings to bfloat16 on the way count: a program that leaves them out, or rounds other values in their place, can miss the bound.
Values may be sent and summed in bfloat16 or wider, within the bound.
No kernel may reach another device: no remote copies, remote signals or barrier semaphores. Data moves between devices by JAX's collectives and lax.ppermute only.
A program may use at most 256 MiB of HBM per device.

```python
import math
import jax
import jax.numpy as jnp
from jax import lax

D = 768
HEADS = 12
HEAD_DIM = 64
FF = 3072
EFF = 3072
SEQ_LEN = 256
TOK_DEV = 512
EXPERTS = 4
CAP = 320
LATENTS = 64
TOKENS = 16384


def draw_routes(key, part):
    sources = TOKENS // TOK_DEV
    key_coin, key_first, key_step = jax.random.split(key, 3)
    block_index = jnp.arange(TOKENS, dtype=jnp.int32) // TOK_DEV
    favoured = block_index * EXPERTS // sources
    coin = jax.random.randint(key_coin, (TOKENS,), 0, 2, dtype=jnp.int32)
    uniform_first = jax.random.randint(key_first, (TOKENS,), 0, EXPERTS, dtype=jnp.int32)
    first_route = jnp.where(coin == 1, favoured, uniform_first).astype(jnp.int32)
    offset = jax.random.randint(key_step, (TOKENS,), 1, EXPERTS, dtype=jnp.int32)
    second_route = ((first_route + offset) % EXPERTS).astype(jnp.int32)
    return jnp.stack([first_route, second_route], axis=1).astype(jnp.int32)


def draw_cotangent(key, part):
    positions = jnp.arange(TOKENS, dtype=jnp.float32)
    growth = jnp.exp(math.log(3.0) * positions / max(TOKENS - 1, 1))[:, None]
    values = jnp.clip(jax.random.normal(key, (TOKENS, D), jnp.float32), -6.0, 6.0) * growth
    return values.astype(jnp.bfloat16)


def level_of(stream_key, shape, shards, smallest, largest):
    loudness, own = 1.0, jax.random.fold_in(stream_key, 6)
    for dim, parts in shards:
        draws = jnp.exp(jax.random.uniform(jax.random.fold_in(own, dim), (parts,), jnp.float32, smallest / len(shards), largest / len(shards)))
        loudness = loudness * jnp.repeat(draws, shape[dim] // parts).reshape([-1 if axis == dim else 1 for axis in range(len(shape))])
    return loudness


def bell_draw(own_key, extent, width, most, cuts=(), kind=jnp.bfloat16):
    values = jax.random.normal(own_key, extent, jnp.float32) * width
    if len(cuts) > 0:
        values = level_of(own_key, extent, cuts, -0.22, 0.18) * values
    return jnp.clip(values, min=-most, max=most).astype(kind)


def setup_inputs(seed: int = 0) -> dict:
    arg_keys = jax.random.split(jax.random.key(seed), 14)
    patches = bell_draw(arg_keys[0], (TOKENS, D), 1.0, 6.0, ((0, 32),))
    time_embed = bell_draw(arg_keys[1], (LATENTS, D), 1.0, 6.0, ((0, 32),))
    ada_weight = bell_draw(arg_keys[2], (D, 6 * D), D ** -0.5, 0.21875)
    ada_bias = bell_draw(arg_keys[3], (6 * D,), 0.5, 3.0, (), jnp.float32)
    qkv_weight = bell_draw(arg_keys[4], (D, 3 * D), D ** -0.5, 0.21875)
    out_weight = bell_draw(arg_keys[5], (D, D), (D // 16) ** -0.5, 0.875)
    up_weight = bell_draw(arg_keys[6], (D, FF), D ** -0.5, 0.21875)
    down_weight = bell_draw(arg_keys[7], (FF, D), FF ** -0.5, 0.109375)
    expert_up = bell_draw(arg_keys[8], (EXPERTS, D, EFF), D ** -0.5, 0.21875, ((0, 4),))
    expert_down = bell_draw(arg_keys[9], (EXPERTS, EFF, D), EFF ** -0.5, 0.109375, ((0, 4),))
    routes = draw_routes(jax.random.fold_in(arg_keys[13], 71), 0)
    gate_weights = jnp.clip(0.2 + 0.6 * jax.random.uniform(arg_keys[11], (TOKENS, 2), jnp.float32) ** level_of(arg_keys[11], (TOKENS, 2), ((0, 32),), -0.2, 0.2), 0.2, 0.8)
    cotangent = draw_cotangent(jax.random.fold_in(arg_keys[13], 71), 0)
    return dict(patches=patches, time_embed=time_embed, ada_weight=ada_weight, ada_bias=ada_bias, qkv_weight=qkv_weight, out_weight=out_weight, up_weight=up_weight, down_weight=down_weight, expert_up=expert_up, expert_down=expert_down, routes=routes, gate_weights=gate_weights, cotangent=cotangent)


@jax.custom_vjp
def low(v):
    return lax.optimization_barrier(v.astype(jnp.bfloat16)).astype(jnp.float32)

@jax.custom_vjp
def low_back(v):
    return v

def low_keep(v):
    return (low(v), None)

def low_pass(kept, grad):
    return (grad,)

def back_keep(v):
    return (v, None)

def back_low(kept, grad):
    return (low(grad),)
low.defvjp(low_keep, low_pass)
low_back.defvjp(back_keep, back_low)

def layer_norm(values_in):
    row_mean = lax.optimization_barrier(jnp.mean(values_in, axis=-1, keepdims=True))
    centered = values_in - row_mean
    row_var = lax.optimization_barrier(jnp.mean(centered * centered, axis=-1, keepdims=True))
    return centered * lax.rsqrt(row_var + 1e-06)

def modulate(values_in, shift_part, scale_part):
    return layer_norm(values_in) * (1.0 + scale_part[:, None, :]) + shift_part[:, None, :]

def gelu_tanh(values_in):
    return jax.nn.gelu(values_in, approximate=True)

def attend_group(triple):
    queries, keys_all, values_all = triple
    scores = low_back(jnp.einsum('gqhd,gkhd->ghqk', queries, keys_all, precision=lax.Precision.HIGHEST) * HEAD_DIM ** (-0.5))
    attn_probs = jax.nn.softmax(scores, axis=-1)
    return jnp.einsum('ghqk,gkhd->gqhd', low(attn_probs), values_all, precision=lax.Precision.HIGHEST)

def slot_table(routes):
    sources = TOKENS // TOK_DEV
    flat_routes = routes.reshape(sources, TOK_DEV * 2).astype(jnp.int32)
    expert_hot = (flat_routes[:, :, None] == jnp.arange(EXPERTS, dtype=jnp.int32)[None, None, :]).astype(jnp.int32)
    earlier = jnp.cumsum(expert_hot, axis=1) - expert_hot
    slot_index = lax.optimization_barrier(jnp.sum(earlier * expert_hot, axis=2)).astype(jnp.int32)
    destination = jnp.where(slot_index < CAP, flat_routes * CAP + slot_index, EXPERTS * CAP).astype(jnp.int32)
    token_index = jnp.broadcast_to((jnp.arange(TOK_DEV * 2, dtype=jnp.int32) // 2)[None, :], destination.shape)
    source_index = jnp.broadcast_to(jnp.arange(sources, dtype=jnp.int32)[:, None], destination.shape)
    owner_table = jnp.full((sources, EXPERTS * CAP + 1), TOK_DEV, dtype=jnp.int32)
    owner_table = owner_table.at[source_index, destination].set(token_index)
    counts = lax.optimization_barrier(jnp.sum(expert_hot, axis=(0, 1))).astype(jnp.int32)
    return (destination.reshape(sources, TOK_DEV, 2), owner_table[:, :EXPERTS * CAP], counts)

def pick_rows(block_rows, row_index):
    return jnp.take(block_rows, row_index, axis=0)

def routed_mixture(second_in, expert_up, expert_down, gate_values, destination, owner_table):
    sources = TOKENS // TOK_DEV
    blocks = second_in.reshape(sources, TOK_DEV, D)
    padded = jnp.concatenate([blocks, jnp.zeros((sources, 1, D), blocks.dtype)], axis=1)
    gathered = jax.vmap(pick_rows)(padded, owner_table)
    expert_rows = gathered.reshape(sources, EXPERTS, CAP, D).transpose(1, 0, 2, 3).reshape(EXPERTS, sources * CAP, D)
    expert_rows = low_back(expert_rows)
    expert_pre = low_back(jnp.einsum('erd,edf->erf', expert_rows, expert_up, precision=lax.Precision.HIGHEST))
    expert_act = low(gelu_tanh(expert_pre))
    expert_out = low_back(low(jnp.einsum('erf,efd->erd', expert_act, expert_down, precision=lax.Precision.HIGHEST)))
    returned = expert_out.reshape(EXPERTS, sources, CAP, D).transpose(1, 0, 2, 3).reshape(sources, EXPERTS * CAP, D)
    returned = jnp.concatenate([returned, jnp.zeros((sources, 1, D), returned.dtype)], axis=1)
    first_pick = jax.vmap(pick_rows)(returned, destination[:, :, 0])
    second_pick = jax.vmap(pick_rows)(returned, destination[:, :, 1])
    weights_in = gate_values.reshape(sources, TOK_DEV, 2)
    mixture = weights_in[:, :, 0:1] * first_pick + weights_in[:, :, 1:2] * second_pick
    return mixture.reshape(TOKENS, D)

def forward(patches, ada_weight, ada_bias, qkv_weight, out_weight, up_weight, down_weight, expert_up, expert_down, cond_act, gate_values, destination, owner_table):
    highest = lax.Precision.HIGHEST
    modulation = jnp.dot(cond_act, ada_weight, precision=highest) + ada_bias
    shift_one, scale_one, gate_one, shift_two, scale_two, gate_two = jnp.split(modulation, 6, axis=1)
    sequences = patches.reshape(LATENTS, SEQ_LEN, D)
    first_in = low(modulate(sequences, shift_one, scale_one)).reshape(TOKENS, D)
    qkv_all = low(low_back(jnp.dot(first_in, qkv_weight, precision=highest)))
    group_size = math.gcd(LATENTS, 16)

    def split_heads(column_start):
        return qkv_all[:, column_start:column_start + D].reshape(LATENTS // group_size, group_size, SEQ_LEN, HEADS, HEAD_DIM)
    attended = lax.map(jax.checkpoint(attend_group), (split_heads(0), split_heads(D), split_heads(2 * D)))
    attended = low_back(low(attended.reshape(TOKENS, D)))
    attn_proj = low_back(jnp.dot(attended, out_weight, precision=highest))
    middle = sequences + gate_one[:, None, :] * attn_proj.reshape(LATENTS, SEQ_LEN, D)
    second_in = low(modulate(middle, shift_two, scale_two)).reshape(TOKENS, D)
    shared_pre = low_back(jnp.dot(second_in, up_weight, precision=highest))
    shared_act = low(gelu_tanh(shared_pre))
    shared_out = low_back(jnp.dot(shared_act, down_weight, precision=highest))
    mixture = routed_mixture(second_in, expert_up, expert_down, gate_values, destination, owner_table)
    branch = (shared_out + mixture).reshape(LATENTS, SEQ_LEN, D)
    return (middle + gate_two[:, None, :] * branch).reshape(TOKENS, D)

def reference(patches, time_embed, ada_weight, ada_bias, qkv_weight, out_weight, up_weight, down_weight, expert_up, expert_down, routes, gate_weights, cotangent):
    destination, owner_table, counts = slot_table(routes)
    cond_act = low(jax.nn.silu(time_embed.astype(jnp.float32)))
    gate_values = gate_weights.astype(jnp.float32)

    def closed(inputs_in, ada_matrix, ada_offset, qkv_matrix, out_matrix, up_matrix, down_matrix, expert_up_in, expert_down_in):
        return forward(inputs_in, ada_matrix, ada_offset, qkv_matrix, out_matrix, up_matrix, down_matrix, expert_up_in, expert_down_in, cond_act, gate_values, destination, owner_table)
    output, pullback = jax.vjp(closed, patches.astype(jnp.float32), ada_weight.astype(jnp.float32), ada_bias.astype(jnp.float32), qkv_weight.astype(jnp.float32), out_weight.astype(jnp.float32), up_weight.astype(jnp.float32), down_weight.astype(jnp.float32), expert_up.astype(jnp.float32), expert_down.astype(jnp.float32))
    gradients = pullback(cotangent.astype(jnp.float32))
    return (output.astype(jnp.bfloat16), gradients[0], gradients[1], gradients[2], gradients[3], gradients[4], gradients[5], gradients[6], gradients[7], gradients[8], counts)
```

```python
import math

import jax
import jax.numpy as jnp
from jax import lax
from jax.sharding import PartitionSpec as P

HEAD_DIM = 64


SQRT_TWO_OVER_PI = math.sqrt(2.0 / math.pi)


def layer_norm(values_in):
    row_mean = jnp.mean(values_in, axis=-1, keepdims=True)
    centered = values_in - row_mean
    row_var = jnp.mean(centered * centered, axis=-1, keepdims=True)
    return centered * lax.rsqrt(row_var + 1e-06)


def modulate(values_in, shift_part, scale_part):
    return layer_norm(values_in) * (1.0 + scale_part[:, None, :]) + shift_part[:, None, :]


def gelu_tanh(values_in):
    return jax.nn.gelu(values_in, approximate=True)


def gelu_slope(values_in):
    squared = values_in * values_in
    tanh_inner = jnp.tanh(SQRT_TWO_OVER_PI * (values_in + 0.044715 * squared * values_in))
    return 0.5 * (1.0 + tanh_inner) + 0.5 * values_in * (
        1.0 - tanh_inner * tanh_inner
    ) * SQRT_TWO_OVER_PI * (1.0 + 3.0 * 0.044715 * squared)


def contract_rows(left_in, right_in):
    return lax.dot_general(
        left_in, right_in, (((0,), (0,)), ((), ())), preferred_element_type=jnp.float32
    )


def project_back(left_in, right_in):
    return lax.dot_general(
        left_in, right_in, (((1,), (1,)), ((), ())), preferred_element_type=jnp.float32
    )


def bits_of(size):
    return size.bit_length() - 1


def label_of(index):
    upper = index >> 1
    return ((upper ^ (upper >> 1)) << 1) | (index & 1)


def index_of(label):
    upper = label >> 1
    shift = 1
    while shift < 32:
        upper = upper ^ (upper >> shift)
        shift *= 2
    return (upper << 1) | (label & 1)


def swap_dp(value, bit):
    size = lax.axis_size("dp")
    return lax.ppermute(
        value, "dp", [(i, index_of(label_of(i) ^ (1 << bit))) for i in range(size)]
    )


def swap_expert(value, bit):
    size = lax.axis_size("expert")
    return lax.ppermute(value, "expert", [(i, i ^ (1 << bit)) for i in range(size)])


def gather_expert(value):
    held = value[None]
    bits = bits_of(lax.axis_size("expert"))
    parts = {0: value}
    for bit in reversed(range(bits)):
        known = list(parts)
        for r in known:
            parts[r | (1 << bit)] = swap_expert(parts[r], bit)
    return jnp.stack([parts[r] for r in range(1 << bits)])


def gather_ordered(value):
    mine = lax.axis_index("expert")
    for bit in range(bits_of(lax.axis_size("expert"))):
        other = swap_expert(value, bit)
        upper = (mine >> bit & 1) == 1
        value = jnp.concatenate(
            [jnp.where(upper, other, value), jnp.where(upper, value, other)], axis=0
        )
    return value


def scatter_expert(parts):
    for bit in range(bits_of(lax.axis_size("expert"))):
        kept = {}
        for r, value in parts.items():
            if r >> bit & 1:
                continue
            other = swap_expert(parts[r | (1 << bit)].astype(jnp.bfloat16), bit)
            kept[r] = value.astype(jnp.float32) + other.astype(jnp.float32)
        parts = kept
    return parts[0]


def gather_dp(value):
    for bit in range(bits_of(lax.axis_size("dp"))):
        value = jnp.concatenate([value, swap_dp(value, bit)], axis=0)
    return value


def scatter_dp(shards, order):
    for bit in order:
        low = [r for r in sorted(shards) if not r >> bit & 1]
        away = jnp.stack([shards[r | (1 << bit)] for r in low])
        came = swap_dp(away, bit)
        shards = {
            r: (shards[r].astype(jnp.float32) + came[i].astype(jnp.float32)).astype(jnp.bfloat16)
            for i, r in enumerate(low)
        }
    return shards[0]


def relative_shards(matrix, size):
    mine = label_of(lax.axis_index("dp"))
    rows = matrix.shape[0] // size
    return {
        r: lax.dynamic_slice_in_dim(matrix, index_of(mine ^ r) * rows, rows, axis=0)
        for r in range(size)
    }


def orders(size):
    bits = bits_of(size)
    return [[(start + step) % bits for step in range(bits)] for start in range(bits)]


def sum_over_dp(matrix, order):
    size = lax.axis_size("dp")
    return scatter_dp(relative_shards(matrix.astype(jnp.bfloat16), size), order)


def sum_over_all(matrix, order):
    core = lax.axis_index("expert") & 1
    half = matrix.shape[1] // 2
    low = matrix.astype(jnp.bfloat16)
    mine = lax.dynamic_slice_in_dim(low, core * half, half, axis=1)
    other = lax.dynamic_slice_in_dim(low, (1 - core) * half, half, axis=1)
    mine = (mine.astype(jnp.float32) + swap_expert(other, 0).astype(jnp.float32)).astype(
        jnp.bfloat16
    )
    total = sum_over_dp(mine, order)
    for bit in range(1, bits_of(lax.axis_size("expert"))):
        total = (
            total.astype(jnp.float32) + swap_expert(total, bit).astype(jnp.float32)
        ).astype(jnp.bfloat16)
    opposite = swap_expert(total, 0)
    first = jnp.where(core == 0, total, opposite)
    second = jnp.where(core == 0, opposite, total)
    return jnp.concatenate([first, second], axis=1).astype(jnp.float32)


def on_device(
    patches,
    time_embed,
    ada_weight,
    ada_bias,
    qkv_weight,
    out_weight,
    up_weight,
    down_weight,
    expert_up,
    expert_down,
    routes,
    gate_weights,
    cotangent,
):
    tokens, model_width = patches.shape
    latents = time_embed.shape[0]
    seq_len = tokens // latents
    head_count = model_width // HEAD_DIM
    experts = lax.axis_size("expert")
    dp_size = lax.axis_size("dp")
    dp_index = lax.axis_index("dp")
    expert_index = lax.axis_index("expert")
    capacity = 5 * tokens // (2 * experts)
    scale_factor = HEAD_DIM ** (-0.5)
    turn = orders(dp_size)

    routes_all = gather_expert(routes.T)
    gates_all = gather_expert(gate_weights.T)
    time_group = gather_expert(time_embed).reshape(experts * latents, model_width)
    cot_all = gather_expert(cotangent)
    time_all = gather_dp(gather_ordered(time_embed))

    named = routes_all == expert_index
    member = jnp.any(named, axis=1)
    gate_here = jnp.sum(jnp.where(named, gates_all, 0.0), axis=1)
    position = jnp.arange(tokens, dtype=jnp.int32)
    before = (position[:, None] < position[None, :]).astype(jnp.bfloat16)
    slot = jnp.dot(
        member.astype(jnp.bfloat16), before, preferred_element_type=jnp.float32
    ).astype(jnp.int32)
    slot = jnp.where(member, slot, capacity)
    pick = (
        slot[:, None, :] == jnp.arange(capacity, dtype=jnp.int32)[None, :, None]
    ).astype(jnp.bfloat16)
    local_counts = jnp.sum(
        (routes[:, :, None] == jnp.arange(experts, dtype=jnp.int32)).astype(jnp.int32),
        axis=(0, 1),
    )

    cond_group = jax.nn.silu(time_group.astype(jnp.float32)).astype(jnp.bfloat16)
    mod_group = jnp.dot(cond_group, ada_weight, preferred_element_type=jnp.float32) + ada_bias
    modulation = mod_group[:latents]
    shift_one, scale_one, gate_one, shift_two, scale_two, gate_two = jnp.split(
        modulation, 6, axis=1
    )
    gate_two_group = mod_group[:, 5 * model_width :].reshape(experts, latents, 1, model_width)
    residual_in = patches.astype(jnp.float32).reshape(latents, seq_len, model_width)
    first_full, first_pull = jax.vjp(modulate, residual_in, shift_one, scale_one)
    first_in = first_full.reshape(tokens, model_width).astype(jnp.bfloat16)
    qkv_all = jnp.dot(first_in, qkv_weight, preferred_element_type=jnp.float32).astype(jnp.bfloat16)
    head_shape = (latents, seq_len, head_count, HEAD_DIM)
    queries = qkv_all[:, :model_width].reshape(head_shape)
    keys_all = qkv_all[:, model_width : 2 * model_width].reshape(head_shape)
    values_all = qkv_all[:, 2 * model_width :].reshape(head_shape)
    scores = (
        jnp.einsum("bqhd,bkhd->bhqk", queries, keys_all, preferred_element_type=jnp.float32)
        * scale_factor
    )
    row_peak = jnp.max(scores, axis=-1, keepdims=True)
    shifted_exp = jnp.exp(scores - row_peak)
    row_total = jnp.sum(shifted_exp, axis=-1, keepdims=True)
    log_total = row_peak + jnp.log(row_total)
    probs_low = (shifted_exp / row_total).astype(jnp.bfloat16)
    attended = jnp.einsum(
        "bhqk,bkhd->bqhd", probs_low, values_all, preferred_element_type=jnp.float32
    )
    attended = attended.reshape(tokens, model_width).astype(jnp.bfloat16)
    attn_proj = jnp.dot(attended, out_weight, preferred_element_type=jnp.float32).reshape(
        latents, seq_len, model_width
    )
    middle = residual_in + gate_one[:, None, :] * attn_proj
    second_full, second_pull = jax.vjp(modulate, middle, shift_two, scale_two)
    second_in = second_full.reshape(tokens, model_width).astype(jnp.bfloat16)
    second_all = gather_expert(second_in)

    shared_pre = jnp.dot(second_in, up_weight, preferred_element_type=jnp.float32)
    shared_act = gelu_tanh(shared_pre).astype(jnp.bfloat16)
    shared_out = jnp.dot(shared_act, down_weight, preferred_element_type=jnp.float32)
    grad_result = cotangent.astype(jnp.float32).reshape(latents, seq_len, model_width)
    grad_branch = (gate_two[:, None, :] * grad_result).reshape(tokens, model_width)
    grad_shared = grad_branch.astype(jnp.bfloat16)
    grad_w_down = contract_rows(shared_act, grad_shared)
    sum_w_down = sum_over_all(grad_w_down, turn[0])
    grad_shared_act = project_back(grad_shared, down_weight)
    grad_shared_pre = (grad_shared_act * gelu_slope(shared_pre)).astype(jnp.bfloat16)
    grad_w_up = contract_rows(second_in, grad_shared_pre)
    sum_w_up = sum_over_all(grad_w_up, turn[1])
    grad_second = project_back(grad_shared_pre, up_weight)

    up_matrix = expert_up[0]
    down_matrix = expert_down[0]
    grad_branch_all = (
        gate_two_group
        * cot_all.astype(jnp.float32).reshape(experts, latents, seq_len, model_width)
    ).reshape(experts, tokens, model_width)
    grad_pair_all = (gate_here[:, :, None] * grad_branch_all).astype(jnp.bfloat16)

    def to_slots(values_in):
        return (
            jnp.einsum("bct,btd->bcd", pick, values_in, preferred_element_type=jnp.float32)
            .astype(jnp.bfloat16)
            .reshape(experts * capacity, model_width)
        )

    def to_tokens(values_in):
        return jnp.einsum(
            "bct,bcd->btd",
            pick,
            values_in.reshape(experts, capacity, model_width),
            preferred_element_type=jnp.float32,
        )

    grad_rows_out = to_slots(grad_pair_all)
    rows_in = to_slots(second_all)
    pre_act = jnp.dot(rows_in, up_matrix, preferred_element_type=jnp.float32)
    act_rows = gelu_tanh(pre_act).astype(jnp.bfloat16)
    grad_e_act = project_back(grad_rows_out, down_matrix)
    grad_e_pre = (grad_e_act * gelu_slope(pre_act)).astype(jnp.bfloat16)
    grad_e_up = contract_rows(rows_in, grad_e_pre)
    sum_e_up = sum_over_dp(grad_e_up, turn[2])
    grad_rows_in = project_back(grad_e_pre, up_matrix).astype(jnp.bfloat16)
    grad_tokens = to_tokens(grad_rows_in)
    grad_second = grad_second + scatter_expert({r: grad_tokens[r] for r in range(experts)})
    grad_e_down = contract_rows(act_rows, grad_rows_out)
    sum_e_down = sum_over_dp(grad_e_down, turn[0])
    out_rows = jnp.dot(act_rows, down_matrix, preferred_element_type=jnp.float32).astype(
        jnp.bfloat16
    )
    mixture_parts = gate_here[:, :, None] * to_tokens(out_rows)
    mixture = scatter_expert({r: mixture_parts[r] for r in range(experts)})

    branch = (shared_out + mixture).reshape(latents, seq_len, model_width)
    result = middle + gate_two[:, None, :] * branch
    block_out = result.reshape(tokens, model_width).astype(jnp.bfloat16)
    grad_gate_two = jnp.sum(grad_result * branch, axis=1)

    grad_mid_norm, grad_shift_two, grad_scale_two = second_pull(
        grad_second.reshape(latents, seq_len, model_width)
    )
    grad_middle = grad_result + grad_mid_norm
    grad_gate_one = jnp.sum(grad_middle * attn_proj, axis=1)
    grad_attn = (
        (gate_one[:, None, :] * grad_middle).reshape(tokens, model_width).astype(jnp.bfloat16)
    )
    grad_w_out = contract_rows(attended, grad_attn)
    sum_w_out = sum_over_all(grad_w_out, turn[1])
    grad_attended = project_back(grad_attn, out_weight).astype(jnp.bfloat16).reshape(head_shape)
    scores_again = (
        jnp.einsum("bqhd,bkhd->bhqk", queries, keys_all, preferred_element_type=jnp.float32)
        * scale_factor
    )
    attn_probs = jnp.exp(scores_again - log_total)
    probs_again = attn_probs.astype(jnp.bfloat16)
    grad_values = jnp.einsum(
        "bhqk,bqhd->bkhd", probs_again, grad_attended, preferred_element_type=jnp.float32
    )
    grad_probs = jnp.einsum(
        "bqhd,bkhd->bhqk", grad_attended, values_all, preferred_element_type=jnp.float32
    )
    grad_scores = (
        attn_probs * (grad_probs - jnp.sum(attn_probs * grad_probs, axis=-1, keepdims=True))
    ).astype(jnp.bfloat16)
    grad_queries = (
        jnp.einsum("bhqk,bkhd->bqhd", grad_scores, keys_all, preferred_element_type=jnp.float32)
        * scale_factor
    )
    grad_keys = (
        jnp.einsum("bhqk,bqhd->bkhd", grad_scores, queries, preferred_element_type=jnp.float32)
        * scale_factor
    )
    grad_qkv_rows = jnp.concatenate(
        [
            grad_queries.reshape(tokens, model_width),
            grad_keys.reshape(tokens, model_width),
            grad_values.reshape(tokens, model_width),
        ],
        axis=1,
    ).astype(jnp.bfloat16)
    grad_w_qkv = contract_rows(first_in, grad_qkv_rows)
    sum_w_qkv = sum_over_all(grad_w_qkv, turn[2])
    grad_first = project_back(grad_qkv_rows, qkv_weight)
    grad_in_norm, grad_shift_one, grad_scale_one = first_pull(
        grad_first.reshape(latents, seq_len, model_width)
    )
    grad_input = (grad_middle + grad_in_norm).reshape(tokens, model_width)

    count_parts = jnp.concatenate([local_counts // 128, local_counts % 128]).astype(jnp.bfloat16)
    count_rows = jnp.zeros((latents, 128), jnp.bfloat16).at[0, : 2 * experts].set(count_parts)
    early = jnp.concatenate(
        [
            grad_gate_one.astype(jnp.bfloat16),
            grad_shift_two.astype(jnp.bfloat16),
            grad_scale_two.astype(jnp.bfloat16),
            grad_gate_two.astype(jnp.bfloat16),
            count_rows,
        ],
        axis=1,
    )
    late = jnp.concatenate(
        [grad_shift_one.astype(jnp.bfloat16), grad_scale_one.astype(jnp.bfloat16)], axis=1
    )

    def gather_all(value):
        return gather_dp(gather_ordered(value))

    early_all = gather_all(early)
    late_all = gather_all(late)
    grad_mod_all = jnp.concatenate([late_all, early_all[:, : 4 * model_width]], axis=1)
    count_sums = jnp.sum(early_all[:, 4 * model_width :].astype(jnp.float32), axis=0).astype(
        jnp.int32
    )
    counts = count_sums[:experts] * 128 + count_sums[experts : 2 * experts]
    cond_all = jax.nn.silu(time_all.astype(jnp.float32)).astype(jnp.bfloat16)
    ada_rows = model_width // dp_size
    cond_mine = lax.dynamic_slice_in_dim(cond_all.T, dp_index * ada_rows, ada_rows, axis=0)
    sum_ada = jnp.dot(cond_mine, grad_mod_all, preferred_element_type=jnp.float32)
    bias_all = jnp.sum(grad_mod_all.astype(jnp.float32), axis=0)
    bias_size = bias_all.shape[0] // dp_size
    sum_bias = lax.dynamic_slice_in_dim(bias_all, dp_index * bias_size, bias_size)
    return (
        block_out,
        grad_input,
        sum_ada,
        sum_bias,
        sum_w_qkv,
        sum_w_out,
        sum_w_up,
        sum_w_down,
        sum_e_up.astype(jnp.float32)[None],
        sum_e_down.astype(jnp.float32)[None],
        counts,
    )


def solution(mesh):
    in_specs = (
        P(("dp", "expert"), None),
        P(("dp", "expert"), None),
        P(),
        P(),
        P(),
        P(),
        P(),
        P(),
        P("expert", None, None),
        P("expert", None, None),
        P(("dp", "expert"), None),
        P(("dp", "expert"), None),
        P(("dp", "expert"), None),
    )
    out_specs = (
        P(("dp", "expert"), None),
        P(("dp", "expert"), None),
        P("dp", None),
        P("dp"),
        P("dp", None),
        P("dp", None),
        P("dp", None),
        P("dp", None),
        P("expert", "dp", None),
        P("expert", "dp", None),
        P(),
    )
    return jax.shard_map(
        on_device, mesh=mesh, in_specs=in_specs, out_specs=out_specs, check_vma=False
    )
```

```python
import functools
import math

import jax
import jax.numpy as jnp
import numpy as np
from jax import lax
from jax.experimental import pallas as pl
from jax.experimental.pallas import tpu as pltpu
from jax.sharding import PartitionSpec as P

HEAD_DIM = 64
VMEM_BYTES = 56 << 20
PARTS = 3
SQRT_TWO_OVER_PI = math.sqrt(2.0 / math.pi)


def nt(a,b): return lax.dot_general(a,b,(((1,),(1,)),((),())),preferred_element_type=jnp.float32)
def nn(a,b): return lax.dot_general(a,b,(((1,),(0,)),((),())),preferred_element_type=jnp.float32)
def tn(a,b): return lax.dot_general(a,b,(((0,),(0,)),((),())),preferred_element_type=jnp.float32)

def normalized(values_in):
    row_mean = jnp.mean(values_in, axis=-1, keepdims=True)
    centered = values_in - row_mean
    row_var = jnp.mean(centered * centered, axis=-1, keepdims=True)
    inverse = lax.rsqrt(row_var + 1e-06)
    return centered * inverse, inverse

def norm_back(grad_out, scale, normal, inverse):
    inner = grad_out * (1.0 + scale)
    mean_inner = jnp.mean(inner, axis=-1, keepdims=True)
    mean_cross = jnp.mean(inner * normal, axis=-1, keepdims=True)
    return inverse * (inner - mean_inner - normal * mean_cross)

def head_lanes(pair, head):
    lane = lax.broadcasted_iota(jnp.int32, pair.shape, 1)
    return jnp.where(lane // HEAD_DIM == head, pair, jnp.zeros_like(pair))

def attn_forward_kernel(x_ref, mod_ref, wqkv_ref, wout_ref, first_ref, qkv_ref, lse_ref, att_ref, proj_ref, second_ref):
    width = x_ref.shape[1]
    x = x_ref[...].astype(jnp.float32)
    mod = mod_ref[0]
    normal, _ = normalized(x)
    first_ref[...] = (normal * (1.0 + mod[1:2]) + mod[0:1]).astype(jnp.bfloat16)
    qkv_ref[...] = nn(first_ref[...], wqkv_ref[...]).astype(jnp.bfloat16)
    lane = 2 * HEAD_DIM
    for pair in range(width // lane):
        q2 = qkv_ref[:, pair * lane : (pair + 1) * lane]
        k2 = qkv_ref[:, width + pair * lane : width + (pair + 1) * lane]
        v2 = qkv_ref[:, 2 * width + pair * lane : 2 * width + (pair + 1) * lane]
        v2t = v2.T
        outs = []
        for head in range(2):
            scores = nt(head_lanes(k2, head), q2) * HEAD_DIM ** (-0.5)
            peak = jnp.max(scores, axis=0, keepdims=True)
            powers = jnp.exp(scores - peak)
            total = jnp.sum(powers, axis=0, keepdims=True)
            lse_ref[0, 2 * pair + head : 2 * pair + head + 1, :] = peak + jnp.log(total)
            probs = (powers * (1.0 / total)).astype(jnp.bfloat16)
            outs.append(nn(v2t[head * HEAD_DIM : (head + 1) * HEAD_DIM], probs))
        both = jnp.concatenate(outs, axis=0).astype(jnp.bfloat16)
        att_ref[:, pair * lane : (pair + 1) * lane] = both.T
    proj = nn(att_ref[...], wout_ref[...])
    proj_ref[...] = proj
    middle = x + mod[2:3] * proj
    normal2, _ = normalized(middle)
    second_ref[...] = (normal2 * (1.0 + mod[4:5]) + mod[3:4]).astype(jnp.bfloat16)

def attn_forward(patches, mod, wqkv, wout):
    tokens, width = patches.shape
    latents = mod.shape[0]
    seq = tokens // latents
    heads = width // HEAD_DIM
    rows = lambda cols: pl.BlockSpec((seq, cols), lambda i: (i, 0))
    whole = lambda a: pl.BlockSpec(a.shape, lambda i: (0, 0), pipeline_mode=pl.Buffered(1))
    return pl.pallas_call(
        attn_forward_kernel, grid=(latents,),
        in_specs=[rows(width), pl.BlockSpec((1,) + mod.shape[1:], lambda i: (i, 0, 0)), whole(wqkv), whole(wout)],
        out_specs=[rows(width), rows(3 * width), pl.BlockSpec((1, heads, seq), lambda i: (i, 0, 0)), rows(width), rows(width), rows(width)],
        out_shape=[jax.ShapeDtypeStruct((tokens, width), jnp.bfloat16), jax.ShapeDtypeStruct((tokens, 3 * width), jnp.bfloat16),
            jax.ShapeDtypeStruct((latents, heads, seq), jnp.float32), jax.ShapeDtypeStruct((tokens, width), jnp.bfloat16),
            jax.ShapeDtypeStruct((tokens, width), jnp.float32), jax.ShapeDtypeStruct((tokens, width), jnp.bfloat16)],
        compiler_params=pltpu.CompilerParams(vmem_limit_bytes=VMEM_BYTES))(patches, mod, wqkv, wout)

def attn_backward_kernel(extra, x_ref, mod_ref, proj_ref, qkv_ref, lse_ref, cot_ref, wout_ref, *rest):
    adds = rest[:extra]
    gqkv_ref, gattn_ref, gmid_ref, gmod_ref = rest[extra:]
    width = x_ref.shape[1]
    x = x_ref[...].astype(jnp.float32)
    mod = mod_ref[0]
    proj = proj_ref[...]
    normal, inverse = normalized(x + mod[2:3] * proj)
    grad_second = adds[0][...].astype(jnp.float32)
    for a in adds[1:]:
        grad_second = grad_second + a[...].astype(jnp.float32)
    gmod_ref[0, 1:2, :] = jnp.sum(grad_second, axis=0, keepdims=True)
    gmod_ref[0, 2:3, :] = jnp.sum(grad_second * normal, axis=0, keepdims=True)
    grad_middle = cot_ref[...].astype(jnp.float32) + norm_back(grad_second, mod[4:5], normal, inverse)
    gmid_ref[...] = grad_middle
    gmod_ref[0, 0:1, :] = jnp.sum(grad_middle * proj, axis=0, keepdims=True)
    gattn_ref[...] = (mod[2:3] * grad_middle).astype(jnp.bfloat16)
    grad_att = nt(gattn_ref[...], wout_ref[...]).astype(jnp.bfloat16)
    lane = 2 * HEAD_DIM
    scale = HEAD_DIM ** (-0.5)
    for pair in range(width // lane):
        sl = slice(pair * lane, (pair + 1) * lane)
        q2 = qkv_ref[:, pair * lane : (pair + 1) * lane]
        k2 = qkv_ref[:, width + pair * lane : width + (pair + 1) * lane]
        v2 = qkv_ref[:, 2 * width + pair * lane : 2 * width + (pair + 1) * lane]
        do2 = grad_att[:, sl]
        k2t = k2.T
        gq, gk, gv = [], [], []
        for head in range(2):
            scores = nt(head_lanes(k2, head), q2) * scale
            probs = jnp.exp(scores - lse_ref[0, 2 * pair + head : 2 * pair + head + 1, :])
            grad_probs = nt(head_lanes(v2, head), do2)
            inner = jnp.sum(probs * grad_probs, axis=0, keepdims=True)
            grad_scores = (probs * (grad_probs - inner)).astype(jnp.bfloat16)
            gv.append(nn(probs.astype(jnp.bfloat16), do2))
            gk.append(nn(grad_scores, q2))
            gq.append(nn(k2t[head * HEAD_DIM : (head + 1) * HEAD_DIM], grad_scores))
        low = lax.broadcasted_iota(jnp.int32, gv[0].shape, 1) < HEAD_DIM
        gqt = (jnp.concatenate(gq, axis=0) * scale).astype(jnp.bfloat16)
        gqkv_ref[:, pair * lane : (pair + 1) * lane] = gqt.T
        gqkv_ref[:, width + pair * lane : width + (pair + 1) * lane] = (jnp.where(low, gk[0], gk[1]) * scale).astype(jnp.bfloat16)
        gqkv_ref[:, 2 * width + pair * lane : 2 * width + (pair + 1) * lane] = jnp.where(low, gv[0], gv[1]).astype(jnp.bfloat16)

def attn_backward(patches, mod, proj, qkv, lse, cot, wout, adds):
    tokens, width = patches.shape
    latents = mod.shape[0]
    seq = tokens // latents
    rows = lambda cols: pl.BlockSpec((seq, cols), lambda i: (i, 0))
    per = lambda a: pl.BlockSpec((1,) + a.shape[1:], lambda i: (i, 0, 0))
    whole = lambda a: pl.BlockSpec(a.shape, lambda i: (0, 0), pipeline_mode=pl.Buffered(1))
    return pl.pallas_call(
        functools.partial(attn_backward_kernel, len(adds)), grid=(latents,),
        in_specs=[rows(width), per(mod), rows(width), rows(3 * width), per(lse), rows(width), whole(wout)] + [rows(width)] * len(adds),
        out_specs=[rows(3 * width), rows(width), rows(width), pl.BlockSpec((1, 3, width), lambda i: (i, 0, 0))],
        out_shape=[jax.ShapeDtypeStruct((tokens, 3 * width), jnp.bfloat16), jax.ShapeDtypeStruct((tokens, width), jnp.bfloat16),
            jax.ShapeDtypeStruct((tokens, width), jnp.float32), jax.ShapeDtypeStruct((latents, 3, width), jnp.float32)],
        compiler_params=pltpu.CompilerParams(vmem_limit_bytes=VMEM_BYTES))(patches, mod, proj, qkv, lse, cot, wout, *adds)

def input_backward_kernel(x_ref, mod_ref, gqkv_ref, gmid_ref, wqkv_ref, gin_ref, gmod_ref):
    mod = mod_ref[0]
    normal, inverse = normalized(x_ref[...].astype(jnp.float32))
    grad_first = nt(gqkv_ref[...], wqkv_ref[...])
    gmod_ref[0, 0:1, :] = jnp.sum(grad_first, axis=0, keepdims=True)
    gmod_ref[0, 1:2, :] = jnp.sum(grad_first * normal, axis=0, keepdims=True)
    gin_ref[...] = gmid_ref[...] + norm_back(grad_first, mod[1:2], normal, inverse)

def input_backward(patches, mod, gqkv, gmid, wqkv):
    tokens, width = patches.shape
    latents = mod.shape[0]
    seq = tokens // latents
    rows = lambda cols: pl.BlockSpec((seq, cols), lambda i: (i, 0))
    per = lambda a: pl.BlockSpec((1,) + a.shape[1:], lambda i: (i, 0, 0))
    whole = lambda a: pl.BlockSpec(a.shape, lambda i: (0, 0), pipeline_mode=pl.Buffered(1))
    return pl.pallas_call(
        input_backward_kernel, grid=(latents,),
        in_specs=[rows(width), per(mod), rows(3 * width), rows(width), whole(wqkv)],
        out_specs=[rows(width), pl.BlockSpec((1, 2, width), lambda i: (i, 0, 0))],
        out_shape=[jax.ShapeDtypeStruct((tokens, width), jnp.float32), jax.ShapeDtypeStruct((latents, 2, width), jnp.float32)],
        compiler_params=pltpu.CompilerParams(vmem_limit_bytes=VMEM_BYTES))(patches, mod, gqkv, gmid, wqkv)


def cost(flops, size):
    return pl.CostEstimate(flops=int(flops), bytes_accessed=int(size), transcendentals=0)


def feed_forward_step(x_ref, g_ref, up_ref, down_ref, act_ref, gpre_ref, out_acc, grad_acc):
    inner_scale = SQRT_TWO_OVER_PI
    cubic = 0.044715
    pre = nn(x_ref[...], up_ref[...])
    grad_act = nt(g_ref[...], down_ref[...])
    squared = pre * pre
    bent = jnp.tanh(pre * (inner_scale + (inner_scale * cubic) * squared))
    half = 0.5 + 0.5 * bent
    act = (pre * half).astype(jnp.bfloat16)
    slope = half + (0.5 * pre) * (1.0 - bent * bent) * (
        inner_scale + (3.0 * cubic * inner_scale) * squared
    )
    grad_pre = (grad_act * slope).astype(jnp.bfloat16)
    act_ref[...] = act
    gpre_ref[...] = grad_pre
    out_acc[...] += nn(act, down_ref[...])
    grad_acc[...] += nt(grad_pre, up_ref[...])


def shared_kernel(
    x_ref, cot_ref, gate_ref, up_ref, down_ref,
    act_ref, gpre_ref, g_ref, out_ref, grad_ref,
    out_acc, grad_acc,
):
    step = pl.program_id(0)
    latents = gate_ref.shape[0]
    seq = x_ref.shape[0] // latents

    @pl.when(step == 0)
    def _():
        out_acc[...] = jnp.zeros_like(out_acc)
        grad_acc[...] = jnp.zeros_like(grad_acc)
        for i in range(latents):
            rows = slice(i * seq, (i + 1) * seq)
            g_ref[rows, :] = (gate_ref[i : i + 1, :] * cot_ref[rows, :].astype(jnp.float32)).astype(
                jnp.bfloat16
            )

    feed_forward_step(x_ref, g_ref, up_ref, down_ref, act_ref, gpre_ref, out_acc, grad_acc)

    @pl.when(step == pl.num_programs(0) - 1)
    def _():
        out_ref[...] = out_acc[...]
        grad_ref[...] = grad_acc[...]


def tile_of(width):
    return width // 4 if width % 512 == 0 else width


def still(array):
    return pl.BlockSpec(
        array.shape, lambda j, n=len(array.shape): (0,) * n, pipeline_mode=pl.Buffered(1)
    )


def shared_forward_backward(x, cot, gate, up, down):
    rows, width = x.shape
    hidden = up.shape[1]
    tile = tile_of(hidden)
    out = jax.ShapeDtypeStruct((rows, width), jnp.float32)
    wide = jax.ShapeDtypeStruct((rows, hidden), jnp.bfloat16)
    fixed = pl.BlockSpec((rows, width), lambda j: (0, 0))
    column = pl.BlockSpec((rows, tile), lambda j: (0, j))
    return pl.pallas_call(
        shared_kernel,
        grid=(hidden // tile,),
        in_specs=[
            still(x), still(cot), still(gate),
            pl.BlockSpec((width, tile), lambda j: (0, j)),
            pl.BlockSpec((tile, width), lambda j: (j, 0)),
        ],
        out_specs=[column, column, fixed, fixed, fixed],
        out_shape=[wide, wide, jax.ShapeDtypeStruct((rows, width), jnp.bfloat16), out, out],
        scratch_shapes=[pltpu.VMEM((rows, width), jnp.float32)] * 2,
        compiler_params=pltpu.CompilerParams(vmem_limit_bytes=VMEM_BYTES),
        cost_estimate=cost(8 * rows * width * hidden, 4 * width * hidden + 4 * rows * hidden),
        name="shared_ffn",
    )(x, cot, gate, up, down)


def expert_kernel(blocks, carried, *refs):
    xs, cots = refs[:blocks], refs[blocks : 2 * blocks]
    slot_row, slot_col, gate_col, gate_two, up_ref, down_ref = refs[2 * blocks : 2 * blocks + 6]
    rest = refs[2 * blocks + 6 + carried :]
    act_ref, gpre_ref, x_ref, g_ref = rest[:4]
    mixes, backs = rest[4 : 4 + blocks], rest[4 + blocks : 4 + 2 * blocks]
    out_acc, grad_acc = rest[4 + 2 * blocks :]
    step = pl.program_id(0)
    tokens = xs[0].shape[0]
    capacity = x_ref.shape[0] // blocks
    latents = gate_two.shape[1]
    seq = tokens // latents

    @pl.when(step == 0)
    def _():
        out_acc[...] = jnp.zeros_like(out_acc)
        grad_acc[...] = jnp.zeros_like(grad_acc)
        for b in range(blocks):
            rows = slice(b * capacity, (b + 1) * capacity)
            places = lax.broadcasted_iota(jnp.int32, (capacity, tokens), 0)
            pick = (places == slot_row[b]).astype(jnp.float32).astype(jnp.bfloat16)
            x_ref[rows, :] = nn(pick, xs[b][...]).astype(jnp.bfloat16)
            grads = []
            for i in range(latents):
                part = slice(i * seq, (i + 1) * seq)
                branch = gate_two[b, i : i + 1, :] * cots[b][part, :].astype(jnp.float32)
                grads.append((gate_col[b, part, :] * branch).astype(jnp.bfloat16))
            grad = jnp.concatenate(grads, axis=0)
            g_ref[rows, :] = nn(pick, grad).astype(jnp.bfloat16)

    feed_forward_step(x_ref, g_ref, up_ref, down_ref, act_ref, gpre_ref, out_acc, grad_acc)

    @pl.when(step == pl.num_programs(0) - 1)
    def _():
        for b in range(blocks):
            rows = slice(b * capacity, (b + 1) * capacity)
            places = lax.broadcasted_iota(jnp.int32, (tokens, capacity), 1)
            pick = (places == slot_col[b]).astype(jnp.float32).astype(jnp.bfloat16)
            backs[b][...] = nn(pick, grad_acc[rows, :].astype(jnp.bfloat16)).astype(jnp.bfloat16)
            mixed = nn(pick, out_acc[rows, :].astype(jnp.bfloat16))
            mixes[b][...] = (gate_col[b] * mixed).astype(jnp.bfloat16)


def expert_forward_backward(
    xs, cots, slot_row, slot_col, gate_col, gate_two, up, down, capacity, groups, group, carried
):
    blocks = len(xs)
    tokens, width = xs[0].shape
    hidden = up.shape[1]
    tile = tile_of(hidden)
    rows = blocks * capacity
    total = rows * groups
    wide = jax.ShapeDtypeStruct((total, hidden), jnp.bfloat16)
    slim = jax.ShapeDtypeStruct((total, width), jnp.bfloat16)
    token = jax.ShapeDtypeStruct((tokens, width), jnp.bfloat16)
    column = pl.BlockSpec((rows, tile), lambda j: (group, j))
    own = pl.BlockSpec((rows, width), lambda j: (group, 0))
    fixed = pl.BlockSpec((tokens, width), lambda j: (0, 0))
    small = [slot_row, slot_col, gate_col, gate_two]
    first = 2 * blocks + 6
    return pl.pallas_call(
        functools.partial(expert_kernel, blocks, len(carried)),
        grid=(hidden // tile,),
        in_specs=[still(a) for a in (*xs, *cots, *small)]
        + [
            pl.BlockSpec((width, tile), lambda j: (0, j)),
            pl.BlockSpec((tile, width), lambda j: (j, 0)),
        ]
        + [pl.BlockSpec(memory_space=pl.ANY)] * len(carried),
        out_specs=[column, column, own, own] + [fixed] * (2 * blocks),
        out_shape=[wide, wide, slim, slim] + [token] * (2 * blocks),
        scratch_shapes=[pltpu.VMEM((rows, width), jnp.float32)] * 2,
        input_output_aliases={first + i: i for i in range(len(carried))},
        compiler_params=pltpu.CompilerParams(vmem_limit_bytes=VMEM_BYTES),
        cost_estimate=cost(8 * rows * width * hidden, 4 * width * hidden + 4 * rows * hidden),
        name="expert_ffn",
    )(*xs, *cots, *small, up, down, *carried)


def weight_grad_kernel(steps, along_columns, moves, table, a_ref, b_ref, *rest):
    count = len({m[0] for m in moves})
    outs = rest[:count]
    sum_ref, sems = rest[count], rest[count + 1]
    step = pl.program_id(0)
    if along_columns:
        turned = rest[count + 2]
        tile = b_ref.shape[1]

        @pl.when(step == 0)
        def _():
            turned[...] = a_ref[...].T

        sum_ref[:, pl.ds(pl.multiple_of(step * tile, tile), tile)] = nn(
            turned[...], b_ref[...]
        ).astype(jnp.bfloat16)
    else:
        tile = a_ref.shape[1]
        sum_ref[pl.ds(pl.multiple_of(step * tile, tile), tile), :] = tn(
            a_ref[...], b_ref[...]
        ).astype(jnp.bfloat16)

    @pl.when(step == steps - 1)
    def _():
        copies = []
        for i, (out, row, rows, row_from, col_from, cols) in enumerate(moves):
            entry, scale, offset = row_from
            start = table[entry] * scale + offset
            if isinstance(col_from, tuple):
                chooser, half, shift = col_from
                column = pl.multiple_of(table[chooser] * half + shift, 128)
            else:
                column = col_from
            copies.append(
                pltpu.make_async_copy(
                    sum_ref.at[pl.ds(pl.multiple_of(start, 8), rows), pl.ds(column, cols)],
                    outs[out].at[pl.ds(row, rows), :],
                    sems.at[i],
                )
            )
        for copy in copies:
            copy.start()
        for copy in copies:
            copy.wait()


def weight_grad(a, b, table, moves, shapes, name):
    rows, left = a.shape
    right = b.shape[1]
    along_columns = left < 1024
    if along_columns:
        tile = right // 3 if right // 3 % 128 == 0 and right > 1024 else right
        steps = right // tile
        specs = [
            pl.BlockSpec((rows, left), lambda j, t: (0, 0), pipeline_mode=pl.Buffered(1)),
            pl.BlockSpec((rows, tile), lambda j, t: (0, j)),
        ]
        extra = [pltpu.VMEM((left, rows), jnp.bfloat16)]
    else:
        tile = tile_of(left)
        steps = left // tile
        specs = [
            pl.BlockSpec((rows, tile), lambda j, t: (0, j)),
            pl.BlockSpec((rows, right), lambda j, t: (0, 0), pipeline_mode=pl.Buffered(1)),
        ]
        extra = []
    return pl.pallas_call(
        functools.partial(weight_grad_kernel, steps, along_columns, moves),
        grid_spec=pltpu.PrefetchScalarGridSpec(
            num_scalar_prefetch=1,
            grid=(steps,),
            in_specs=specs,
            out_specs=[pl.BlockSpec(memory_space=pl.ANY)] * len(shapes),
            scratch_shapes=[
                pltpu.VMEM((left, right), jnp.bfloat16),
                pltpu.SemaphoreType.DMA((len(moves),)),
                *extra,
            ],
        ),
        out_shape=[jax.ShapeDtypeStruct(s, jnp.bfloat16) for s in shapes],
        compiler_params=pltpu.CompilerParams(vmem_limit_bytes=VMEM_BYTES),
        cost_estimate=cost(2 * rows * left * right, 2 * left * right + 2 * rows * (left + right)),
        name=name,
    )(table, a, b)


def bits_of(size):
    return size.bit_length() - 1


def label_of(index):
    upper = index >> 1
    return ((upper ^ (upper >> 1)) << 1) | (index & 1)


def index_of(label):
    upper = label >> 1
    shift = 1
    while shift < 32:
        upper = upper ^ (upper >> shift)
        shift *= 2
    return (upper << 1) | (label & 1)


def swap_dp(value, bit):
    size = lax.axis_size("dp")
    return lax.ppermute(
        value, "dp", [(i, index_of(label_of(i) ^ (1 << bit))) for i in range(size)]
    )


def swap_expert(value, bit):
    size = lax.axis_size("expert")
    return lax.ppermute(value, "expert", [(i, i ^ (1 << bit)) for i in range(size)])


def gather_expert(value):
    bits = bits_of(lax.axis_size("expert"))
    parts = {0: value}
    for bit in reversed(range(bits)):
        for r in list(parts):
            parts[r | (1 << bit)] = swap_expert(parts[r], bit)
    return [parts[r] for r in range(1 << bits)]


def gather_ordered(value):
    mine = lax.axis_index("expert")
    for bit in range(bits_of(lax.axis_size("expert"))):
        other = swap_expert(value, bit)
        upper = (mine >> bit & 1) == 1
        value = jnp.concatenate(
            [jnp.where(upper, other, value), jnp.where(upper, value, other)], axis=0
        )
    return value


def scatter_expert(parts):
    parts = [[part] for part in parts]
    for bit in range(bits_of(lax.axis_size("expert"))):
        left = []
        for kept, away in zip(parts[::2], parts[1::2]):
            away = away[0] if len(away) == 1 else added(away).astype(jnp.bfloat16)
            kept = kept if len(kept) == 1 else [added(kept).astype(jnp.bfloat16)]
            left.append([*kept, swap_expert(away, bit)])
        parts = left
    return parts[0]


def gather_dp(value):
    for bit in range(bits_of(lax.axis_size("dp"))):
        value = jnp.concatenate([value, swap_dp(value, bit)], axis=0)
    return value


def orders(size):
    bits = bits_of(size)
    return [[(start + step) % bits for step in range(bits)] for start in range(PARTS)]


def shard_table(size):
    places = np.zeros((PARTS, size), np.int32)
    for part, order in enumerate(orders(size)):
        for place in range(size):
            for step, bit in enumerate(order):
                if place >> (len(order) - 1 - step) & 1:
                    places[part, place] |= 1 << bit
    owners = index_of(label_of(lax.axis_index("dp")) ^ jnp.asarray(places.reshape(-1)))
    core = lax.axis_index("expert") & 1
    return jnp.concatenate([owners, core[None], 1 - core[None]]).astype(jnp.int32)


def pieces_moves(size, left, right, by_rows):
    shard = left // size
    moves = []
    for part in range(PARTS):
        for place in range(size):
            out = 2 * part + (place >= size // 2)
            at = place % (size // 2)
            entry = part * size + place
            if by_rows:
                rows = shard // PARTS
                moves.append((out, at * rows, rows, (entry, shard, part * rows), 0, right))
            else:
                cols = right // PARTS
                moves.append((out, at * shard, shard, (entry, shard, 0), part * cols, cols))
    if by_rows:
        shape = (left // 2 // PARTS, right)
    else:
        shape = (left // 2, right // PARTS)
    return moves, [shape] * (2 * PARTS)


def dense_moves(size, left, right):
    shard = left // size
    half = right // 2
    cols = half // PARTS
    moves = []
    for out in range(2):
        for part in range(PARTS):
            for place in range(size):
                entry = part * size + place
                chooser = PARTS * size + (1 - out)
                moves.append(
                    (
                        out, part * left + place * shard, shard,
                        (entry, shard, 0), (chooser, half, part * cols), cols,
                    )
                )
    return moves, [(PARTS * left, cols)] * 2


def added(parts):
    total = parts[0].astype(jnp.float32)
    for part in parts[1:]:
        total = total + part.astype(jnp.float32)
    return total


def sum_over_dp(away, kept, order):
    for step, bit in enumerate(order):
        kept = [*kept, swap_dp(away, bit)]
        half = kept[0].shape[0] // 2
        if step + 1 < len(order):
            away = added([k[half:] for k in kept]).astype(jnp.bfloat16)
            kept = [k[:half] for k in kept]
    return added(kept)


def sum_pieces(pieces, size, by_rows):
    sums = [
        sum_over_dp(pieces[2 * part + 1], [pieces[2 * part]], order)
        for part, order in enumerate(orders(size))
    ]
    return jnp.concatenate(sums, axis=0 if by_rows else 1)


def sum_dense(away, mine, size):
    kept = [mine, swap_expert(away, 0)]
    left = mine.shape[0] // PARTS
    sums = []
    for part, order in enumerate(orders(size)):
        low = [k[part * left : part * left + left // 2] for k in kept]
        high = [k[part * left + left // 2 : (part + 1) * left] for k in kept]
        sums.append(sum_over_dp(added(high).astype(jnp.bfloat16), low, order))
    total = jnp.concatenate(sums, axis=1).astype(jnp.bfloat16)
    for bit in range(1, bits_of(lax.axis_size("expert"))):
        total = added([total, swap_expert(total, bit)]).astype(jnp.bfloat16)
    opposite = swap_expert(total, 0)
    upper = (lax.axis_index("expert") & 1) == 1
    return jnp.concatenate(
        [jnp.where(upper, opposite, total), jnp.where(upper, total, opposite)], axis=1
    ).astype(jnp.float32)


def on_device(
    patches,
    time_embed,
    ada_weight,
    ada_bias,
    qkv_weight,
    out_weight,
    up_weight,
    down_weight,
    expert_up,
    expert_down,
    routes,
    gate_weights,
    cotangent,
):
    tokens, width = patches.shape
    latents = time_embed.shape[0]
    seq_len = tokens // latents
    experts = lax.axis_size("expert")
    dp_size = lax.axis_size("dp")
    dp_index = lax.axis_index("dp")
    expert_index = lax.axis_index("expert")
    capacity = 5 * tokens // (2 * experts)
    table = shard_table(dp_size)

    cond = jax.nn.silu(time_embed.astype(jnp.float32)).astype(jnp.bfloat16)
    modulation = jnp.dot(cond, ada_weight, preferred_element_type=jnp.float32) + ada_bias
    mod = modulation.reshape(latents, 6, width)

    cots = gather_expert(cotangent)
    routes_all = jnp.stack(gather_expert(routes.T))
    gates_all = jnp.stack(gather_expert(gate_weights.T))
    time_group = jnp.concatenate(gather_expert(time_embed))
    time_all = gather_dp(gather_ordered(time_embed))

    cond_group = jax.nn.silu(time_group.astype(jnp.float32)).astype(jnp.bfloat16)
    gate_two_group = (
        jnp.dot(cond_group, ada_weight[:, 5 * width :], preferred_element_type=jnp.float32)
        + ada_bias[5 * width :]
    ).reshape(experts, latents, width)
    named = routes_all == expert_index
    member = jnp.any(named, axis=1)
    gate_here = jnp.sum(jnp.where(named, gates_all, 0.0), axis=1)
    position = jnp.arange(tokens, dtype=jnp.int32)
    before = (position[:, None] < position[None, :]).astype(jnp.bfloat16)
    slot = jnp.dot(
        member.astype(jnp.bfloat16), before, preferred_element_type=jnp.float32
    ).astype(jnp.int32)
    slot = jnp.where(member, slot, capacity)
    local_counts = jnp.sum(
        (routes[:, :, None] == jnp.arange(experts, dtype=jnp.int32)).astype(jnp.int32),
        axis=(0, 1),
    )
    slot_row, slot_col, gate_col = slot[:, None, :], slot[:, :, None], gate_here[:, :, None]

    first_in, qkv_all, log_total, attended, attn_proj, second_in = attn_forward(
        patches, mod, qkv_weight, out_weight
    )
    seconds = gather_expert(second_in)

    shared_act, grad_shared_pre, grad_shared, shared_out, grad_second = shared_forward_backward(
        second_in, cotangent, mod[:, 5], up_weight, down_weight
    )

    group_size = 2
    groups = experts // group_size
    carried = []
    mixes, backs = [], []
    for group in range(groups):
        span = slice(group * group_size, (group + 1) * group_size)
        results = expert_forward_backward(
            seconds[span], cots[span], slot_row[span], slot_col[span], gate_col[span],
            gate_two_group[span], expert_up[0], expert_down[0], capacity, groups, group, carried,
        )
        carried = results[:4]
        mixes += results[4 : 4 + group_size]
        backs += results[4 + group_size :]
    act_rows, grad_pre_rows, rows_in, grad_rows = carried
    back_kept, back_came = scatter_expert(backs)
    mix_kept, mix_came = scatter_expert(mixes)

    moves, shapes = pieces_moves(dp_size, act_rows.shape[1], width, True)
    down_pieces = weight_grad(act_rows, grad_rows, table, moves, shapes, "grad_expert_down")
    sum_e_down = sum_pieces(down_pieces, dp_size, True)
    moves, shapes = pieces_moves(dp_size, width, act_rows.shape[1], False)
    up_pieces = weight_grad(rows_in, grad_pre_rows, table, moves, shapes, "grad_expert_up")
    sum_e_up = sum_pieces(up_pieces, dp_size, False)

    moves, shapes = dense_moves(dp_size, shared_act.shape[1], width)
    sum_w_down = sum_dense(
        *weight_grad(shared_act, grad_shared, table, moves, shapes, "grad_down"), dp_size
    )
    moves, shapes = dense_moves(dp_size, width, shared_act.shape[1])
    sum_w_up = sum_dense(
        *weight_grad(second_in, grad_shared_pre, table, moves, shapes, "grad_up"), dp_size
    )

    grad_qkv_rows, grad_attn, grad_middle, grad_mod_early = attn_backward(
        patches, mod, attn_proj, qkv_all, log_total, cotangent, out_weight,
        [grad_second, back_kept, back_came],
    )
    moves, shapes = dense_moves(dp_size, width, 3 * width)
    sum_w_qkv = sum_dense(
        *weight_grad(first_in, grad_qkv_rows, table, moves, shapes, "grad_qkv"), dp_size
    )
    moves, shapes = dense_moves(dp_size, width, width)
    sum_w_out = sum_dense(
        *weight_grad(attended, grad_attn, table, moves, shapes, "grad_out"), dp_size
    )
    grad_input, grad_mod_late = input_backward(
        patches, mod, grad_qkv_rows, grad_middle, qkv_weight
    )

    middle = patches.astype(jnp.float32).reshape(latents, seq_len, width) + mod[
        :, 2:3
    ] * attn_proj.reshape(latents, seq_len, width)
    branch = (shared_out + added([mix_kept, mix_came])).reshape(latents, seq_len, width)
    block_out = (middle + mod[:, 5:6] * branch).reshape(tokens, width).astype(jnp.bfloat16)
    grad_gate_two = jnp.sum(
        cotangent.astype(jnp.float32).reshape(latents, seq_len, width) * branch, axis=1
    )

    count_parts = jnp.concatenate([local_counts // 128, local_counts % 128]).astype(jnp.bfloat16)
    count_rows = jnp.zeros((latents, 128), jnp.bfloat16).at[0, : 2 * experts].set(count_parts)
    early = jnp.concatenate(
        [
            grad_mod_early.reshape(latents, 3 * width).astype(jnp.bfloat16),
            grad_gate_two.astype(jnp.bfloat16),
            count_rows,
        ],
        axis=1,
    )
    late = grad_mod_late.reshape(latents, 2 * width).astype(jnp.bfloat16)
    early_all = gather_dp(gather_ordered(early))
    late_all = gather_dp(gather_ordered(late))
    grad_mod_all = jnp.concatenate([late_all, early_all[:, : 4 * width]], axis=1)
    count_sums = jnp.sum(early_all[:, 4 * width :].astype(jnp.float32), axis=0).astype(jnp.int32)
    counts = count_sums[:experts] * 128 + count_sums[experts : 2 * experts]
    cond_all = jax.nn.silu(time_all.astype(jnp.float32)).astype(jnp.bfloat16)
    ada_rows = width // dp_size
    cond_mine = lax.dynamic_slice_in_dim(cond_all.T, dp_index * ada_rows, ada_rows, axis=0)
    sum_ada = jnp.dot(cond_mine, grad_mod_all, preferred_element_type=jnp.float32)
    bias_all = jnp.sum(grad_mod_all.astype(jnp.float32), axis=0)
    bias_size = bias_all.shape[0] // dp_size
    sum_bias = lax.dynamic_slice_in_dim(bias_all, dp_index * bias_size, bias_size)
    return (
        block_out,
        grad_input,
        sum_ada,
        sum_bias,
        sum_w_qkv,
        sum_w_out,
        sum_w_up,
        sum_w_down,
        sum_e_up[None],
        sum_e_down[None],
        counts,
    )


def solution(mesh):
    in_specs = (
        P(("dp", "expert"), None),
        P(("dp", "expert"), None),
        P(),
        P(),
        P(),
        P(),
        P(),
        P(),
        P("expert", None, None),
        P("expert", None, None),
        P(("dp", "expert"), None),
        P(("dp", "expert"), None),
        P(("dp", "expert"), None),
    )
    out_specs = (
        P(("dp", "expert"), None),
        P(("dp", "expert"), None),
        P("dp", None),
        P("dp"),
        P("dp", None),
        P("dp", None),
        P("dp", None),
        P("dp", None),
        P("expert", "dp", None),
        P("expert", "dp", None),
        P(),
    )
    return jax.shard_map(
        on_device, mesh=mesh, in_specs=in_specs, out_specs=out_specs, check_vma=False
    )
```

```python
import functools
import math

import jax
import jax.numpy as jnp
import numpy as np
from jax import lax
from jax.experimental import pallas as pl
from jax.experimental.pallas import tpu as pltpu
from jax.sharding import PartitionSpec as P

HEAD_DIM = 64
VMEM_BYTES = 56 << 20
SHRINK = 1
SQRT_TWO_OVER_PI = math.sqrt(2.0 / math.pi)


def nt(a,b): return lax.dot_general(a,b,(((1,),(1,)),((),())),preferred_element_type=jnp.float32)
def nn(a,b): return lax.dot_general(a,b,(((1,),(0,)),((),())),preferred_element_type=jnp.float32)
def tn(a,b): return lax.dot_general(a,b,(((0,),(0,)),((),())),preferred_element_type=jnp.float32)

def normalized(values_in):
    row_mean = jnp.mean(values_in, axis=-1, keepdims=True)
    centered = values_in - row_mean
    row_var = jnp.mean(centered * centered, axis=-1, keepdims=True)
    inverse = lax.rsqrt(row_var + 1e-06)
    return centered * inverse, inverse

def norm_back(grad_out, scale, normal, inverse):
    inner = grad_out * (1.0 + scale)
    mean_inner = jnp.mean(inner, axis=-1, keepdims=True)
    mean_cross = jnp.mean(inner * normal, axis=-1, keepdims=True)
    return inverse * (inner - mean_inner - normal * mean_cross)

def head_lanes(pair, head):
    lane = lax.broadcasted_iota(jnp.int32, pair.shape, 1)
    return jnp.where(lane // HEAD_DIM == head, pair, jnp.zeros_like(pair))

def attn_forward_kernel(x_ref, mod_ref, wqkv_ref, wout_ref, first_ref, qkv_ref, lse_ref, att_ref, proj_ref, second_ref):
    width = x_ref.shape[1]
    x = x_ref[...].astype(jnp.float32)
    mod = mod_ref[0]
    normal, _ = normalized(x)
    first_ref[...] = (normal * (1.0 + mod[1:2]) + mod[0:1]).astype(jnp.bfloat16)
    qkv_ref[...] = nn(first_ref[...], wqkv_ref[...]).astype(jnp.bfloat16)
    lane = 2 * HEAD_DIM
    for pair in range(width // lane):
        q2 = qkv_ref[:, pair * lane : (pair + 1) * lane]
        k2 = qkv_ref[:, width + pair * lane : width + (pair + 1) * lane]
        v2 = qkv_ref[:, 2 * width + pair * lane : 2 * width + (pair + 1) * lane]
        v2t = v2.T
        outs = []
        for head in range(2):
            scores = nt(head_lanes(k2, head), q2) * HEAD_DIM ** (-0.5)
            peak = jnp.max(scores, axis=0, keepdims=True)
            powers = jnp.exp(scores - peak)
            total = jnp.sum(powers, axis=0, keepdims=True)
            lse_ref[0, 2 * pair + head : 2 * pair + head + 1, :] = peak + jnp.log(total)
            probs = (powers * (1.0 / total)).astype(jnp.bfloat16)
            outs.append(nn(v2t[head * HEAD_DIM : (head + 1) * HEAD_DIM], probs))
        both = jnp.concatenate(outs, axis=0).astype(jnp.bfloat16)
        att_ref[:, pair * lane : (pair + 1) * lane] = both.T
    proj = nn(att_ref[...], wout_ref[...])
    proj_ref[...] = proj
    middle = x + mod[2:3] * proj
    normal2, _ = normalized(middle)
    second_ref[...] = (normal2 * (1.0 + mod[4:5]) + mod[3:4]).astype(jnp.bfloat16)

def attn_forward(patches, mod, wqkv, wout):
    tokens, width = patches.shape
    latents = mod.shape[0]
    seq = tokens // latents
    heads = width // HEAD_DIM
    rows = lambda cols: pl.BlockSpec((seq, cols), lambda i: (i, 0))
    whole = lambda a: pl.BlockSpec(a.shape, lambda i: (0, 0), pipeline_mode=pl.Buffered(1))
    return pl.pallas_call(
        attn_forward_kernel, grid=(latents,),
        in_specs=[rows(width), pl.BlockSpec((1,) + mod.shape[1:], lambda i: (i, 0, 0)), whole(wqkv), whole(wout)],
        out_specs=[rows(width), rows(3 * width), pl.BlockSpec((1, heads, seq), lambda i: (i, 0, 0)), rows(width), rows(width), rows(width)],
        out_shape=[jax.ShapeDtypeStruct((tokens, width), jnp.bfloat16), jax.ShapeDtypeStruct((tokens, 3 * width), jnp.bfloat16),
            jax.ShapeDtypeStruct((latents, heads, seq), jnp.float32), jax.ShapeDtypeStruct((tokens, width), jnp.bfloat16),
            jax.ShapeDtypeStruct((tokens, width), jnp.float32), jax.ShapeDtypeStruct((tokens, width), jnp.bfloat16)],
        compiler_params=pltpu.CompilerParams(vmem_limit_bytes=VMEM_BYTES))(patches, mod, wqkv, wout)

def attn_backward_kernel(extra, x_ref, mod_ref, proj_ref, qkv_ref, lse_ref, cot_ref, wout_ref, *rest):
    adds = rest[:extra]
    gqkv_ref, gattn_ref, gmid_ref, gmod_ref = rest[extra:]
    width = x_ref.shape[1]
    x = x_ref[...].astype(jnp.float32)
    mod = mod_ref[0]
    proj = proj_ref[...]
    normal, inverse = normalized(x + mod[2:3] * proj)
    grad_second = adds[0][...].astype(jnp.float32)
    for a in adds[1:]:
        grad_second = grad_second + a[...].astype(jnp.float32)
    gmod_ref[0, 1:2, :] = jnp.sum(grad_second, axis=0, keepdims=True)
    gmod_ref[0, 2:3, :] = jnp.sum(grad_second * normal, axis=0, keepdims=True)
    grad_middle = cot_ref[...].astype(jnp.float32) + norm_back(grad_second, mod[4:5], normal, inverse)
    gmid_ref[...] = grad_middle
    gmod_ref[0, 0:1, :] = jnp.sum(grad_middle * proj, axis=0, keepdims=True)
    gattn_ref[...] = (mod[2:3] * grad_middle).astype(jnp.bfloat16)
    grad_att = nt(gattn_ref[...], wout_ref[...]).astype(jnp.bfloat16)
    lane = 2 * HEAD_DIM
    scale = HEAD_DIM ** (-0.5)
    for pair in range(width // lane):
        sl = slice(pair * lane, (pair + 1) * lane)
        q2 = qkv_ref[:, pair * lane : (pair + 1) * lane]
        k2 = qkv_ref[:, width + pair * lane : width + (pair + 1) * lane]
        v2 = qkv_ref[:, 2 * width + pair * lane : 2 * width + (pair + 1) * lane]
        do2 = grad_att[:, sl]
        k2t = k2.T
        gq, gk, gv = [], [], []
        for head in range(2):
            scores = nt(head_lanes(k2, head), q2) * scale
            probs = jnp.exp(scores - lse_ref[0, 2 * pair + head : 2 * pair + head + 1, :])
            grad_probs = nt(head_lanes(v2, head), do2)
            inner = jnp.sum(probs * grad_probs, axis=0, keepdims=True)
            grad_scores = (probs * (grad_probs - inner)).astype(jnp.bfloat16)
            gv.append(nn(probs.astype(jnp.bfloat16), do2))
            gk.append(nn(grad_scores, q2))
            gq.append(nn(k2t[head * HEAD_DIM : (head + 1) * HEAD_DIM], grad_scores))
        low = lax.broadcasted_iota(jnp.int32, gv[0].shape, 1) < HEAD_DIM
        gqt = (jnp.concatenate(gq, axis=0) * scale).astype(jnp.bfloat16)
        gqkv_ref[:, pair * lane : (pair + 1) * lane] = gqt.T
        gqkv_ref[:, width + pair * lane : width + (pair + 1) * lane] = (jnp.where(low, gk[0], gk[1]) * scale).astype(jnp.bfloat16)
        gqkv_ref[:, 2 * width + pair * lane : 2 * width + (pair + 1) * lane] = jnp.where(low, gv[0], gv[1]).astype(jnp.bfloat16)

def attn_backward(patches, mod, proj, qkv, lse, cot, wout, adds):
    tokens, width = patches.shape
    latents = mod.shape[0]
    seq = tokens // latents
    rows = lambda cols: pl.BlockSpec((seq, cols), lambda i: (i, 0))
    per = lambda a: pl.BlockSpec((1,) + a.shape[1:], lambda i: (i, 0, 0))
    whole = lambda a: pl.BlockSpec(a.shape, lambda i: (0, 0), pipeline_mode=pl.Buffered(1))
    return pl.pallas_call(
        functools.partial(attn_backward_kernel, len(adds)), grid=(latents,),
        in_specs=[rows(width), per(mod), rows(width), rows(3 * width), per(lse), rows(width), whole(wout)] + [rows(width)] * len(adds),
        out_specs=[rows(3 * width), rows(width), rows(width), pl.BlockSpec((1, 3, width), lambda i: (i, 0, 0))],
        out_shape=[jax.ShapeDtypeStruct((tokens, 3 * width), jnp.bfloat16), jax.ShapeDtypeStruct((tokens, width), jnp.bfloat16),
            jax.ShapeDtypeStruct((tokens, width), jnp.float32), jax.ShapeDtypeStruct((latents, 3, width), jnp.float32)],
        compiler_params=pltpu.CompilerParams(vmem_limit_bytes=VMEM_BYTES))(patches, mod, proj, qkv, lse, cot, wout, *adds)

def input_backward_kernel(x_ref, mod_ref, gqkv_ref, gmid_ref, wqkv_ref, gin_ref, gmod_ref):
    mod = mod_ref[0]
    normal, inverse = normalized(x_ref[...].astype(jnp.float32))
    grad_first = nt(gqkv_ref[...], wqkv_ref[...])
    gmod_ref[0, 0:1, :] = jnp.sum(grad_first, axis=0, keepdims=True)
    gmod_ref[0, 1:2, :] = jnp.sum(grad_first * normal, axis=0, keepdims=True)
    gin_ref[...] = gmid_ref[...] + norm_back(grad_first, mod[1:2], normal, inverse)

def input_backward(patches, mod, gqkv, gmid, wqkv):
    tokens, width = patches.shape
    latents = mod.shape[0]
    seq = tokens // latents
    rows = lambda cols: pl.BlockSpec((seq, cols), lambda i: (i, 0))
    per = lambda a: pl.BlockSpec((1,) + a.shape[1:], lambda i: (i, 0, 0))
    whole = lambda a: pl.BlockSpec(a.shape, lambda i: (0, 0), pipeline_mode=pl.Buffered(1))
    return pl.pallas_call(
        input_backward_kernel, grid=(latents,),
        in_specs=[rows(width), per(mod), rows(3 * width), rows(width), whole(wqkv)],
        out_specs=[rows(width), pl.BlockSpec((1, 2, width), lambda i: (i, 0, 0))],
        out_shape=[jax.ShapeDtypeStruct((tokens, width), jnp.float32), jax.ShapeDtypeStruct((latents, 2, width), jnp.float32)],
        compiler_params=pltpu.CompilerParams(vmem_limit_bytes=VMEM_BYTES))(patches, mod, gqkv, gmid, wqkv)


def cost(flops, size):
    return pl.CostEstimate(flops=int(flops) // SHRINK, bytes_accessed=int(size) // SHRINK, transcendentals=0)


def feed_forward_step(x_ref, g_ref, up_ref, down_ref, act_ref, gpre_ref, out_acc, grad_acc):
    inner_scale = SQRT_TWO_OVER_PI
    cubic = 0.044715
    pre = nn(x_ref[...], up_ref[...])
    grad_act = nt(g_ref[...], down_ref[...])
    squared = pre * pre
    bent = jnp.tanh(pre * (inner_scale + (inner_scale * cubic) * squared))
    half = 0.5 + 0.5 * bent
    act = (pre * half).astype(jnp.bfloat16)
    slope = half + (0.5 * pre) * (1.0 - bent * bent) * (
        inner_scale + (3.0 * cubic * inner_scale) * squared
    )
    grad_pre = (grad_act * slope).astype(jnp.bfloat16)
    act_ref[...] = act
    gpre_ref[...] = grad_pre
    out_acc[...] += nn(act, down_ref[...])
    grad_acc[...] += nt(grad_pre, up_ref[...])


def shared_kernel(
    x_ref, cot_ref, gate_ref, up_ref, down_ref,
    act_ref, gpre_ref, g_ref, out_ref, grad_ref,
    out_acc, grad_acc,
):
    step = pl.program_id(0)
    latents = gate_ref.shape[0]
    seq = x_ref.shape[0] // latents

    @pl.when(step == 0)
    def _():
        out_acc[...] = jnp.zeros_like(out_acc)
        grad_acc[...] = jnp.zeros_like(grad_acc)
        for i in range(latents):
            rows = slice(i * seq, (i + 1) * seq)
            g_ref[rows, :] = (gate_ref[i : i + 1, :] * cot_ref[rows, :].astype(jnp.float32)).astype(
                jnp.bfloat16
            )

    feed_forward_step(x_ref, g_ref, up_ref, down_ref, act_ref, gpre_ref, out_acc, grad_acc)

    @pl.when(step == pl.num_programs(0) - 1)
    def _():
        out_ref[...] = out_acc[...]
        grad_ref[...] = grad_acc[...]


def tile_of(width):
    return width // 4 if width % 512 == 0 else width


def still(array):
    return pl.BlockSpec(
        array.shape, lambda j, n=len(array.shape): (0,) * n, pipeline_mode=pl.Buffered(1)
    )


def shared_forward_backward(x, cot, gate, up, down):
    rows, width = x.shape
    hidden = up.shape[1]
    tile = tile_of(hidden)
    out = jax.ShapeDtypeStruct((rows, width), jnp.float32)
    wide = jax.ShapeDtypeStruct((rows, hidden), jnp.bfloat16)
    fixed = pl.BlockSpec((rows, width), lambda j: (0, 0))
    column = pl.BlockSpec((rows, tile), lambda j: (0, j))
    return pl.pallas_call(
        shared_kernel,
        grid=(hidden // tile,),
        in_specs=[
            still(x), still(cot), still(gate),
            pl.BlockSpec((width, tile), lambda j: (0, j)),
            pl.BlockSpec((tile, width), lambda j: (j, 0)),
        ],
        out_specs=[column, column, fixed, fixed, fixed],
        out_shape=[wide, wide, jax.ShapeDtypeStruct((rows, width), jnp.bfloat16), out, out],
        scratch_shapes=[pltpu.VMEM((rows, width), jnp.float32)] * 2,
        compiler_params=pltpu.CompilerParams(vmem_limit_bytes=VMEM_BYTES),
        cost_estimate=cost(8 * rows * width * hidden, 4 * width * hidden + 4 * rows * hidden),
        name="shared_ffn",
    )(x, cot, gate, up, down)


def expert_kernel(blocks, carried, *refs):
    xs, cots = refs[:blocks], refs[blocks : 2 * blocks]
    slot_row, slot_col, gate_col, gate_two, up_ref, down_ref = refs[2 * blocks : 2 * blocks + 6]
    rest = refs[2 * blocks + 6 + carried :]
    act_ref, gpre_ref, x_ref, g_ref = rest[:4]
    mixes, backs = rest[4 : 4 + blocks], rest[4 + blocks : 4 + 2 * blocks]
    out_acc, grad_acc = rest[4 + 2 * blocks :]
    step = pl.program_id(0)
    tokens = xs[0].shape[0]
    capacity = x_ref.shape[0] // blocks
    latents = gate_two.shape[1]
    seq = tokens // latents

    @pl.when(step == 0)
    def _():
        out_acc[...] = jnp.zeros_like(out_acc)
        grad_acc[...] = jnp.zeros_like(grad_acc)
        for b in range(blocks):
            rows = slice(b * capacity, (b + 1) * capacity)
            places = lax.broadcasted_iota(jnp.int32, (capacity, tokens), 0)
            pick = (places == slot_row[b]).astype(jnp.float32).astype(jnp.bfloat16)
            x_ref[rows, :] = nn(pick, xs[b][...]).astype(jnp.bfloat16)
            grads = []
            for i in range(latents):
                part = slice(i * seq, (i + 1) * seq)
                branch = gate_two[b, i : i + 1, :] * cots[b][part, :].astype(jnp.float32)
                grads.append((gate_col[b, part, :] * branch).astype(jnp.bfloat16))
            grad = jnp.concatenate(grads, axis=0)
            g_ref[rows, :] = nn(pick, grad).astype(jnp.bfloat16)

    feed_forward_step(x_ref, g_ref, up_ref, down_ref, act_ref, gpre_ref, out_acc, grad_acc)

    @pl.when(step == pl.num_programs(0) - 1)
    def _():
        for b in range(blocks):
            rows = slice(b * capacity, (b + 1) * capacity)
            places = lax.broadcasted_iota(jnp.int32, (tokens, capacity), 1)
            pick = (places == slot_col[b]).astype(jnp.float32).astype(jnp.bfloat16)
            backs[b][...] = nn(pick, grad_acc[rows, :].astype(jnp.bfloat16)).astype(jnp.bfloat16)
            mixed = nn(pick, out_acc[rows, :].astype(jnp.bfloat16))
            mixes[b][...] = (gate_col[b] * mixed).astype(jnp.bfloat16)


def expert_forward_backward(
    xs, cots, slot_row, slot_col, gate_col, gate_two, up, down, capacity, groups, group, carried
):
    blocks = len(xs)
    tokens, width = xs[0].shape
    hidden = up.shape[1]
    tile = tile_of(hidden)
    rows = blocks * capacity
    wide = jax.ShapeDtypeStruct((rows * groups, hidden), jnp.bfloat16)
    slim = jax.ShapeDtypeStruct((rows * groups, width), jnp.bfloat16)
    mixture = jax.ShapeDtypeStruct((tokens * groups, width), jnp.bfloat16)
    token = jax.ShapeDtypeStruct((tokens, width), jnp.bfloat16)
    column = pl.BlockSpec((rows, tile), lambda j: (group, j))
    own = pl.BlockSpec((rows, width), lambda j: (group, 0))
    mixed = pl.BlockSpec((tokens, width), lambda j: (group, 0))
    fixed = pl.BlockSpec((tokens, width), lambda j: (0, 0))
    small = [slot_row, slot_col, gate_col, gate_two]
    first = 2 * blocks + 6
    return pl.pallas_call(
        functools.partial(expert_kernel, blocks, len(carried)),
        grid=(hidden // tile,),
        in_specs=[still(a) for a in (*xs, *cots)]
        + [
            pl.BlockSpec(
                (blocks,) + a.shape[1:], lambda j, n=len(a.shape) - 1: (group,) + (0,) * n,
                pipeline_mode=pl.Buffered(1),
            )
            for a in small
        ]
        + [
            pl.BlockSpec((width, tile), lambda j: (0, j)),
            pl.BlockSpec((tile, width), lambda j: (j, 0)),
        ]
        + [pl.BlockSpec(memory_space=pl.ANY)] * len(carried),
        out_specs=[column, column, own, own] + [mixed] * blocks + [fixed] * blocks,
        scratch_shapes=[pltpu.VMEM((rows, width), jnp.float32)] * 2,
        out_shape=[wide, wide, slim, slim] + [mixture] * blocks + [token] * blocks,
        input_output_aliases={first + i: i for i in range(len(carried))},
        compiler_params=pltpu.CompilerParams(vmem_limit_bytes=VMEM_BYTES),
        cost_estimate=cost(8 * rows * width * hidden, 4 * width * hidden + 4 * rows * hidden),
        name="expert_ffn",
    )(*xs, *cots, *small, up, down, *carried)


def route_kernel(index_ref, info_ref, time_ref, ada_ref, bias_ref, row_ref, col_ref, gate_ref, two_ref):
    experts, _, tokens = row_ref.shape
    latents = time_ref.shape[0] // experts
    expert = index_ref[0]
    slots, gates = [], []
    before = (
        lax.broadcasted_iota(jnp.int32, (tokens, tokens), 0)
        < lax.broadcasted_iota(jnp.int32, (tokens, tokens), 1)
    ).astype(jnp.float32).astype(jnp.bfloat16)
    for r in range(experts):
        routes = info_ref[r, 0:2, :].astype(jnp.int32)
        named = routes == expert
        member = jnp.sum(named.astype(jnp.float32), axis=0, keepdims=True)
        earlier = nn(member.astype(jnp.bfloat16), before)
        slot = jnp.where(member > 0.5, earlier, float(tokens))
        row_ref[r] = slot.astype(jnp.int32)
        slots.append(slot)
        gates.append(
            jnp.sum(jnp.where(named, info_ref[r, 2:4, :], 0.0), axis=0, keepdims=True)
        )
    turned = jnp.concatenate(slots + gates, axis=0).T
    for r in range(experts):
        col_ref[r] = turned[:, r : r + 1].astype(jnp.int32)
        gate_ref[r] = turned[:, experts + r : experts + r + 1]
    times = time_ref[...]
    cond = (times / (1.0 + jnp.exp(-times))).astype(jnp.bfloat16)
    gate_two = nn(cond, ada_ref[...]) + bias_ref[...]
    for r in range(experts):
        two_ref[r] = gate_two[r * latents : (r + 1) * latents]


def route(expert, info, times, ada_weight, ada_bias, tokens):
    experts = info.shape[0]
    width = times.shape[1]
    latents = times.shape[0] // experts
    vmem = pl.BlockSpec(memory_space=pltpu.VMEM)
    return pl.pallas_call(
        route_kernel,
        grid=(1,),
        in_specs=[
            pl.BlockSpec(memory_space=pltpu.SMEM), still(info), still(times),
            pl.BlockSpec((width, width), lambda j: (0, 5)),
            pl.BlockSpec((1, width), lambda j: (0, 5)),
        ],
        out_specs=[vmem] * 4,
        out_shape=[
            jax.ShapeDtypeStruct((experts, 1, tokens), jnp.int32),
            jax.ShapeDtypeStruct((experts, tokens, 1), jnp.int32),
            jax.ShapeDtypeStruct((experts, tokens, 1), jnp.float32),
            jax.ShapeDtypeStruct((experts, latents, width), jnp.float32),
        ],
        compiler_params=pltpu.CompilerParams(vmem_limit_bytes=VMEM_BYTES),
        name="route",
    )(expert, info, times, ada_weight, ada_bias[None])


def weight_grad_kernel(steps, by_columns, moves, outs, carried, table, a_ref, b_ref, *rest):
    rest = rest[carried:]
    out_refs = rest[:outs]
    sum_ref, sems = rest[outs], rest[outs + 1]
    step = pl.program_id(0)
    if by_columns:
        turned = rest[outs + 2]

        @pl.when(step == 0)
        def _():
            turned[...] = a_ref[...].T

        sum_ref[step] = nn(turned[...], b_ref[...]).astype(jnp.bfloat16)
    else:
        sum_ref[step] = tn(a_ref[...], b_ref[...]).astype(jnp.bfloat16)

    def copies(at):
        for i, (when, out, row, rows, terms, col_from, cols) in enumerate(moves):
            if at is not None and when != at:
                continue
            start = terms[0]
            for entry, scale in terms[1:]:
                start = start + table[entry] * scale
            if len(terms) > 1:
                start = pl.multiple_of(start, 8)
            if isinstance(col_from, tuple):
                chooser, half = col_from
                column = pl.multiple_of(table[chooser] * half, 128)
            else:
                column = col_from
            yield pltpu.make_async_copy(
                sum_ref.at[when, pl.ds(start, rows), pl.ds(column, cols)],
                out_refs[out].at[pl.ds(row, rows), :],
                sems.at[i],
            )

    for at in range(steps):

        @pl.when(step == at)
        def _(at=at):
            for copy in copies(at):
                copy.start()

    @pl.when(step == steps - 1)
    def _():
        for copy in copies(None):
            copy.wait()


def weight_grad(a, b, table, plan, shapes, carried, name):
    tile, by_columns, a_map, b_map, moves = plan
    rows, left = a.shape
    right = b.shape[1]
    if by_columns:
        steps = right // tile
        specs = [
            pl.BlockSpec((rows, left), a_map, pipeline_mode=pl.Buffered(1)),
            pl.BlockSpec((rows, tile), b_map),
        ]
        scratch = [pltpu.VMEM((steps, left, tile), jnp.bfloat16)]
        extra = [pltpu.VMEM((left, rows), jnp.bfloat16)]
    else:
        steps = left // tile
        specs = [
            pl.BlockSpec((rows, tile), a_map),
            pl.BlockSpec((rows, right), b_map, pipeline_mode=pl.Buffered(1)),
        ]
        scratch = [pltpu.VMEM((steps, tile, right), jnp.bfloat16)]
        extra = []
    anywhere = pl.BlockSpec(memory_space=pl.ANY)
    return pl.pallas_call(
        functools.partial(
            weight_grad_kernel, steps, by_columns, moves, len(shapes), len(carried)
        ),
        grid_spec=pltpu.PrefetchScalarGridSpec(
            num_scalar_prefetch=1,
            grid=(steps,),
            in_specs=specs + [anywhere] * len(carried),
            out_specs=[anywhere] * len(shapes),
            scratch_shapes=[*scratch, pltpu.SemaphoreType.DMA((len(moves),)), *extra],
        ),
        out_shape=[jax.ShapeDtypeStruct(s, jnp.bfloat16) for s in shapes],
        input_output_aliases={3 + i: i for i in range(len(carried))},
        compiler_params=pltpu.CompilerParams(vmem_limit_bytes=VMEM_BYTES),
        cost_estimate=cost(2 * rows * left * right, 2 * left * right + 2 * rows * (left + right)),
        name=name,
    )(table, a, b, *carried)


def bits_of(size):
    return size.bit_length() - 1


def label_of(index):
    upper = index >> 1
    return ((upper ^ (upper >> 1)) << 1) | (index & 1)


def index_of(label):
    upper = label >> 1
    shift = 1
    while shift < 32:
        upper = upper ^ (upper >> shift)
        shift *= 2
    return (upper << 1) | (label & 1)


def swap_dp(value, bit):
    size = lax.axis_size("dp")
    return lax.ppermute(
        value, "dp", [(i, index_of(label_of(i) ^ (1 << bit))) for i in range(size)]
    )


def swap_expert(value, bit):
    size = lax.axis_size("expert")
    return lax.ppermute(value, "expert", [(i, i ^ (1 << bit)) for i in range(size)])


def gather_expert(value):
    bits = bits_of(lax.axis_size("expert"))
    parts = {0: value}
    for bit in reversed(range(bits)):
        for r in list(parts):
            parts[r | (1 << bit)] = swap_expert(parts[r], bit)
    return [parts[r] for r in range(1 << bits)]


def gather_ordered(value):
    mine = lax.axis_index("expert")
    for bit in range(bits_of(lax.axis_size("expert"))):
        other = swap_expert(value, bit)
        upper = (mine >> bit & 1) == 1
        value = jnp.concatenate(
            [jnp.where(upper, other, value), jnp.where(upper, value, other)], axis=0
        )
    return value


def gather_expert_stacked(value):
    held, places = value[None], [0]
    for bit in reversed(range(bits_of(lax.axis_size("expert")))):
        held = jnp.concatenate([held, swap_expert(held, bit)])
        places += [place | (1 << bit) for place in places]
    return jnp.concatenate([held[places.index(r)][None] for r in range(len(places))])


def scatter_expert(parts, first_bit=0):
    parts = [[part] for part in parts]
    for bit in range(first_bit, bits_of(lax.axis_size("expert"))):
        left = []
        for kept, away in zip(parts[::2], parts[1::2]):
            away = away[0].astype(jnp.bfloat16) if len(away) == 1 else added(away).astype(jnp.bfloat16)
            kept = kept if len(kept) == 1 else [added(kept).astype(jnp.bfloat16)]
            left.append([*kept, swap_expert(away, bit)])
        parts = left
    return parts[0]


def gather_dp_step(value, bit):
    return jnp.concatenate([value, swap_dp(value, bit)], axis=0)


def gather_dp(value):
    for bit in range(bits_of(lax.axis_size("dp"))):
        value = gather_dp_step(value, bit)
    return value


LINE, PAIR = 4, 2
CORE, CHIP = 8, 10


def tuned(mesh_dp, experts):
    return mesh_dp == LINE * PAIR and experts == 4


def shard_table():
    dp, expert = lax.axis_index("dp"), lax.axis_index("expert")
    relative = jnp.arange(LINE * PAIR, dtype=jnp.int32)
    owners = (dp // PAIR + relative // PAIR) % LINE * PAIR + (dp % PAIR ^ relative % PAIR)
    core, chip = expert & 1, expert >> 1
    return jnp.concatenate([owners, jnp.stack([core, 1 - core, chip, 1 - chip])]).astype(jnp.int32)


def relatives():
    return [(2 * along + across, along, across) for along in range(LINE) for across in range(PAIR)]


def by_shard(shard, moves):
    return (shard, False, lambda j, t: (0, t[j]), lambda j, t: (0, 0), moves)


def halves_map(half_steps):
    return lambda j, t: (
        0,
        jnp.where(j < half_steps, t[CORE + 1] * half_steps + j, (t[CORE] - 1) * half_steps + j),
    )


def expert_down_plan(width, hidden):
    shard = hidden // 8
    moves = [
        (relative, along, across * shard, shard, (0,), 0, width)
        for relative, along, across in relatives()
    ]
    return by_shard(shard, moves), [(PAIR * shard, width)] * LINE


def expert_up_plan(width, hidden):
    shard = width // 8
    steps = hidden // width
    moves = [
        (step, across, (along * steps + step) * shard, shard, (0, (relative, shard)), 0, width)
        for step in range(steps)
        for relative, along, across in relatives()
    ]
    plan = (width, True, lambda j, t: (0, 0), lambda j, t: (0, j), moves)
    return plan, [(LINE * steps * shard, width)] * PAIR


def dense_place(chip_first, chip, along, across):
    outer, inner = (chip, across) if chip_first else (across, chip)
    return (2 * outer + inner) * LINE + along


def dense_up_plan(width, hidden):
    cols, shard = width // 2, width // 8
    rows = shard // 2
    unit = rows * (hidden // width)
    half_steps = hidden // width // 2
    moves = []
    for step in range(2 * half_steps):
        for block in range(2):
            column = 2 * (step % half_steps) + block
            for relative, along, across in relatives():
                for chip in range(2):
                    row = dense_place(True, chip, along, across) * unit + column * rows
                    source = (0, (relative, shard), (CHIP + chip, rows))
                    moves.append((step, step // half_steps, row, rows, source, block * cols, cols))
    return (width, True, lambda j, t: (0, 0), halves_map(half_steps), moves)


def dense_down_plan(width, hidden):
    cols = width // 2
    unit = hidden // 8 // 2
    moves = []
    for relative, along, across in relatives():
        for out in range(2):
            for chip in range(2):
                row = (16 + dense_place(False, chip, along, across)) * unit
                source = (0, (CHIP + chip, unit))
                moves.append((relative, out, row, unit, source, (CORE + 1 - out, cols), cols))
    return by_shard(hidden // 8, moves)


def tail_plan(width, first, count):
    cols, shard = width // 2, width // 8
    rows = shard // 2
    moves = []
    for step in range(2):
        for block in range(count):
            for relative, along, across in relatives():
                for chip in range(2):
                    row = (dense_place(True, chip, along, across) * 4 + first + block) * rows
                    source = (0, (relative, shard), (CHIP + chip, rows))
                    moves.append((step, step, row, rows, source, block * cols, cols))
    return (count * cols, True, lambda j, t: (0, 0), halves_map(1), moves)


def low(parts):
    return added(parts).astype(jnp.bfloat16)


def sync(*values):
    return lax.optimization_barrier(values)


def cut(arrays, count):
    left = arrays[0].shape[0] // count
    return [[a[i * left : (i + 1) * left] for a in arrays] for i in range(count)]


def swap_pair(value):
    return lax.ppermute(value, "dp", [(i, i ^ 1) for i in range(LINE * PAIR)])


def move_line(value, pairs):
    return lax.ppermute(
        value, "dp", [(a * PAIR + i, b * PAIR + i) for a, b in pairs for i in range(PAIR)]
    )


UP = [(0, 1), (1, 2), (2, 3)]
DOWN = [(1, 0), (2, 1), (3, 2)]


def line_first(far, near):
    return move_line(far, UP[:1]), move_line(near, DOWN[2:])


def line_second(middle):
    return move_line(middle, UP[:2]), move_line(middle, DOWN[1:])


def line_third(near, far):
    return move_line(near, UP), move_line(far, DOWN)


def line_direct(parts):
    return [
        move_line(low(parts[ahead]), [(i, (i + ahead) % LINE) for i in range(LINE)])
        for ahead in range(1, LINE)
    ]


def both_chips(total):
    other = swap_expert(total, 1)
    upper = (lax.axis_index("expert") >> 1) == 1
    return jnp.concatenate([jnp.where(upper, other, total), jnp.where(upper, total, other)], axis=0)


def both_cores(total):
    other = swap_expert(total, 0)
    upper = (lax.axis_index("expert") & 1) == 1
    return jnp.where(upper, other, total), jnp.where(upper, total, other)


def swap_stack(held, bit):
    return jnp.concatenate([held, swap_expert(held, bit)])


def stack_order(held):
    places = [0]
    for bit in reversed(range(bits_of(held.shape[0]))):
        places += [place | (1 << bit) for place in places]
    return jnp.concatenate([held[places.index(r)][None] for r in range(len(places))])


def gather_chips(value):
    parts = {0: value}
    for bit in reversed(range(1, bits_of(lax.axis_size("expert")))):
        for r in list(parts):
            parts[r | (1 << bit)] = swap_expert(parts[r], bit)
    return parts


def rows_to_columns(stacked, count):
    rows = stacked.shape[0] // count
    return jnp.concatenate([stacked[i * rows : (i + 1) * rows] for i in range(count)], axis=1)


def added(parts):
    total = parts[0].astype(jnp.float32)
    for part in parts[1:]:
        total = total + part.astype(jnp.float32)
    return total


def scatter_far(parts):
    came = []
    for bit in range(1, bits_of(lax.axis_size("expert"))):
        left = []
        for kept, away in zip(parts[::2], parts[1::2]):
            moved = swap_expert(away, bit)
            if kept is None:
                came.append(moved)
                left.append(None)
            else:
                left.append(added([kept, moved]).astype(jnp.bfloat16))
        parts = left
    return came


def on_device(
    patches,
    time_embed,
    ada_weight,
    ada_bias,
    qkv_weight,
    out_weight,
    up_weight,
    down_weight,
    expert_up,
    expert_down,
    routes,
    gate_weights,
    cotangent,
):
    tokens, width = patches.shape
    latents = time_embed.shape[0]
    seq_len = tokens // latents
    experts = lax.axis_size("expert")
    dp_size = lax.axis_size("dp")
    dp_index = lax.axis_index("dp")
    expert_index = lax.axis_index("expert")
    capacity = 5 * tokens // (2 * experts)

    hidden = up_weight.shape[1]
    blocks = 2
    groups = experts // blocks
    table = shard_table()

    info = jnp.concatenate(
        [
            routes.T.astype(jnp.float32),
            gate_weights.T,
            time_embed.astype(jnp.float32).reshape(-1, tokens),
        ],
        axis=0,
    )
    info = swap_stack(info[None], bits_of(experts) - 1)
    info, cotangent = sync(info, cotangent)
    cots = gather_chips(cotangent)
    cots[1] = swap_expert(cotangent, 0)
    for bit in reversed(range(bits_of(experts) - 1)):
        info = swap_stack(info, bit)
    info_all = stack_order(info)
    cond = jax.nn.silu(time_embed.astype(jnp.float32)).astype(jnp.bfloat16)
    modulation = jnp.dot(cond, ada_weight, preferred_element_type=jnp.float32) + ada_bias
    mod = modulation.reshape(latents, 6, width)
    first_in, qkv_all, log_total, attended, attn_proj, second_in = attn_forward(
        patches, mod, qkv_weight, out_weight
    )
    second_in, info_all, cots[1] = sync(second_in, info_all, cots[1])

    seconds = gather_chips(second_in)
    seconds[1] = swap_expert(second_in, 0)
    routed = route(
        expert_index[None], info_all[:, :4], info_all[:, 4:].reshape(experts * latents, width),
        ada_weight, ada_bias, tokens,
    )
    routed, seconds[1] = sync(routed, seconds[1])
    for r in range(2, experts, 2):
        cots[r + 1] = swap_expert(cots[r], 0)

    def run_group(group, carried):
        span = range(group * blocks, (group + 1) * blocks)
        results = expert_forward_backward(
            [seconds[r] for r in span], [cots[r] for r in span], *routed, expert_up[0], expert_down[0],
            capacity, groups, group, carried,
        )
        return results[: 4 + blocks], results[4 + blocks :]

    carried, near = run_group(0, [])
    carried, near, seconds, cots = sync(carried, near, seconds, cots)
    for r in range(2, experts, 2):
        seconds[r + 1] = swap_expert(seconds[r], 0)
    near_came = swap_expert(near[1], 0)
    backs = {}
    for group in range(1, groups):
        carried, backs[group] = run_group(group, carried)
    carried, backs, near_came = sync(carried, backs, near_came)
    act_rows, grad_pre_rows, rows_in, grad_rows, mix_even, mix_odd = carried

    fast = tuned(dp_size, experts)
    backs_came = {group: swap_expert(backs[group][1], 0) for group in backs}
    ups, downs, first_downs = (), (), ()
    if fast:
        plan, shapes = expert_down_plan(width, hidden)
        downs = weight_grad(act_rows, grad_rows, table, plan, shapes, [], "grad_expert_down")
    downs, backs_came, rows_in = sync(downs, backs_came, rows_in)
    far = [None] + [low([backs[group][0], backs_came[group]]) for group in range(1, groups)]
    far_sum = scatter_far(far)
    if fast:
        first_downs = line_first(downs[3], downs[1])
        plan, shapes = expert_up_plan(width, hidden)
        ups = weight_grad(rows_in, grad_pre_rows, table, plan, shapes, [], "grad_expert_up")
    ups, second_in = sync(ups, second_in)

    mix_came = swap_expert(mix_odd, 0)
    if fast:
        up_came = swap_pair(ups[1])
    shared = shared_forward_backward(second_in, cotangent, mod[:, 5], up_weight, down_weight)
    shared, far_sum, mix_came, first_downs = sync(shared, far_sum, mix_came, first_downs)
    shared_act, grad_shared_pre, grad_shared, shared_out, grad_second = shared
    mix = added([mix_even, mix_came])
    mix = scatter_expert([mix[i * tokens : (i + 1) * tokens] for i in range(groups)], 1)
    if fast:
        second_downs = line_second(low([downs[2], *first_downs]))
        dense_shapes = [(2 * hidden, width // 2)] * 2
        dense = weight_grad(
            second_in, grad_shared_pre, table, dense_up_plan(width, hidden), dense_shapes, [], "grad_up"
        )
        dense = weight_grad(
            shared_act, grad_shared, table, dense_down_plan(width, hidden), dense_shapes, dense,
            "grad_down",
        )
        dense, attn_proj, mix = sync(dense, attn_proj, mix)
        dense_came = swap_expert(dense[0], 0)

    backward = attn_backward(
        patches, mod, attn_proj, qkv_all, log_total, cotangent, out_weight,
        [grad_second, near[0], near_came, *far_sum],
    )
    if fast:
        backward, dense_came, second_downs = sync(backward, dense_came, second_downs)
    grad_qkv_rows, grad_attn, grad_middle, grad_mod_early = backward
    if fast:
        third_downs = line_third(low([downs[1], second_downs[0]]), low([downs[3], second_downs[1]]))
        first, second = cut([dense[1], dense_came], 2)
        first, second = cut(first, 2), cut(second, 2)
        first_came = swap_expert(low(first[1]), 1)
        second_came = swap_pair(low(second[1]))
        tail_shapes = [(4 * width, width // 2)] * 2
        tail = weight_grad(
            first_in, grad_qkv_rows, table, tail_plan(width, 0, 3), tail_shapes, [], "grad_qkv"
        )
        tail = weight_grad(
            attended, grad_attn, table, tail_plan(width, 3, 1), tail_shapes, tail, "grad_out"
        )
        tail, up_came, grad_middle = sync(tail, up_came, grad_middle)
        tail_came = swap_expert(tail[0], 0)
        ups = cut([ups[0], up_came], LINE)
        up_near, up_far = low(ups[1]), low(ups[3])
        up_cames = line_first(up_far, up_near)
    inner = input_backward(patches, mod, grad_qkv_rows, grad_middle, qkv_weight)
    grad_input, grad_mod_late = inner

    middle = patches.astype(jnp.float32).reshape(latents, seq_len, width) + mod[
        :, 2:3
    ] * attn_proj.reshape(latents, seq_len, width)
    branch = (shared_out + added(mix)).reshape(latents, seq_len, width)
    block_out = (middle + mod[:, 5:6] * branch).reshape(tokens, width).astype(jnp.bfloat16)
    grad_gate_two = jnp.sum(
        cotangent.astype(jnp.float32).reshape(latents, seq_len, width) * branch, axis=1
    )
    local_counts = jnp.sum(
        (routes[:, :, None] == jnp.arange(experts, dtype=jnp.int32)).astype(jnp.int32),
        axis=(0, 1),
    )
    count_parts = jnp.concatenate([local_counts // 128, local_counts % 128]).astype(jnp.bfloat16)
    count_rows = jnp.zeros((latents, 128), jnp.bfloat16).at[0, : 2 * experts].set(count_parts)
    mods = jnp.concatenate(
        [
            grad_mod_late.reshape(latents, 2 * width).astype(jnp.bfloat16),
            grad_mod_early.reshape(latents, 3 * width).astype(jnp.bfloat16),
            grad_gate_two.astype(jnp.bfloat16),
            cond,
            count_rows,
        ],
        axis=1,
    )

    if fast:
        mods, block_out, tail_came, third_downs, first_came, second_came = sync(
            mods, block_out, tail_came, third_downs, first_came, second_came
        )
        own, away = cut([downs[0], *third_downs], 2)
        down_came = swap_pair(low(away))
        second = cut([*second[0], second_came], 2)
        second_came = swap_expert(low(second[1]), 1)
        first = cut([*first[0], first_came], 2)
        first_came = swap_pair(low(first[1]))
        third = cut([tail[1], tail_came], 2)
        third_came = swap_expert(low(third[1]), 1)
        mods_all = gather_ordered(mods)
        up_cames, second_came, down_came, mods_all = sync(up_cames, second_came, down_came, mods_all)

        up_cames = line_second(low([*ups[2], *up_cames]))
        second = cut([*second[0], second_came], LINE)
        second_cames = line_direct(second)
        sum_e_down = added([*own, down_came])
        mods_all = gather_dp_step(mods_all, 0)
        up_cames, first_came, third_came, mods_all, sum_e_down = sync(
            up_cames, first_came, third_came, mods_all, sum_e_down
        )

        third = cut([*third[0], third_came], 2)
        third_came = swap_pair(low(third[1]))
        up_cames = line_third(low([up_near, up_cames[0]]), low([up_far, up_cames[1]]))
        first = cut([*first[0], first_came], LINE)
        first_cames = line_direct(first)
        mods_all = gather_dp_step(mods_all, 1)
        second_cames, up_cames, third_came, mods_all = sync(
            second_cames, up_cames, third_came, mods_all
        )

        third = cut([*third[0], third_came], LINE)
        third_cames = line_direct(third)
        mods_all = gather_dp_step(mods_all, 2)
        sum_e_up = rows_to_columns(added([*ups[0], *up_cames]), hidden // width)
        first_cames, sum_e_up = sync(first_cames, sum_e_up)
        dense_total = both_chips(
            jnp.concatenate([low([*first[0], *first_cames]), low([*second[0], *second_cames])], axis=0)
        )
        tail_total = both_chips(low([*third[0], *third_cames]))
        dense_sums, tail_sums = both_cores(dense_total), both_cores(tail_total)

        def columns(arrays):
            return jnp.concatenate(arrays, axis=1).astype(jnp.float32)

        half = hidden // 16
        sum_w_up, sum_w_down = [], []
        for chip in range(2):
            at = 2 * half * chip
            sum_w_up.append(
                columns([rows_to_columns(s[at : at + half], hidden // width) for s in dense_sums])
            )
            sum_w_down.append(columns([s[at + half : at + 2 * half] for s in dense_sums]))
        sum_w_up, sum_w_down = jnp.concatenate(sum_w_up), jnp.concatenate(sum_w_down)
        half = width // 16
        sum_w_qkv, sum_w_out = [], []
        for chip in range(2):
            at = 4 * half * chip
            sum_w_qkv.append(
                columns([rows_to_columns(s[at : at + 3 * half], 3) for s in tail_sums])
            )
            sum_w_out.append(columns([s[at + 3 * half : at + 4 * half] for s in tail_sums]))
        sum_w_qkv, sum_w_out = jnp.concatenate(sum_w_qkv), jnp.concatenate(sum_w_out)
    else:
        mods_all = gather_dp(gather_ordered(mods))

        def summed(left, right, axes):
            share = lax.psum_scatter(
                tn(left, right).astype(jnp.bfloat16), "dp", scatter_dimension=0, tiled=True
            )
            return (lax.psum(share, axes) if axes else share).astype(jnp.float32)

        sum_w_up = summed(second_in, grad_shared_pre, "expert")
        sum_w_down = summed(shared_act, grad_shared, "expert")
        sum_w_qkv = summed(first_in, grad_qkv_rows, "expert")
        sum_w_out = summed(attended, grad_attn, "expert")
        sum_e_up = summed(rows_in, grad_pre_rows, None)
        sum_e_down = summed(act_rows, grad_rows, None)

    grad_mod_all = mods_all[:, : 6 * width]
    count_sums = jnp.sum(mods_all[:, 7 * width :].astype(jnp.float32), axis=0).astype(jnp.int32)
    counts = count_sums[:experts] * 128 + count_sums[experts : 2 * experts]
    ada_rows = width // dp_size
    cond_mine = lax.dynamic_slice_in_dim(
        mods_all[:, 6 * width : 7 * width].T, dp_index * ada_rows, ada_rows, axis=0
    )
    sum_ada = jnp.dot(cond_mine, grad_mod_all, preferred_element_type=jnp.float32)
    bias_all = jnp.sum(grad_mod_all.astype(jnp.float32), axis=0)
    bias_size = bias_all.shape[0] // dp_size
    sum_bias = lax.dynamic_slice_in_dim(bias_all, dp_index * bias_size, bias_size)
    return (
        block_out,
        grad_input,
        sum_ada,
        sum_bias,
        sum_w_qkv,
        sum_w_out,
        sum_w_up,
        sum_w_down,
        sum_e_up[None],
        sum_e_down[None],
        counts,
    )


def solution(mesh):
    in_specs = (
        P(("dp", "expert"), None),
        P(("dp", "expert"), None),
        P(),
        P(),
        P(),
        P(),
        P(),
        P(),
        P("expert", None, None),
        P("expert", None, None),
        P(("dp", "expert"), None),
        P(("dp", "expert"), None),
        P(("dp", "expert"), None),
    )
    out_specs = (
        P(("dp", "expert"), None),
        P(("dp", "expert"), None),
        P("dp", None),
        P("dp"),
        P("dp", None),
        P("dp", None),
        P("dp", None),
        P("dp", None),
        P("expert", "dp", None),
        P("expert", "dp", None),
        P(),
    )
    return jax.shard_map(
        on_device, mesh=mesh, in_specs=in_specs, out_specs=out_specs, check_vma=False
    )
```

```python
import functools
import math

import jax
import jax.numpy as jnp
import numpy as np
from jax import lax
from jax.experimental import pallas as pl
from jax.experimental.pallas import tpu as pltpu
from jax.sharding import PartitionSpec as P

HEAD_DIM = 64
VMEM_BYTES = 56 << 20
SHRINK = 1
SQRT_TWO_OVER_PI = math.sqrt(2.0 / math.pi)


def nt(a,b): return lax.dot_general(a,b,(((1,),(1,)),((),())),preferred_element_type=jnp.float32)
def nn(a,b): return lax.dot_general(a,b,(((1,),(0,)),((),())),preferred_element_type=jnp.float32)
def tn(a,b): return lax.dot_general(a,b,(((0,),(0,)),((),())),preferred_element_type=jnp.float32)

def normalized(values_in):
    row_mean = jnp.mean(values_in, axis=-1, keepdims=True)
    centered = values_in - row_mean
    row_var = jnp.mean(centered * centered, axis=-1, keepdims=True)
    inverse = lax.rsqrt(row_var + 1e-06)
    return centered * inverse, inverse

def norm_back(grad_out, scale, normal, inverse):
    inner = grad_out * (1.0 + scale)
    mean_inner = jnp.mean(inner, axis=-1, keepdims=True)
    mean_cross = jnp.mean(inner * normal, axis=-1, keepdims=True)
    return inverse * (inner - mean_inner - normal * mean_cross)

def head_lanes(pair, head):
    lane = lax.broadcasted_iota(jnp.int32, pair.shape, 1)
    return jnp.where(lane // HEAD_DIM == head, pair, jnp.zeros_like(pair))

def attn_forward_kernel(x_ref, mod_ref, wqkv_ref, wout_ref, first_ref, qkv_ref, lse_ref, att_ref, proj_ref, second_ref):
    width = x_ref.shape[1]
    x = x_ref[...].astype(jnp.float32)
    mod = mod_ref[0]
    normal, _ = normalized(x)
    first_ref[...] = (normal * (1.0 + mod[1:2]) + mod[0:1]).astype(jnp.bfloat16)
    qkv_ref[...] = nn(first_ref[...], wqkv_ref[...]).astype(jnp.bfloat16)
    lane = 2 * HEAD_DIM
    for pair in range(width // lane):
        q2 = qkv_ref[:, pair * lane : (pair + 1) * lane]
        k2 = qkv_ref[:, width + pair * lane : width + (pair + 1) * lane]
        v2 = qkv_ref[:, 2 * width + pair * lane : 2 * width + (pair + 1) * lane]
        v2t = v2.T
        outs = []
        for head in range(2):
            scores = nt(head_lanes(k2, head), q2) * HEAD_DIM ** (-0.5)
            peak = jnp.max(scores, axis=0, keepdims=True)
            powers = jnp.exp(scores - peak)
            total = jnp.sum(powers, axis=0, keepdims=True)
            lse_ref[0, 2 * pair + head : 2 * pair + head + 1, :] = peak + jnp.log(total)
            probs = (powers * (1.0 / total)).astype(jnp.bfloat16)
            outs.append(nn(v2t[head * HEAD_DIM : (head + 1) * HEAD_DIM], probs))
        both = jnp.concatenate(outs, axis=0).astype(jnp.bfloat16)
        att_ref[:, pair * lane : (pair + 1) * lane] = both.T
    proj = nn(att_ref[...], wout_ref[...])
    proj_ref[...] = proj
    middle = x + mod[2:3] * proj
    normal2, _ = normalized(middle)
    second_ref[...] = (normal2 * (1.0 + mod[4:5]) + mod[3:4]).astype(jnp.bfloat16)

def attn_forward(patches, mod, wqkv, wout):
    tokens, width = patches.shape
    latents = mod.shape[0]
    seq = tokens // latents
    heads = width // HEAD_DIM
    rows = lambda cols: pl.BlockSpec((seq, cols), lambda i: (i, 0))
    whole = lambda a: pl.BlockSpec(a.shape, lambda i: (0, 0), pipeline_mode=pl.Buffered(1))
    return pl.pallas_call(
        attn_forward_kernel, grid=(latents,),
        in_specs=[rows(width), pl.BlockSpec((1,) + mod.shape[1:], lambda i: (i, 0, 0)), whole(wqkv), whole(wout)],
        out_specs=[rows(width), rows(3 * width), pl.BlockSpec((1, heads, seq), lambda i: (i, 0, 0)), rows(width), rows(width), rows(width)],
        out_shape=[jax.ShapeDtypeStruct((tokens, width), jnp.bfloat16), jax.ShapeDtypeStruct((tokens, 3 * width), jnp.bfloat16),
            jax.ShapeDtypeStruct((latents, heads, seq), jnp.float32), jax.ShapeDtypeStruct((tokens, width), jnp.bfloat16),
            jax.ShapeDtypeStruct((tokens, width), jnp.float32), jax.ShapeDtypeStruct((tokens, width), jnp.bfloat16)],
        compiler_params=pltpu.CompilerParams(vmem_limit_bytes=VMEM_BYTES), cost_estimate=cost(8 * tokens * width * width, 8 * width * width), name="attn_forward")(patches, mod, wqkv, wout)

def attn_backward_kernel(extra, x_ref, mod_ref, proj_ref, qkv_ref, lse_ref, cot_ref, wout_ref, *rest):
    adds = rest[:extra]
    gqkv_ref, gattn_ref, gmid_ref, gmod_ref = rest[extra:]
    width = x_ref.shape[1]
    x = x_ref[...].astype(jnp.float32)
    mod = mod_ref[0]
    proj = proj_ref[...]
    normal, inverse = normalized(x + mod[2:3] * proj)
    grad_second = adds[0][...].astype(jnp.float32)
    for a in adds[1:]:
        grad_second = grad_second + a[...].astype(jnp.float32)
    gmod_ref[0, 1:2, :] = jnp.sum(grad_second, axis=0, keepdims=True)
    gmod_ref[0, 2:3, :] = jnp.sum(grad_second * normal, axis=0, keepdims=True)
    grad_middle = cot_ref[...].astype(jnp.float32) + norm_back(grad_second, mod[4:5], normal, inverse)
    gmid_ref[...] = grad_middle
    gmod_ref[0, 0:1, :] = jnp.sum(grad_middle * proj, axis=0, keepdims=True)
    gattn_ref[...] = (mod[2:3] * grad_middle).astype(jnp.bfloat16)
    grad_att = nt(gattn_ref[...], wout_ref[...]).astype(jnp.bfloat16)
    lane = 2 * HEAD_DIM
    scale = HEAD_DIM ** (-0.5)
    for pair in range(width // lane):
        sl = slice(pair * lane, (pair + 1) * lane)
        q2 = qkv_ref[:, pair * lane : (pair + 1) * lane]
        k2 = qkv_ref[:, width + pair * lane : width + (pair + 1) * lane]
        v2 = qkv_ref[:, 2 * width + pair * lane : 2 * width + (pair + 1) * lane]
        do2 = grad_att[:, sl]
        k2t = k2.T
        gq, gk, gv = [], [], []
        for head in range(2):
            scores = nt(head_lanes(k2, head), q2) * scale
            probs = jnp.exp(scores - lse_ref[0, 2 * pair + head : 2 * pair + head + 1, :])
            grad_probs = nt(head_lanes(v2, head), do2)
            inner = jnp.sum(probs * grad_probs, axis=0, keepdims=True)
            grad_scores = (probs * (grad_probs - inner)).astype(jnp.bfloat16)
            gv.append(nn(probs.astype(jnp.bfloat16), do2))
            gk.append(nn(grad_scores, q2))
            gq.append(nn(k2t[head * HEAD_DIM : (head + 1) * HEAD_DIM], grad_scores))
        low = lax.broadcasted_iota(jnp.int32, gv[0].shape, 1) < HEAD_DIM
        gqt = (jnp.concatenate(gq, axis=0) * scale).astype(jnp.bfloat16)
        gqkv_ref[:, pair * lane : (pair + 1) * lane] = gqt.T
        gqkv_ref[:, width + pair * lane : width + (pair + 1) * lane] = (jnp.where(low, gk[0], gk[1]) * scale).astype(jnp.bfloat16)
        gqkv_ref[:, 2 * width + pair * lane : 2 * width + (pair + 1) * lane] = jnp.where(low, gv[0], gv[1]).astype(jnp.bfloat16)

def attn_backward(patches, mod, proj, qkv, lse, cot, wout, adds):
    tokens, width = patches.shape
    latents = mod.shape[0]
    seq = tokens // latents
    rows = lambda cols: pl.BlockSpec((seq, cols), lambda i: (i, 0))
    per = lambda a: pl.BlockSpec((1,) + a.shape[1:], lambda i: (i, 0, 0))
    whole = lambda a: pl.BlockSpec(a.shape, lambda i: (0, 0), pipeline_mode=pl.Buffered(1))
    return pl.pallas_call(
        functools.partial(attn_backward_kernel, len(adds)), grid=(latents,),
        in_specs=[rows(width), per(mod), rows(width), rows(3 * width), per(lse), rows(width), whole(wout)] + [rows(width)] * len(adds),
        out_specs=[rows(3 * width), rows(width), rows(width), pl.BlockSpec((1, 3, width), lambda i: (i, 0, 0))],
        out_shape=[jax.ShapeDtypeStruct((tokens, 3 * width), jnp.bfloat16), jax.ShapeDtypeStruct((tokens, width), jnp.bfloat16),
            jax.ShapeDtypeStruct((tokens, width), jnp.float32), jax.ShapeDtypeStruct((latents, 3, width), jnp.float32)],
        compiler_params=pltpu.CompilerParams(vmem_limit_bytes=VMEM_BYTES), cost_estimate=cost(8 * tokens * width * width, 8 * width * width), name="attn_backward")(patches, mod, proj, qkv, lse, cot, wout, *adds)

def input_backward_kernel(x_ref, mod_ref, gqkv_ref, gmid_ref, wqkv_ref, gin_ref, gmod_ref):
    mod = mod_ref[0]
    normal, inverse = normalized(x_ref[...].astype(jnp.float32))
    grad_first = nt(gqkv_ref[...], wqkv_ref[...])
    gmod_ref[0, 0:1, :] = jnp.sum(grad_first, axis=0, keepdims=True)
    gmod_ref[0, 1:2, :] = jnp.sum(grad_first * normal, axis=0, keepdims=True)
    gin_ref[...] = gmid_ref[...] + norm_back(grad_first, mod[1:2], normal, inverse)

def input_backward(patches, mod, gqkv, gmid, wqkv):
    tokens, width = patches.shape
    latents = mod.shape[0]
    seq = tokens // latents
    rows = lambda cols: pl.BlockSpec((seq, cols), lambda i: (i, 0))
    per = lambda a: pl.BlockSpec((1,) + a.shape[1:], lambda i: (i, 0, 0))
    whole = lambda a: pl.BlockSpec(a.shape, lambda i: (0, 0), pipeline_mode=pl.Buffered(1))
    return pl.pallas_call(
        input_backward_kernel, grid=(latents,),
        in_specs=[rows(width), per(mod), rows(3 * width), rows(width), whole(wqkv)],
        out_specs=[rows(width), pl.BlockSpec((1, 2, width), lambda i: (i, 0, 0))],
        out_shape=[jax.ShapeDtypeStruct((tokens, width), jnp.float32), jax.ShapeDtypeStruct((latents, 2, width), jnp.float32)],
        compiler_params=pltpu.CompilerParams(vmem_limit_bytes=VMEM_BYTES), cost_estimate=cost(6 * tokens * width * width, 6 * width * width), name="input_backward")(patches, mod, gqkv, gmid, wqkv)


def cost(flops, size):
    return pl.CostEstimate(flops=int(flops) // SHRINK, bytes_accessed=int(size) // SHRINK, transcendentals=0)


def feed_forward_step(x_ref, g_ref, up_ref, down_ref, act_ref, gpre_ref, out_acc, grad_acc):
    inner_scale = SQRT_TWO_OVER_PI
    cubic = 0.044715
    pre = nn(x_ref[...], up_ref[...])
    grad_act = nt(g_ref[...], down_ref[...])
    squared = pre * pre
    bent = jnp.tanh(pre * (inner_scale + (inner_scale * cubic) * squared))
    half = 0.5 + 0.5 * bent
    act = (pre * half).astype(jnp.bfloat16)
    slope = half + (0.5 * pre) * (1.0 - bent * bent) * (
        inner_scale + (3.0 * cubic * inner_scale) * squared
    )
    grad_pre = (grad_act * slope).astype(jnp.bfloat16)
    act_ref[...] = act
    gpre_ref[...] = grad_pre
    out_acc[...] += nn(act, down_ref[...])
    grad_acc[...] += nt(grad_pre, up_ref[...])


def shared_kernel(
    x_ref, cot_ref, gate_ref, up_ref, down_ref,
    act_ref, gpre_ref, g_ref, out_ref, grad_ref,
    out_acc, grad_acc,
):
    step = pl.program_id(0)
    latents = gate_ref.shape[0]
    seq = x_ref.shape[0] // latents

    @pl.when(step == 0)
    def _():
        out_acc[...] = jnp.zeros_like(out_acc)
        grad_acc[...] = jnp.zeros_like(grad_acc)
        for i in range(latents):
            rows = slice(i * seq, (i + 1) * seq)
            g_ref[rows, :] = (gate_ref[i : i + 1, :] * cot_ref[rows, :].astype(jnp.float32)).astype(
                jnp.bfloat16
            )

    feed_forward_step(x_ref, g_ref, up_ref, down_ref, act_ref, gpre_ref, out_acc, grad_acc)

    @pl.when(step == pl.num_programs(0) - 1)
    def _():
        out_ref[...] = out_acc[...]
        grad_ref[...] = grad_acc[...]


def tile_of(width):
    return width // 4 if width % 512 == 0 else width


def still(array):
    return pl.BlockSpec(
        array.shape, lambda j, n=len(array.shape): (0,) * n, pipeline_mode=pl.Buffered(1)
    )


def shared_forward_backward(x, cot, gate, up, down):
    rows, width = x.shape
    hidden = up.shape[1]
    tile = tile_of(hidden)
    out = jax.ShapeDtypeStruct((rows, width), jnp.float32)
    wide = jax.ShapeDtypeStruct((rows, hidden), jnp.bfloat16)
    fixed = pl.BlockSpec((rows, width), lambda j: (0, 0))
    column = pl.BlockSpec((rows, tile), lambda j: (0, j))
    return pl.pallas_call(
        shared_kernel,
        grid=(hidden // tile,),
        in_specs=[
            still(x), still(cot), still(gate),
            pl.BlockSpec((width, tile), lambda j: (0, j)),
            pl.BlockSpec((tile, width), lambda j: (j, 0)),
        ],
        out_specs=[column, column, fixed, fixed, fixed],
        out_shape=[wide, wide, jax.ShapeDtypeStruct((rows, width), jnp.bfloat16), out, out],
        scratch_shapes=[pltpu.VMEM((rows, width), jnp.float32)] * 2,
        compiler_params=pltpu.CompilerParams(vmem_limit_bytes=VMEM_BYTES),
        cost_estimate=cost(8 * rows * width * hidden, 4 * width * hidden + 4 * rows * hidden),
        name="shared_ffn",
    )(x, cot, gate, up, down)


def expert_kernel(blocks, carried, *refs):
    xs, cots = refs[:blocks], refs[blocks : 2 * blocks]
    slot_row, slot_col, gate_col, gate_two, up_ref, down_ref = refs[2 * blocks : 2 * blocks + 6]
    rest = refs[2 * blocks + 6 + carried :]
    act_ref, gpre_ref, x_ref, g_ref = rest[:4]
    mixes, backs = rest[4 : 4 + blocks], rest[4 + blocks : 4 + 2 * blocks]
    out_acc, grad_acc = rest[4 + 2 * blocks :]
    step = pl.program_id(0)
    tokens = xs[0].shape[0]
    capacity = x_ref.shape[0] // blocks
    latents = gate_two.shape[1]
    seq = tokens // latents

    @pl.when(step == 0)
    def _():
        out_acc[...] = jnp.zeros_like(out_acc)
        grad_acc[...] = jnp.zeros_like(grad_acc)
        for b in range(blocks):
            rows = slice(b * capacity, (b + 1) * capacity)
            places = lax.broadcasted_iota(jnp.int32, (capacity, tokens), 0)
            pick = (places == slot_row[b]).astype(jnp.float32).astype(jnp.bfloat16)
            x_ref[rows, :] = nn(pick, xs[b][...]).astype(jnp.bfloat16)
            grads = []
            for i in range(latents):
                part = slice(i * seq, (i + 1) * seq)
                branch = gate_two[b, i : i + 1, :] * cots[b][part, :].astype(jnp.float32)
                grads.append((gate_col[b, part, :] * branch).astype(jnp.bfloat16))
            grad = jnp.concatenate(grads, axis=0)
            g_ref[rows, :] = nn(pick, grad).astype(jnp.bfloat16)

    feed_forward_step(x_ref, g_ref, up_ref, down_ref, act_ref, gpre_ref, out_acc, grad_acc)

    @pl.when(step == pl.num_programs(0) - 1)
    def _():
        for b in range(blocks):
            rows = slice(b * capacity, (b + 1) * capacity)
            places = lax.broadcasted_iota(jnp.int32, (tokens, capacity), 1)
            pick = (places == slot_col[b]).astype(jnp.float32).astype(jnp.bfloat16)
            backs[b][...] = nn(pick, grad_acc[rows, :].astype(jnp.bfloat16)).astype(jnp.bfloat16)
            mixed = nn(pick, out_acc[rows, :].astype(jnp.bfloat16))
            mixes[b][...] = (gate_col[b] * mixed).astype(jnp.bfloat16)


def expert_forward_backward(
    xs, cots, slot_row, slot_col, gate_col, gate_two, up, down, capacity, groups, group, carried
):
    blocks = len(xs)
    tokens, width = xs[0].shape
    hidden = up.shape[1]
    tile = tile_of(hidden)
    rows = blocks * capacity
    wide = jax.ShapeDtypeStruct((rows * groups, hidden), jnp.bfloat16)
    slim = jax.ShapeDtypeStruct((rows * groups, width), jnp.bfloat16)
    mixture = jax.ShapeDtypeStruct((tokens * groups, width), jnp.bfloat16)
    token = jax.ShapeDtypeStruct((tokens, width), jnp.bfloat16)
    column = pl.BlockSpec((rows, tile), lambda j: (group, j))
    own = pl.BlockSpec((rows, width), lambda j: (group, 0))
    mixed = pl.BlockSpec((tokens, width), lambda j: (group, 0))
    fixed = pl.BlockSpec((tokens, width), lambda j: (0, 0))
    small = [slot_row, slot_col, gate_col, gate_two]
    first = 2 * blocks + 6
    return pl.pallas_call(
        functools.partial(expert_kernel, blocks, len(carried)),
        grid=(hidden // tile,),
        in_specs=[still(a) for a in (*xs, *cots)]
        + [
            pl.BlockSpec(
                (blocks,) + a.shape[1:], lambda j, n=len(a.shape) - 1: (group,) + (0,) * n,
                pipeline_mode=pl.Buffered(1),
            )
            for a in small
        ]
        + [
            pl.BlockSpec((width, tile), lambda j: (0, j)),
            pl.BlockSpec((tile, width), lambda j: (j, 0)),
        ]
        + [pl.BlockSpec(memory_space=pl.ANY)] * len(carried),
        out_specs=[column, column, own, own] + [mixed] * blocks + [fixed] * blocks,
        scratch_shapes=[pltpu.VMEM((rows, width), jnp.float32)] * 2,
        out_shape=[wide, wide, slim, slim] + [mixture] * blocks + [token] * blocks,
        input_output_aliases={first + i: i for i in range(len(carried))},
        compiler_params=pltpu.CompilerParams(vmem_limit_bytes=VMEM_BYTES),
        cost_estimate=cost(8 * rows * width * hidden, 4 * width * hidden + 4 * rows * hidden),
        name="expert_ffn",
    )(*xs, *cots, *small, up, down, *carried)


def route_kernel(index_ref, info_ref, time_ref, ada_ref, bias_ref, row_ref, col_ref, gate_ref, two_ref):
    experts, _, tokens = row_ref.shape
    latents = time_ref.shape[0] // experts
    expert = index_ref[0]
    slots, gates = [], []
    before = (
        lax.broadcasted_iota(jnp.int32, (tokens, tokens), 0)
        < lax.broadcasted_iota(jnp.int32, (tokens, tokens), 1)
    ).astype(jnp.float32).astype(jnp.bfloat16)
    for r in range(experts):
        routes = info_ref[r, 0:2, :].astype(jnp.int32)
        named = routes == expert
        member = jnp.sum(named.astype(jnp.float32), axis=0, keepdims=True)
        earlier = nn(member.astype(jnp.bfloat16), before)
        slot = jnp.where(member > 0.5, earlier, float(tokens))
        row_ref[r] = slot.astype(jnp.int32)
        slots.append(slot)
        gates.append(
            jnp.sum(jnp.where(named, info_ref[r, 2:4, :], 0.0), axis=0, keepdims=True)
        )
    turned = jnp.concatenate(slots + gates, axis=0).T
    for r in range(experts):
        col_ref[r] = turned[:, r : r + 1].astype(jnp.int32)
        gate_ref[r] = turned[:, experts + r : experts + r + 1]
    times = time_ref[...]
    cond = (times / (1.0 + jnp.exp(-times))).astype(jnp.bfloat16)
    gate_two = nn(cond, ada_ref[...]) + bias_ref[...]
    for r in range(experts):
        two_ref[r] = gate_two[r * latents : (r + 1) * latents]


def route(expert, info, times, ada_weight, ada_bias, tokens):
    experts = info.shape[0]
    width = times.shape[1]
    latents = times.shape[0] // experts
    vmem = pl.BlockSpec(memory_space=pltpu.VMEM)
    return pl.pallas_call(
        route_kernel,
        grid=(1,),
        in_specs=[
            pl.BlockSpec(memory_space=pltpu.SMEM), still(info), still(times),
            pl.BlockSpec((width, width), lambda j: (0, 5)),
            pl.BlockSpec((1, width), lambda j: (0, 5)),
        ],
        out_specs=[vmem] * 4,
        out_shape=[
            jax.ShapeDtypeStruct((experts, 1, tokens), jnp.int32),
            jax.ShapeDtypeStruct((experts, tokens, 1), jnp.int32),
            jax.ShapeDtypeStruct((experts, tokens, 1), jnp.float32),
            jax.ShapeDtypeStruct((experts, latents, width), jnp.float32),
        ],
        compiler_params=pltpu.CompilerParams(vmem_limit_bytes=VMEM_BYTES),
        name="route",
    )(expert, info, times, ada_weight, ada_bias[None])


def weight_grad_kernel(steps, by_columns, moves, outs, carried, table, a_ref, b_ref, *rest):
    rest = rest[carried:]
    out_refs = rest[:outs]
    sum_ref, sems = rest[outs], rest[outs + 1]
    step = pl.program_id(0)
    if by_columns:
        turned = rest[outs + 2]

        @pl.when(step == 0)
        def _():
            turned[...] = a_ref[...].T

        sum_ref[step] = nn(turned[...], b_ref[...]).astype(jnp.bfloat16)
    else:
        sum_ref[step] = tn(a_ref[...], b_ref[...]).astype(jnp.bfloat16)

    def copies(at):
        for i, (when, out, row, rows, terms, col_from, cols) in enumerate(moves):
            if at is not None and when != at:
                continue
            start = terms[0]
            for entry, scale in terms[1:]:
                start = start + table[entry] * scale
            if len(terms) > 1:
                start = pl.multiple_of(start, 8)
            if isinstance(col_from, tuple):
                chooser, half = col_from
                column = pl.multiple_of(table[chooser] * half, 128)
            else:
                column = col_from
            yield pltpu.make_async_copy(
                sum_ref.at[when, pl.ds(start, rows), pl.ds(column, cols)],
                out_refs[out].at[pl.ds(row, rows), :],
                sems.at[i],
            )

    for at in range(steps):

        @pl.when(step == at)
        def _(at=at):
            for copy in copies(at):
                copy.start()

    @pl.when(step == steps - 1)
    def _():
        for copy in copies(None):
            copy.wait()


def weight_grad(a, b, table, plan, shapes, carried, name):
    tile, by_columns, a_map, b_map, moves = plan
    rows, left = a.shape
    right = b.shape[1]
    if by_columns:
        steps = right // tile
        specs = [
            pl.BlockSpec((rows, left), a_map, pipeline_mode=pl.Buffered(1)),
            pl.BlockSpec((rows, tile), b_map),
        ]
        scratch = [pltpu.VMEM((steps, left, tile), jnp.bfloat16)]
        extra = [pltpu.VMEM((left, rows), jnp.bfloat16)]
    else:
        steps = left // tile
        specs = [
            pl.BlockSpec((rows, tile), a_map),
            pl.BlockSpec((rows, right), b_map, pipeline_mode=pl.Buffered(1)),
        ]
        scratch = [pltpu.VMEM((steps, tile, right), jnp.bfloat16)]
        extra = []
    anywhere = pl.BlockSpec(memory_space=pl.ANY)
    return pl.pallas_call(
        functools.partial(
            weight_grad_kernel, steps, by_columns, moves, len(shapes), len(carried)
        ),
        grid_spec=pltpu.PrefetchScalarGridSpec(
            num_scalar_prefetch=1,
            grid=(steps,),
            in_specs=specs + [anywhere] * len(carried),
            out_specs=[anywhere] * len(shapes),
            scratch_shapes=[*scratch, pltpu.SemaphoreType.DMA((len(moves),)), *extra],
        ),
        out_shape=[jax.ShapeDtypeStruct(s, jnp.bfloat16) for s in shapes],
        input_output_aliases={3 + i: i for i in range(len(carried))},
        compiler_params=pltpu.CompilerParams(vmem_limit_bytes=VMEM_BYTES),
        cost_estimate=cost(2 * rows * left * right, 2 * left * right + 2 * rows * (left + right)),
        name=name,
    )(table, a, b, *carried)


def bits_of(size):
    return size.bit_length() - 1


def label_of(index):
    upper = index >> 1
    return ((upper ^ (upper >> 1)) << 1) | (index & 1)


def index_of(label):
    upper = label >> 1
    shift = 1
    while shift < 32:
        upper = upper ^ (upper >> shift)
        shift *= 2
    return (upper << 1) | (label & 1)


def swap_dp(value, bit):
    size = lax.axis_size("dp")
    return lax.ppermute(
        value, "dp", [(i, index_of(label_of(i) ^ (1 << bit))) for i in range(size)]
    )


def swap_expert(value, bit):
    size = lax.axis_size("expert")
    step = size - 1 if bit is None else 1 << bit
    return lax.ppermute(value, "expert", [(i, i ^ step) for i in range(size)])


def gather_expert(value):
    bits = bits_of(lax.axis_size("expert"))
    parts = {0: value}
    for bit in reversed(range(bits)):
        for r in list(parts):
            parts[r | (1 << bit)] = swap_expert(parts[r], bit)
    return [parts[r] for r in range(1 << bits)]


def gather_ordered(value):
    mine = lax.axis_index("expert")
    for bit in range(bits_of(lax.axis_size("expert"))):
        other = swap_expert(value, bit)
        upper = (mine >> bit & 1) == 1
        value = jnp.concatenate(
            [jnp.where(upper, other, value), jnp.where(upper, value, other)], axis=0
        )
    return value


def gather_expert_stacked(value):
    held, places = value[None], [0]
    for bit in reversed(range(bits_of(lax.axis_size("expert")))):
        held = jnp.concatenate([held, swap_expert(held, bit)])
        places += [place | (1 << bit) for place in places]
    return jnp.concatenate([held[places.index(r)][None] for r in range(len(places))])


def scatter_expert(parts, first_bit=0):
    parts = [[part] for part in parts]
    for bit in range(first_bit, bits_of(lax.axis_size("expert"))):
        left = []
        for kept, away in zip(parts[::2], parts[1::2]):
            away = away[0].astype(jnp.bfloat16) if len(away) == 1 else added(away).astype(jnp.bfloat16)
            kept = kept if len(kept) == 1 else [added(kept).astype(jnp.bfloat16)]
            left.append([*kept, swap_expert(away, bit)])
        parts = left
    return parts[0]


def gather_dp_step(value, bit):
    return jnp.concatenate([value, swap_dp(value, bit)], axis=0)


def gather_dp(value):
    for bit in range(bits_of(lax.axis_size("dp"))):
        value = gather_dp_step(value, bit)
    return value


LINE, PAIR = 4, 2
CORE, CHIP, AHEAD = 8, 10, 12


def tuned(mesh_dp, experts):
    return mesh_dp == LINE * PAIR and experts == 4


def shard_table():
    dp, expert = lax.axis_index("dp"), lax.axis_index("expert")
    relative = jnp.arange(LINE * PAIR, dtype=jnp.int32)
    place, along, across = dp // PAIR, relative // PAIR, dp % PAIR ^ relative % PAIR
    inwards = jnp.where(place < LINE // 2, place + along, place - along + LINE) % LINE
    ahead = (place + along) % LINE
    core, chip = expert & 1, expert >> 1
    return jnp.concatenate(
        [inwards * PAIR + across, jnp.stack([core, 1 - core, chip, 1 - chip]), ahead * PAIR + across]
    ).astype(jnp.int32)


def relatives():
    return [(2 * along + across, along, across) for along in range(LINE) for across in range(PAIR)]


def by_shard(shard, first, moves):
    return (shard, False, lambda j, t: (0, t[first + j]), lambda j, t: (0, 0), moves)


def halves_map(half_steps):
    return lambda j, t: (
        0,
        jnp.where(j < half_steps, t[CORE + 1] * half_steps + j, (t[CORE] - 1) * half_steps + j),
    )


def expert_down_plan(width, hidden):
    shard = hidden // 8
    moves = [
        (relative, along, across * shard, shard, (0,), 0, width)
        for relative, along, across in relatives()
    ]
    return by_shard(shard, 0, moves), [(PAIR * shard, width)] * LINE


def expert_up_plan(width, hidden):
    shard = width // 8
    steps = hidden // width
    moves = [
        (step, across, (along * steps + step) * shard, shard, (0, (relative, shard)), 0, width)
        for step in range(steps)
        for relative, along, across in relatives()
    ]
    plan = (width, True, lambda j, t: (0, 0), lambda j, t: (0, j), moves)
    return plan, [(LINE * steps * shard, width)] * PAIR


def dense_place(chip_first, chip, along, across):
    outer, inner = (chip, across) if chip_first else (across, chip)
    return (2 * outer + inner) * LINE + along


def dense_up_plan(width, hidden):
    cols, shard = width // 2, width // 8
    rows = shard // 2
    unit = rows * (hidden // width)
    half_steps = hidden // width // 2
    moves = []
    for step in range(2 * half_steps):
        for block in range(2):
            column = 2 * (step % half_steps) + block
            for relative, along, across in relatives():
                for chip in range(2):
                    row = dense_place(True, chip, along, across) * unit + column * rows
                    source = (0, (AHEAD + relative, shard), (CHIP + chip, rows))
                    moves.append((step, step // half_steps, row, rows, source, block * cols, cols))
    return (width, True, lambda j, t: (0, 0), halves_map(half_steps), moves)


def dense_down_plan(width, hidden):
    cols = width // 2
    unit = hidden // 8 // 2
    moves = []
    for relative, along, across in relatives():
        for out in range(2):
            for chip in range(2):
                row = (16 + dense_place(False, chip, along, across)) * unit
                source = (0, (CHIP + chip, unit))
                moves.append((relative, out, row, unit, source, (CORE + 1 - out, cols), cols))
    return by_shard(hidden // 8, AHEAD, moves)


def tail_plan(width, first, count):
    cols, shard = width // 2, width // 8
    rows = shard // 2
    moves = []
    for step in range(2):
        for block in range(count):
            for relative, along, across in relatives():
                for chip in range(2):
                    row = (dense_place(True, chip, along, across) * 4 + first + block) * rows
                    source = (0, (AHEAD + relative, shard), (CHIP + chip, rows))
                    moves.append((step, step, row, rows, source, block * cols, cols))
    return (count * cols, True, lambda j, t: (0, 0), halves_map(1), moves)


def low(parts):
    return added(parts).astype(jnp.bfloat16)


def sum_blocks(addends, blocks, count):
    rows, cols = addends[0].shape[0] // count, addends[0].shape[1]
    return sum_spans(
        [addends], [[(0, block * rows)] for block in blocks], rows, cols, "sum_blocks"
    )


def sum_line(first, second):
    rows, cols = first[0].shape[0] // LINE, first[0].shape[1]
    spans = [[(0, ahead * rows), (1, ahead * rows)] for ahead in range(1, LINE)]
    return sum_spans([first, second], spans, rows, cols, "sum_line")


def sum_spans(groups, spans, rows, cols, name):
    sizes = [len(group) for group in groups]

    def kernel(*refs):
        outs = refs[sum(sizes) :]
        for out, parts in zip(outs, spans):
            for at, (group, start) in enumerate(parts):
                first = sum(sizes[:group])
                for piece in range(rows // 48):
                    here = pl.ds(start + piece * 48, 48)
                    total = refs[first][here, :].astype(jnp.float32)
                    for ref in refs[first + 1 : first + sizes[group]]:
                        total = total + ref[here, :].astype(jnp.float32)
                    out[pl.ds(at * rows + piece * 48, 48), :] = total.astype(jnp.bfloat16)

    arrays = [array for group in groups for array in group]
    vmem = pl.BlockSpec(memory_space=pltpu.VMEM)
    return pl.pallas_call(
        kernel,
        in_specs=[vmem] * len(arrays),
        out_specs=[vmem] * len(spans),
        out_shape=[jax.ShapeDtypeStruct((len(p) * rows, cols), jnp.bfloat16) for p in spans],
        compiler_params=pltpu.CompilerParams(vmem_limit_bytes=VMEM_BYTES),
        name=name,
    )(*arrays)


def sync(*values):
    return lax.optimization_barrier(values)


def cut(arrays, count):
    left = arrays[0].shape[0] // count
    return [[a[i * left : (i + 1) * left] for a in arrays] for i in range(count)]


def swap_pair(value):
    return lax.ppermute(value, "dp", [(i, i ^ 1) for i in range(LINE * PAIR)])


def move_line(value, pairs):
    return lax.ppermute(
        value, "dp", [(a * PAIR + i, b * PAIR + i) for a, b in pairs for i in range(PAIR)]
    )


OUTSIDE = [(0, 1), (1, 0), (2, 3), (3, 2)]


def at_end():
    place = lax.axis_index("dp") // PAIR
    return (place == 0) | (place == LINE - 1)


def line_first(outer):
    return move_line(outer, OUTSIDE)


def move_inside(value):
    experts = lax.axis_size("expert")
    pairs = []
    for place in range(LINE):
        for rest in range(PAIR * experts):
            here = place * PAIR * experts + rest
            there = here ^ 1 if place in (0, LINE - 1) else (LINE - 1 - place) * PAIR * experts + rest
            pairs.append((here, there))
    return lax.ppermute(value, ("dp", "expert"), pairs)


def line_second(middle, came):
    return move_line(low(middle), OUTSIDE), move_inside(low([*middle, came]))


def third_parts(inner, outside, inside):
    return jnp.where(at_end(), low(inner), inside), low([*inner, outside])


def line_third(outside, inside):
    return move_line(outside, OUTSIDE), move_inside(inside)


def line_last(own, first, outside, inside):
    return [*own, outside, jnp.where(at_end(), first, inside)]


def line_direct(aways):
    return [
        move_line(away, [(i, (i + ahead) % LINE) for i in range(LINE)])
        for ahead, away in enumerate(aways, 1)
    ]


def swap_both(value, dp_step, expert_step):
    experts = lax.axis_size("expert")
    pairs = [
        (dp * experts + expert, (dp ^ dp_step) * experts + (expert ^ expert_step))
        for dp in range(LINE * PAIR)
        for expert in range(experts)
    ]
    return lax.ppermute(value, ("dp", "expert"), pairs)


def swap_plane(aways):
    return [swap_pair(aways[0]), swap_expert(aways[1], 1), swap_both(aways[2], 1, 2)]


def share_quarters(total):
    return [swap_expert(total, 0), swap_expert(total, 1), swap_expert(total, None)]


def order_quarters(total, cames):
    core, chip, both = cames
    expert = lax.axis_index("expert")
    right, upper = (expert & 1) == 1, (expert >> 1) == 1
    mine = jnp.where(upper, chip, total), jnp.where(upper, total, chip)
    other = jnp.where(upper, both, core), jnp.where(upper, core, both)
    return [
        [jnp.where(right, o, s) for o, s in zip(other, mine)],
        [jnp.where(right, s, o) for o, s in zip(other, mine)],
    ]


def swap_stack(held, bit):
    return jnp.concatenate([held, swap_expert(held, bit)])


def stack_order(held):
    places = [0]
    for bit in reversed(range(bits_of(held.shape[0]))):
        places += [place | (1 << bit) for place in places]
    return jnp.concatenate([held[places.index(r)][None] for r in range(len(places))])


def gather_chips(value):
    parts = {0: value}
    for bit in reversed(range(1, bits_of(lax.axis_size("expert")))):
        for r in list(parts):
            parts[r | (1 << bit)] = swap_expert(parts[r], bit)
    return parts


def rows_to_columns(stacked, count):
    rows = stacked.shape[0] // count
    return jnp.concatenate([stacked[i * rows : (i + 1) * rows] for i in range(count)], axis=1)


def added(parts):
    total = parts[0].astype(jnp.float32)
    for part in parts[1:]:
        total = total + part.astype(jnp.float32)
    return total


def scatter_far(parts):
    came = []
    for bit in range(1, bits_of(lax.axis_size("expert"))):
        left = []
        for kept, away in zip(parts[::2], parts[1::2]):
            moved = swap_expert(away, bit)
            if kept is None:
                came.append(moved)
                left.append(None)
            else:
                left.append(added([kept, moved]).astype(jnp.bfloat16))
        parts = left
    return came


def on_device(
    patches,
    time_embed,
    ada_weight,
    ada_bias,
    qkv_weight,
    out_weight,
    up_weight,
    down_weight,
    expert_up,
    expert_down,
    routes,
    gate_weights,
    cotangent,
):
    tokens, width = patches.shape
    latents = time_embed.shape[0]
    seq_len = tokens // latents
    experts = lax.axis_size("expert")
    dp_size = lax.axis_size("dp")
    dp_index = lax.axis_index("dp")
    expert_index = lax.axis_index("expert")
    capacity = 5 * tokens // (2 * experts)

    hidden = up_weight.shape[1]
    blocks = 2
    groups = experts // blocks
    table = shard_table()

    info = jnp.concatenate(
        [
            routes.T.astype(jnp.float32),
            gate_weights.T,
            time_embed.astype(jnp.float32).reshape(-1, tokens),
        ],
        axis=0,
    )
    info = swap_stack(info[None], bits_of(experts) - 1)
    info, cotangent = sync(info, cotangent)
    cots = gather_chips(cotangent)
    cots[1] = swap_expert(cotangent, 0)
    for bit in reversed(range(bits_of(experts) - 1)):
        info = swap_stack(info, bit)
    info_all = stack_order(info)
    cond = jax.nn.silu(time_embed.astype(jnp.float32)).astype(jnp.bfloat16)
    modulation = jnp.dot(cond, ada_weight, preferred_element_type=jnp.float32) + ada_bias
    mod = modulation.reshape(latents, 6, width)
    first_in, qkv_all, log_total, attended, attn_proj, second_in = attn_forward(
        patches, mod, qkv_weight, out_weight
    )
    second_in, info_all, cots = sync(second_in, info_all, cots)

    seconds = gather_chips(second_in)
    seconds[1] = swap_expert(second_in, 0)
    routed = route(
        expert_index[None], info_all[:, :4], info_all[:, 4:].reshape(experts * latents, width),
        ada_weight, ada_bias, tokens,
    )
    routed, seconds[1] = sync(routed, seconds[1])
    for r in range(2, experts, 2):
        cots[r + 1] = swap_expert(cots[r], 0)

    def run_group(group, carried):
        span = range(group * blocks, (group + 1) * blocks)
        results = expert_forward_backward(
            [seconds[r] for r in span], [cots[r] for r in span], *routed, expert_up[0], expert_down[0],
            capacity, groups, group, carried,
        )
        return results[: 4 + blocks], results[4 + blocks :]

    carried, near = run_group(0, [])
    carried, near, seconds, cots = sync(carried, near, seconds, cots)
    for r in range(2, experts, 2):
        seconds[r + 1] = swap_expert(seconds[r], 0)
    near_came = swap_expert(near[1], 0)
    backs = {}
    for group in range(1, groups):
        carried, backs[group] = run_group(group, carried)
    carried, backs, near_came = sync(carried, backs, near_came)
    act_rows, grad_pre_rows, rows_in, grad_rows, mix_even, mix_odd = carried

    fast = tuned(dp_size, experts)
    backs_came = {group: swap_expert(backs[group][1], 0) for group in backs}
    ups, downs, first_downs = (), (), ()
    if fast:
        plan, shapes = expert_down_plan(width, hidden)
        downs = weight_grad(act_rows, grad_rows, table, plan, shapes, [], "grad_expert_down")
    downs, backs_came, rows_in = sync(downs, backs_came, rows_in)
    far = [None] + [low([backs[group][0], backs_came[group]]) for group in range(1, groups)]
    far_sum = scatter_far(far)
    if fast:
        first_downs = line_first(downs[3])
        plan, shapes = expert_up_plan(width, hidden)
        ups = weight_grad(rows_in, grad_pre_rows, table, plan, shapes, [], "grad_expert_up")
    ups, second_in = sync(ups, second_in)

    mix_came = swap_expert(mix_odd, 0)
    if fast:
        up_came = swap_pair(ups[1])
    shared = shared_forward_backward(second_in, cotangent, mod[:, 5], up_weight, down_weight)
    shared, far_sum, mix_came, first_downs = sync(shared, far_sum, mix_came, first_downs)
    shared_act, grad_shared_pre, grad_shared, shared_out, grad_second = shared
    mix = added([mix_even, mix_came])
    mix = scatter_expert([mix[i * tokens : (i + 1) * tokens] for i in range(groups)], 1)
    if fast:
        second_downs = line_second([downs[2]], first_downs)
        dense_shapes = [(2 * hidden, width // 2)] * 2
        dense = weight_grad(
            second_in, grad_shared_pre, table, dense_up_plan(width, hidden), dense_shapes, [], "grad_up"
        )
        dense = weight_grad(
            shared_act, grad_shared, table, dense_down_plan(width, hidden), dense_shapes, dense,
            "grad_down",
        )
        dense, attn_proj, mix, second_downs, up_came = sync(
            dense, attn_proj, mix, second_downs, up_came
        )
        dense_came = swap_expert(dense[0], 0)
        third = third_parts([downs[1]], *second_downs)
        ups = cut([ups[0], up_came], LINE)
        up_outer = low(ups[3])
        third, up_outer, dense_came, attn_proj = sync(third, up_outer, dense_came, attn_proj)
        third_downs = line_third(*third)
        up_first = line_first(up_outer)
        first, second = cut([dense[1], dense_came], 2)
        first, second = cut(first, 2), cut(second, 2)
        aways = low(first[1]), low(second[1])
        aways, attn_proj = sync(aways, attn_proj)
        first_came = swap_expert(aways[0], 1)
        second_came = swap_pair(aways[1])

    backward = attn_backward(
        patches, mod, attn_proj, qkv_all, log_total, cotangent, out_weight,
        [grad_second, near[0], near_came, *far_sum],
    )
    grad_qkv_rows, grad_attn, grad_middle, grad_mod_early = backward
    if fast:
        tail_shapes = [(4 * width, width // 2)] * 2
        tail = weight_grad(
            first_in, grad_qkv_rows, table, tail_plan(width, 0, 3), tail_shapes, [], "grad_qkv"
        )
        tail = weight_grad(
            attended, grad_attn, table, tail_plan(width, 3, 1), tail_shapes, tail, "grad_out"
        )
        tail, third_downs, first_came, second_came, grad_middle = sync(
            tail, third_downs, first_came, second_came, grad_middle
        )
        tail_came = swap_expert(tail[0], 0)
        second = cut([*second[0], second_came], 2)
        first = cut([*first[0], first_came], 2)
        aways = low(first[1]), low(second[1])
        aways, grad_middle = sync(aways, grad_middle)
        first_came = swap_pair(aways[0])
        second_came = swap_expert(aways[1], 1)
    inner = input_backward(patches, mod, grad_qkv_rows, grad_middle, qkv_weight)
    if fast:
        inner, tail_came, up_first = sync(inner, tail_came, up_first)
        third = cut([tail[1], tail_came], 4)
        away = sum_blocks([tail[1], tail_came], [1, 2, 3], 4)
        away, inner, mix, first_came, second_came, third_downs, up_first = sync(
            away, inner, mix, first_came, second_came, third_downs, up_first
        )
        third_cames = swap_plane(away)
        up_cames = line_second(ups[2], up_first)
        dense_halves = [*first[0], first_came], [*second[0], second_came]
        first = cut(dense_halves[0], LINE)
        second = cut(dense_halves[1], LINE)
        aways = sum_line(dense_halves[0], dense_halves[1])
        own, away = cut(line_last([downs[0]], first_downs, *third_downs), 2)
        away = low(away)
        aways, away, mix = sync(aways, away, mix)
    grad_input, grad_mod_late = inner

    middle = patches.astype(jnp.float32).reshape(latents, seq_len, width) + mod[
        :, 2:3
    ] * attn_proj.reshape(latents, seq_len, width)
    branch = (shared_out + added(mix)).reshape(latents, seq_len, width)
    block_out = (middle + mod[:, 5:6] * branch).reshape(tokens, width).astype(jnp.bfloat16)
    grad_gate_two = jnp.sum(
        cotangent.astype(jnp.float32).reshape(latents, seq_len, width) * branch, axis=1
    )
    local_counts = jnp.sum(
        (routes[:, :, None] == jnp.arange(experts, dtype=jnp.int32)).astype(jnp.int32),
        axis=(0, 1),
    )
    count_parts = jnp.concatenate([local_counts // 128, local_counts % 128]).astype(jnp.bfloat16)
    count_rows = jnp.zeros((latents, 128), jnp.bfloat16).at[0, : 2 * experts].set(count_parts)
    mods = jnp.concatenate(
        [
            grad_mod_late.reshape(latents, 2 * width).astype(jnp.bfloat16),
            grad_mod_early.reshape(latents, 3 * width).astype(jnp.bfloat16),
            grad_gate_two.astype(jnp.bfloat16),
            cond,
            count_rows,
        ],
        axis=1,
    )

    if fast:
        line_cames = line_direct(aways)
        third_cames, mods, block_out = sync(third_cames, mods, block_out)
        third = cut([*third[0], *third_cames], LINE)
        tail_aways = [low(part) for part in third[1:]]
        tail_aways, line_cames, mods = sync(tail_aways, line_cames, mods)
        third_cames = line_direct(tail_aways)
        mods_all = gather_ordered(mods)
        up_third = third_parts(ups[1], *up_cames)
        third_cames, up_third, away, mods_all = sync(third_cames, up_third, away, mods_all)
        up_cames = line_third(*up_third)
        down_came = swap_pair(away)
        dense_total = low([jnp.concatenate([added(first[0]), added(second[0])]), *line_cames])
        tail_total = low([*third[0], *third_cames])
        totals = jnp.concatenate([dense_total, tail_total], axis=0)
        totals, mods_all = sync(totals, mods_all)
        cames = share_quarters(totals)
        for bit in range(bits_of(dp_size)):
            mods_all = gather_dp_step(mods_all, bit)
        quarters = order_quarters(totals, cames)
        sum_e_up = rows_to_columns(added(line_last(ups[0], up_first, *up_cames)), hidden // width)
        sum_e_down = added([*own, down_came])
        rows = dense_total.shape[0]
        dense_sums = [jnp.concatenate([q[:rows] for q in chips]) for chips in quarters]
        tail_sums = [jnp.concatenate([q[rows:] for q in chips]) for chips in quarters]

        def columns(arrays):
            return jnp.concatenate(arrays, axis=1).astype(jnp.float32)

        half = hidden // 16
        sum_w_up, sum_w_down = [], []
        for chip in range(2):
            at = 2 * half * chip
            sum_w_up.append(
                columns([rows_to_columns(s[at : at + half], hidden // width) for s in dense_sums])
            )
            sum_w_down.append(columns([s[at + half : at + 2 * half] for s in dense_sums]))
        sum_w_up, sum_w_down = jnp.concatenate(sum_w_up), jnp.concatenate(sum_w_down)
        half = width // 16
        sum_w_qkv, sum_w_out = [], []
        for chip in range(2):
            at = 4 * half * chip
            sum_w_qkv.append(
                columns([rows_to_columns(s[at : at + 3 * half], 3) for s in tail_sums])
            )
            sum_w_out.append(columns([s[at + 3 * half : at + 4 * half] for s in tail_sums]))
        sum_w_qkv, sum_w_out = jnp.concatenate(sum_w_qkv), jnp.concatenate(sum_w_out)
    else:
        mods_all = gather_dp(gather_ordered(mods))

        def summed(left, right, axes):
            share = lax.psum_scatter(
                tn(left, right).astype(jnp.bfloat16), "dp", scatter_dimension=0, tiled=True
            )
            return (lax.psum(share, axes) if axes else share).astype(jnp.float32)

        sum_w_up = summed(second_in, grad_shared_pre, "expert")
        sum_w_down = summed(shared_act, grad_shared, "expert")
        sum_w_qkv = summed(first_in, grad_qkv_rows, "expert")
        sum_w_out = summed(attended, grad_attn, "expert")
        sum_e_up = summed(rows_in, grad_pre_rows, None)
        sum_e_down = summed(act_rows, grad_rows, None)

    grad_mod_all = mods_all[:, : 6 * width]
    count_sums = jnp.sum(mods_all[:, 7 * width :].astype(jnp.float32), axis=0).astype(jnp.int32)
    counts = count_sums[:experts] * 128 + count_sums[experts : 2 * experts]
    ada_rows = width // dp_size
    cond_mine = lax.dynamic_slice_in_dim(
        mods_all[:, 6 * width : 7 * width].T, dp_index * ada_rows, ada_rows, axis=0
    )
    sum_ada = jnp.dot(cond_mine, grad_mod_all, preferred_element_type=jnp.float32)
    bias_all = jnp.sum(grad_mod_all.astype(jnp.float32), axis=0)
    bias_size = bias_all.shape[0] // dp_size
    sum_bias = lax.dynamic_slice_in_dim(bias_all, dp_index * bias_size, bias_size)
    return (
        block_out,
        grad_input,
        sum_ada,
        sum_bias,
        sum_w_qkv,
        sum_w_out,
        sum_w_up,
        sum_w_down,
        sum_e_up[None],
        sum_e_down[None],
        counts,
    )


def solution(mesh):
    in_specs = (
        P(("dp", "expert"), None),
        P(("dp", "expert"), None),
        P(),
        P(),
        P(),
        P(),
        P(),
        P(),
        P("expert", None, None),
        P("expert", None, None),
        P(("dp", "expert"), None),
        P(("dp", "expert"), None),
        P(("dp", "expert"), None),
    )
    out_specs = (
        P(("dp", "expert"), None),
        P(("dp", "expert"), None),
        P("dp", None),
        P("dp"),
        P("dp", None),
        P("dp", None),
        P("dp", None),
        P("dp", None),
        P("expert", "dp", None),
        P("expert", "dp", None),
        P(),
    )
    return jax.shard_map(
        on_device, mesh=mesh, in_specs=in_specs, out_specs=out_specs, check_vma=False
    )
```

```python
import functools
import math

import jax
import jax.numpy as jnp
import numpy as np
from jax import lax
from jax.experimental import pallas as pl
from jax.experimental.pallas import tpu as pltpu
from jax.sharding import PartitionSpec as P

HEAD_DIM = 64
VMEM_BYTES = 56 << 20
SHRINK = 1
SQRT_TWO_OVER_PI = math.sqrt(2.0 / math.pi)


def nt(a,b): return lax.dot_general(a,b,(((1,),(1,)),((),())),preferred_element_type=jnp.float32)
def nn(a,b): return lax.dot_general(a,b,(((1,),(0,)),((),())),preferred_element_type=jnp.float32)
def tn(a,b): return lax.dot_general(a,b,(((0,),(0,)),((),())),preferred_element_type=jnp.float32)

def normalized(values_in):
    row_mean = jnp.mean(values_in, axis=-1, keepdims=True)
    centered = values_in - row_mean
    row_var = jnp.mean(centered * centered, axis=-1, keepdims=True)
    inverse = lax.rsqrt(row_var + 1e-06)
    return centered * inverse, inverse

def norm_back(grad_out, scale, normal, inverse):
    inner = grad_out * (1.0 + scale)
    mean_inner = jnp.mean(inner, axis=-1, keepdims=True)
    mean_cross = jnp.mean(inner * normal, axis=-1, keepdims=True)
    return inverse * (inner - mean_inner - normal * mean_cross)

def head_lanes(pair, head):
    lane = lax.broadcasted_iota(jnp.int32, pair.shape, 1)
    return jnp.where(lane // HEAD_DIM == head, pair, jnp.zeros_like(pair))

def attn_forward_kernel(x_ref, mod_ref, wqkv_ref, wout_ref, first_ref, qkv_ref, lse_ref, att_ref, proj_ref, second_ref):
    width = x_ref.shape[1]
    x = x_ref[...].astype(jnp.float32)
    mod = mod_ref[0]
    normal, _ = normalized(x)
    first_ref[...] = (normal * (1.0 + mod[1:2]) + mod[0:1]).astype(jnp.bfloat16)
    qkv_ref[...] = nn(first_ref[...], wqkv_ref[...]).astype(jnp.bfloat16)
    lane = 2 * HEAD_DIM
    for pair in range(width // lane):
        q2 = qkv_ref[:, pair * lane : (pair + 1) * lane]
        k2 = qkv_ref[:, width + pair * lane : width + (pair + 1) * lane]
        v2 = qkv_ref[:, 2 * width + pair * lane : 2 * width + (pair + 1) * lane]
        v2t = v2.T
        outs = []
        for head in range(2):
            scores = nt(head_lanes(k2, head), q2) * HEAD_DIM ** (-0.5)
            peak = jnp.max(scores, axis=0, keepdims=True)
            powers = jnp.exp(scores - peak)
            total = jnp.sum(powers, axis=0, keepdims=True)
            lse_ref[0, 2 * pair + head : 2 * pair + head + 1, :] = peak + jnp.log(total)
            probs = (powers * (1.0 / total)).astype(jnp.bfloat16)
            outs.append(nn(v2t[head * HEAD_DIM : (head + 1) * HEAD_DIM], probs))
        both = jnp.concatenate(outs, axis=0).astype(jnp.bfloat16)
        att_ref[:, pair * lane : (pair + 1) * lane] = both.T
    proj = nn(att_ref[...], wout_ref[...])
    proj_ref[...] = proj
    middle = x + mod[2:3] * proj
    normal2, _ = normalized(middle)
    second_ref[...] = (normal2 * (1.0 + mod[4:5]) + mod[3:4]).astype(jnp.bfloat16)

def attn_forward(patches, mod, wqkv, wout):
    tokens, width = patches.shape
    latents = mod.shape[0]
    seq = tokens // latents
    heads = width // HEAD_DIM
    rows = lambda cols: pl.BlockSpec((seq, cols), lambda i: (i, 0))
    whole = lambda a: pl.BlockSpec(a.shape, lambda i: (0, 0), pipeline_mode=pl.Buffered(1))
    return pl.pallas_call(
        attn_forward_kernel, grid=(latents,),
        in_specs=[rows(width), pl.BlockSpec((1,) + mod.shape[1:], lambda i: (i, 0, 0)), whole(wqkv), whole(wout)],
        out_specs=[rows(width), rows(3 * width), pl.BlockSpec((1, heads, seq), lambda i: (i, 0, 0)), rows(width), rows(width), rows(width)],
        out_shape=[jax.ShapeDtypeStruct((tokens, width), jnp.bfloat16), jax.ShapeDtypeStruct((tokens, 3 * width), jnp.bfloat16),
            jax.ShapeDtypeStruct((latents, heads, seq), jnp.float32), jax.ShapeDtypeStruct((tokens, width), jnp.bfloat16),
            jax.ShapeDtypeStruct((tokens, width), jnp.float32), jax.ShapeDtypeStruct((tokens, width), jnp.bfloat16)],
        compiler_params=pltpu.CompilerParams(vmem_limit_bytes=VMEM_BYTES), cost_estimate=cost(8 * tokens * width * width, 8 * width * width), name="attn_forward")(patches, mod, wqkv, wout)

def attn_backward_kernel(extra, x_ref, mod_ref, proj_ref, qkv_ref, lse_ref, cot_ref, wout_ref, *rest):
    adds = rest[:extra]
    gqkv_ref, gattn_ref, gmid_ref, gmod_ref = rest[extra:]
    width = x_ref.shape[1]
    x = x_ref[...].astype(jnp.float32)
    mod = mod_ref[0]
    proj = proj_ref[...]
    normal, inverse = normalized(x + mod[2:3] * proj)
    grad_second = adds[0][...].astype(jnp.float32)
    for a in adds[1:]:
        grad_second = grad_second + a[...].astype(jnp.float32)
    gmod_ref[0, 1:2, :] = jnp.sum(grad_second, axis=0, keepdims=True)
    gmod_ref[0, 2:3, :] = jnp.sum(grad_second * normal, axis=0, keepdims=True)
    grad_middle = cot_ref[...].astype(jnp.float32) + norm_back(grad_second, mod[4:5], normal, inverse)
    gmid_ref[...] = grad_middle
    gmod_ref[0, 0:1, :] = jnp.sum(grad_middle * proj, axis=0, keepdims=True)
    gattn_ref[...] = (mod[2:3] * grad_middle).astype(jnp.bfloat16)
    grad_att = nt(gattn_ref[...], wout_ref[...]).astype(jnp.bfloat16)
    lane = 2 * HEAD_DIM
    scale = HEAD_DIM ** (-0.5)
    for pair in range(width // lane):
        sl = slice(pair * lane, (pair + 1) * lane)
        q2 = qkv_ref[:, pair * lane : (pair + 1) * lane]
        k2 = qkv_ref[:, width + pair * lane : width + (pair + 1) * lane]
        v2 = qkv_ref[:, 2 * width + pair * lane : 2 * width + (pair + 1) * lane]
        do2 = grad_att[:, sl]
        k2t = k2.T
        gq, gk, gv = [], [], []
        for head in range(2):
            scores = nt(head_lanes(k2, head), q2) * scale
            probs = jnp.exp(scores - lse_ref[0, 2 * pair + head : 2 * pair + head + 1, :])
            grad_probs = nt(head_lanes(v2, head), do2)
            inner = jnp.sum(probs * grad_probs, axis=0, keepdims=True)
            grad_scores = (probs * (grad_probs - inner)).astype(jnp.bfloat16)
            gv.append(nn(probs.astype(jnp.bfloat16), do2))
            gk.append(nn(grad_scores, q2))
            gq.append(nn(k2t[head * HEAD_DIM : (head + 1) * HEAD_DIM], grad_scores))
        low = lax.broadcasted_iota(jnp.int32, gv[0].shape, 1) < HEAD_DIM
        gqt = (jnp.concatenate(gq, axis=0) * scale).astype(jnp.bfloat16)
        gqkv_ref[:, pair * lane : (pair + 1) * lane] = gqt.T
        gqkv_ref[:, width + pair * lane : width + (pair + 1) * lane] = (jnp.where(low, gk[0], gk[1]) * scale).astype(jnp.bfloat16)
        gqkv_ref[:, 2 * width + pair * lane : 2 * width + (pair + 1) * lane] = jnp.where(low, gv[0], gv[1]).astype(jnp.bfloat16)

def attn_backward(patches, mod, proj, qkv, lse, cot, wout, adds):
    tokens, width = patches.shape
    latents = mod.shape[0]
    seq = tokens // latents
    rows = lambda cols: pl.BlockSpec((seq, cols), lambda i: (i, 0))
    per = lambda a: pl.BlockSpec((1,) + a.shape[1:], lambda i: (i, 0, 0))
    whole = lambda a: pl.BlockSpec(a.shape, lambda i: (0, 0), pipeline_mode=pl.Buffered(1))
    return pl.pallas_call(
        functools.partial(attn_backward_kernel, len(adds)), grid=(latents,),
        in_specs=[rows(width), per(mod), rows(width), rows(3 * width), per(lse), rows(width), whole(wout)] + [rows(width)] * len(adds),
        out_specs=[rows(3 * width), rows(width), rows(width), pl.BlockSpec((1, 3, width), lambda i: (i, 0, 0))],
        out_shape=[jax.ShapeDtypeStruct((tokens, 3 * width), jnp.bfloat16), jax.ShapeDtypeStruct((tokens, width), jnp.bfloat16),
            jax.ShapeDtypeStruct((tokens, width), jnp.float32), jax.ShapeDtypeStruct((latents, 3, width), jnp.float32)],
        compiler_params=pltpu.CompilerParams(vmem_limit_bytes=VMEM_BYTES), cost_estimate=cost(8 * tokens * width * width, 8 * width * width), name="attn_backward")(patches, mod, proj, qkv, lse, cot, wout, *adds)

def input_backward_kernel(x_ref, mod_ref, gqkv_ref, gmid_ref, wqkv_ref, gin_ref, gmod_ref):
    mod = mod_ref[0]
    normal, inverse = normalized(x_ref[...].astype(jnp.float32))
    grad_first = nt(gqkv_ref[...], wqkv_ref[...])
    gmod_ref[0, 0:1, :] = jnp.sum(grad_first, axis=0, keepdims=True)
    gmod_ref[0, 1:2, :] = jnp.sum(grad_first * normal, axis=0, keepdims=True)
    gin_ref[...] = gmid_ref[...] + norm_back(grad_first, mod[1:2], normal, inverse)

def input_backward(patches, mod, gqkv, gmid, wqkv):
    tokens, width = patches.shape
    latents = mod.shape[0]
    seq = tokens // latents
    rows = lambda cols: pl.BlockSpec((seq, cols), lambda i: (i, 0))
    per = lambda a: pl.BlockSpec((1,) + a.shape[1:], lambda i: (i, 0, 0))
    whole = lambda a: pl.BlockSpec(a.shape, lambda i: (0, 0), pipeline_mode=pl.Buffered(1))
    return pl.pallas_call(
        input_backward_kernel, grid=(latents,),
        in_specs=[rows(width), per(mod), rows(3 * width), rows(width), whole(wqkv)],
        out_specs=[rows(width), pl.BlockSpec((1, 2, width), lambda i: (i, 0, 0))],
        out_shape=[jax.ShapeDtypeStruct((tokens, width), jnp.float32), jax.ShapeDtypeStruct((latents, 2, width), jnp.float32)],
        compiler_params=pltpu.CompilerParams(vmem_limit_bytes=VMEM_BYTES), cost_estimate=cost(6 * tokens * width * width, 6 * width * width), name="input_backward")(patches, mod, gqkv, gmid, wqkv)


def cost(flops, size):
    return pl.CostEstimate(flops=int(flops) // SHRINK, bytes_accessed=int(size) // SHRINK, transcendentals=0)


def feed_forward_step(x_ref, g_ref, up_ref, down_ref, act_ref, gpre_ref, out_acc, grad_acc):
    inner_scale = SQRT_TWO_OVER_PI
    cubic = 0.044715
    pre = nn(x_ref[...], up_ref[...])
    grad_act = nt(g_ref[...], down_ref[...])
    squared = pre * pre
    bent = jnp.tanh(pre * (inner_scale + (inner_scale * cubic) * squared))
    half = 0.5 + 0.5 * bent
    act = (pre * half).astype(jnp.bfloat16)
    slope = half + (0.5 * pre) * (1.0 - bent * bent) * (
        inner_scale + (3.0 * cubic * inner_scale) * squared
    )
    grad_pre = (grad_act * slope).astype(jnp.bfloat16)
    act_ref[...] = act
    gpre_ref[...] = grad_pre
    out_acc[...] += nn(act, down_ref[...])
    grad_acc[...] += nt(grad_pre, up_ref[...])


def shared_kernel(
    x_ref, cot_ref, gate_ref, up_ref, down_ref,
    act_ref, gpre_ref, g_ref, out_ref, grad_ref,
    out_acc, grad_acc,
):
    step = pl.program_id(0)
    latents = gate_ref.shape[0]
    seq = x_ref.shape[0] // latents

    @pl.when(step == 0)
    def _():
        out_acc[...] = jnp.zeros_like(out_acc)
        grad_acc[...] = jnp.zeros_like(grad_acc)
        for i in range(latents):
            rows = slice(i * seq, (i + 1) * seq)
            g_ref[rows, :] = (gate_ref[i : i + 1, :] * cot_ref[rows, :].astype(jnp.float32)).astype(
                jnp.bfloat16
            )

    feed_forward_step(x_ref, g_ref, up_ref, down_ref, act_ref, gpre_ref, out_acc, grad_acc)

    @pl.when(step == pl.num_programs(0) - 1)
    def _():
        out_ref[...] = out_acc[...]
        grad_ref[...] = grad_acc[...]


def tile_of(width):
    return width // 4 if width % 512 == 0 else width


def still(array):
    return pl.BlockSpec(
        array.shape, lambda j, n=len(array.shape): (0,) * n, pipeline_mode=pl.Buffered(1)
    )


def shared_forward_backward(x, cot, gate, up, down):
    rows, width = x.shape
    hidden = up.shape[1]
    tile = tile_of(hidden)
    out = jax.ShapeDtypeStruct((rows, width), jnp.float32)
    wide = jax.ShapeDtypeStruct((rows, hidden), jnp.bfloat16)
    fixed = pl.BlockSpec((rows, width), lambda j: (0, 0))
    column = pl.BlockSpec((rows, tile), lambda j: (0, j))
    return pl.pallas_call(
        shared_kernel,
        grid=(hidden // tile,),
        in_specs=[
            still(x), still(cot), still(gate),
            pl.BlockSpec((width, tile), lambda j: (0, j)),
            pl.BlockSpec((tile, width), lambda j: (j, 0)),
        ],
        out_specs=[column, column, fixed, fixed, fixed],
        out_shape=[wide, wide, jax.ShapeDtypeStruct((rows, width), jnp.bfloat16), out, out],
        scratch_shapes=[pltpu.VMEM((rows, width), jnp.float32)] * 2,
        compiler_params=pltpu.CompilerParams(vmem_limit_bytes=VMEM_BYTES),
        cost_estimate=cost(8 * rows * width * hidden, 4 * width * hidden + 4 * rows * hidden),
        name="shared_ffn",
    )(x, cot, gate, up, down)


def expert_kernel(blocks, carried, *refs):
    xs, cots = refs[:blocks], refs[blocks : 2 * blocks]
    slot_row, slot_col, gate_col, gate_two, up_ref, down_ref = refs[2 * blocks : 2 * blocks + 6]
    rest = refs[2 * blocks + 6 + carried :]
    act_ref, gpre_ref, x_ref, g_ref = rest[:4]
    mixes, backs = rest[4 : 4 + blocks], rest[4 + blocks : 4 + 2 * blocks]
    out_acc, grad_acc = rest[4 + 2 * blocks :]
    step = pl.program_id(0)
    tokens = xs[0].shape[0]
    capacity = x_ref.shape[0] // blocks
    latents = gate_two.shape[1]
    seq = tokens // latents

    @pl.when(step == 0)
    def _():
        out_acc[...] = jnp.zeros_like(out_acc)
        grad_acc[...] = jnp.zeros_like(grad_acc)
        for b in range(blocks):
            rows = slice(b * capacity, (b + 1) * capacity)
            places = lax.broadcasted_iota(jnp.int32, (capacity, tokens), 0)
            pick = (places == slot_row[b]).astype(jnp.float32).astype(jnp.bfloat16)
            x_ref[rows, :] = nn(pick, xs[b][...]).astype(jnp.bfloat16)
            grads = []
            for i in range(latents):
                part = slice(i * seq, (i + 1) * seq)
                branch = gate_two[b, i : i + 1, :] * cots[b][part, :].astype(jnp.float32)
                grads.append((gate_col[b, part, :] * branch).astype(jnp.bfloat16))
            grad = jnp.concatenate(grads, axis=0)
            g_ref[rows, :] = nn(pick, grad).astype(jnp.bfloat16)

    feed_forward_step(x_ref, g_ref, up_ref, down_ref, act_ref, gpre_ref, out_acc, grad_acc)

    @pl.when(step == pl.num_programs(0) - 1)
    def _():
        for b in range(blocks):
            rows = slice(b * capacity, (b + 1) * capacity)
            places = lax.broadcasted_iota(jnp.int32, (tokens, capacity), 1)
            pick = (places == slot_col[b]).astype(jnp.float32).astype(jnp.bfloat16)
            backs[b][...] = nn(pick, grad_acc[rows, :].astype(jnp.bfloat16)).astype(jnp.bfloat16)
            mixed = nn(pick, out_acc[rows, :].astype(jnp.bfloat16))
            mixes[b][...] = (gate_col[b] * mixed).astype(jnp.bfloat16)


def expert_forward_backward(
    xs, cots, slot_row, slot_col, gate_col, gate_two, up, down, capacity, groups, group, carried
):
    blocks = len(xs)
    tokens, width = xs[0].shape
    hidden = up.shape[1]
    tile = tile_of(hidden)
    rows = blocks * capacity
    wide = jax.ShapeDtypeStruct((rows * groups, hidden), jnp.bfloat16)
    slim = jax.ShapeDtypeStruct((rows * groups, width), jnp.bfloat16)
    mixture = jax.ShapeDtypeStruct((tokens * groups, width), jnp.bfloat16)
    token = jax.ShapeDtypeStruct((tokens, width), jnp.bfloat16)
    column = pl.BlockSpec((rows, tile), lambda j: (group, j))
    own = pl.BlockSpec((rows, width), lambda j: (group, 0))
    mixed = pl.BlockSpec((tokens, width), lambda j: (group, 0))
    fixed = pl.BlockSpec((tokens, width), lambda j: (0, 0))
    small = [slot_row, slot_col, gate_col, gate_two]
    first = 2 * blocks + 6
    return pl.pallas_call(
        functools.partial(expert_kernel, blocks, len(carried)),
        grid=(hidden // tile,),
        in_specs=[still(a) for a in (*xs, *cots)]
        + [
            pl.BlockSpec(
                (blocks,) + a.shape[1:], lambda j, n=len(a.shape) - 1: (group,) + (0,) * n,
                pipeline_mode=pl.Buffered(1),
            )
            for a in small
        ]
        + [
            pl.BlockSpec((width, tile), lambda j: (0, j)),
            pl.BlockSpec((tile, width), lambda j: (j, 0)),
        ]
        + [pl.BlockSpec(memory_space=pl.ANY)] * len(carried),
        out_specs=[column, column, own, own] + [mixed] * blocks + [fixed] * blocks,
        scratch_shapes=[pltpu.VMEM((rows, width), jnp.float32)] * 2,
        out_shape=[wide, wide, slim, slim] + [mixture] * blocks + [token] * blocks,
        input_output_aliases={first + i: i for i in range(len(carried))},
        compiler_params=pltpu.CompilerParams(vmem_limit_bytes=VMEM_BYTES),
        cost_estimate=cost(8 * rows * width * hidden, 4 * width * hidden + 4 * rows * hidden),
        name="expert_ffn",
    )(*xs, *cots, *small, up, down, *carried)


def route_kernel(index_ref, info_ref, time_ref, ada_ref, bias_ref, row_ref, col_ref, gate_ref, two_ref):
    experts, _, tokens = row_ref.shape
    latents = time_ref.shape[0] // experts
    expert = index_ref[0]
    slots, gates = [], []
    before = (
        lax.broadcasted_iota(jnp.int32, (tokens, tokens), 0)
        < lax.broadcasted_iota(jnp.int32, (tokens, tokens), 1)
    ).astype(jnp.float32).astype(jnp.bfloat16)
    for r in range(experts):
        routes = info_ref[r, 0:2, :].astype(jnp.int32)
        named = routes == expert
        member = jnp.sum(named.astype(jnp.float32), axis=0, keepdims=True)
        earlier = nn(member.astype(jnp.bfloat16), before)
        slot = jnp.where(member > 0.5, earlier, float(tokens))
        row_ref[r] = slot.astype(jnp.int32)
        slots.append(slot)
        gates.append(
            jnp.sum(jnp.where(named, info_ref[r, 2:4, :], 0.0), axis=0, keepdims=True)
        )
    turned = jnp.concatenate(slots + gates, axis=0).T
    for r in range(experts):
        col_ref[r] = turned[:, r : r + 1].astype(jnp.int32)
        gate_ref[r] = turned[:, experts + r : experts + r + 1]
    times = time_ref[...]
    cond = (times / (1.0 + jnp.exp(-times))).astype(jnp.bfloat16)
    gate_two = nn(cond, ada_ref[...]) + bias_ref[...]
    for r in range(experts):
        two_ref[r] = gate_two[r * latents : (r + 1) * latents]


def route(expert, info, times, ada_weight, ada_bias, tokens):
    experts = info.shape[0]
    width = times.shape[1]
    latents = times.shape[0] // experts
    vmem = pl.BlockSpec(memory_space=pltpu.VMEM)
    return pl.pallas_call(
        route_kernel,
        grid=(1,),
        in_specs=[
            pl.BlockSpec(memory_space=pltpu.SMEM), still(info), still(times),
            pl.BlockSpec((width, width), lambda j: (0, 5)),
            pl.BlockSpec((1, width), lambda j: (0, 5)),
        ],
        out_specs=[vmem] * 4,
        out_shape=[
            jax.ShapeDtypeStruct((experts, 1, tokens), jnp.int32),
            jax.ShapeDtypeStruct((experts, tokens, 1), jnp.int32),
            jax.ShapeDtypeStruct((experts, tokens, 1), jnp.float32),
            jax.ShapeDtypeStruct((experts, latents, width), jnp.float32),
        ],
        compiler_params=pltpu.CompilerParams(vmem_limit_bytes=VMEM_BYTES),
        name="route",
    )(expert, info, times, ada_weight, ada_bias[None])


def weight_grad_kernel(steps, by_columns, moves, outs, carried, table, a_ref, b_ref, *rest):
    rest = rest[carried:]
    out_refs = rest[:outs]
    sum_ref, sems = rest[outs], rest[outs + 1]
    step = pl.program_id(0)
    if by_columns:
        turned = rest[outs + 2]

        @pl.when(step == 0)
        def _():
            turned[...] = a_ref[...].T

        sum_ref[step] = nn(turned[...], b_ref[...]).astype(jnp.bfloat16)
    else:
        sum_ref[step] = tn(a_ref[...], b_ref[...]).astype(jnp.bfloat16)

    def copies(at):
        for i, (when, out, row, rows, terms, col_from, cols) in enumerate(moves):
            if at is not None and when != at:
                continue
            start = terms[0]
            for entry, scale in terms[1:]:
                start = start + table[entry] * scale
            if len(terms) > 1:
                start = pl.multiple_of(start, 8)
            if isinstance(col_from, tuple):
                chooser, half = col_from
                column = pl.multiple_of(table[chooser] * half, 128)
            else:
                column = col_from
            yield pltpu.make_async_copy(
                sum_ref.at[when, pl.ds(start, rows), pl.ds(column, cols)],
                out_refs[out].at[pl.ds(row, rows), :],
                sems.at[i],
            )

    for at in range(steps):

        @pl.when(step == at)
        def _(at=at):
            for copy in copies(at):
                copy.start()

    @pl.when(step == steps - 1)
    def _():
        for copy in copies(None):
            copy.wait()


def weight_grad(a, b, table, plan, shapes, carried, name):
    tile, by_columns, a_map, b_map, moves = plan
    rows, left = a.shape
    right = b.shape[1]
    if by_columns:
        steps = right // tile
        specs = [
            pl.BlockSpec((rows, left), a_map, pipeline_mode=pl.Buffered(1)),
            pl.BlockSpec((rows, tile), b_map),
        ]
        scratch = [pltpu.VMEM((steps, left, tile), jnp.bfloat16)]
        extra = [pltpu.VMEM((left, rows), jnp.bfloat16)]
    else:
        steps = left // tile
        specs = [
            pl.BlockSpec((rows, tile), a_map),
            pl.BlockSpec((rows, right), b_map, pipeline_mode=pl.Buffered(1)),
        ]
        scratch = [pltpu.VMEM((steps, tile, right), jnp.bfloat16)]
        extra = []
    anywhere = pl.BlockSpec(memory_space=pl.ANY)
    return pl.pallas_call(
        functools.partial(
            weight_grad_kernel, steps, by_columns, moves, len(shapes), len(carried)
        ),
        grid_spec=pltpu.PrefetchScalarGridSpec(
            num_scalar_prefetch=1,
            grid=(steps,),
            in_specs=specs + [anywhere] * len(carried),
            out_specs=[anywhere] * len(shapes),
            scratch_shapes=[*scratch, pltpu.SemaphoreType.DMA((len(moves),)), *extra],
        ),
        out_shape=[jax.ShapeDtypeStruct(s, jnp.bfloat16) for s in shapes],
        input_output_aliases={3 + i: i for i in range(len(carried))},
        compiler_params=pltpu.CompilerParams(vmem_limit_bytes=VMEM_BYTES),
        cost_estimate=cost(2 * rows * left * right, 2 * left * right + 2 * rows * (left + right)),
        name=name,
    )(table, a, b, *carried)


def bits_of(size):
    return size.bit_length() - 1


def label_of(index):
    upper = index >> 1
    return ((upper ^ (upper >> 1)) << 1) | (index & 1)


def index_of(label):
    upper = label >> 1
    shift = 1
    while shift < 32:
        upper = upper ^ (upper >> shift)
        shift *= 2
    return (upper << 1) | (label & 1)


def swap_dp(value, bit):
    size = lax.axis_size("dp")
    return lax.ppermute(
        value, "dp", [(i, index_of(label_of(i) ^ (1 << bit))) for i in range(size)]
    )


def swap_expert(value, bit):
    size = lax.axis_size("expert")
    step = size - 1 if bit is None else 1 << bit
    return lax.ppermute(value, "expert", [(i, i ^ step) for i in range(size)])


def gather_expert(value):
    bits = bits_of(lax.axis_size("expert"))
    parts = {0: value}
    for bit in reversed(range(bits)):
        for r in list(parts):
            parts[r | (1 << bit)] = swap_expert(parts[r], bit)
    return [parts[r] for r in range(1 << bits)]


def gather_ordered(value):
    mine = lax.axis_index("expert")
    for bit in range(bits_of(lax.axis_size("expert"))):
        other = swap_expert(value, bit)
        upper = (mine >> bit & 1) == 1
        value = jnp.concatenate(
            [jnp.where(upper, other, value), jnp.where(upper, value, other)], axis=0
        )
    return value


def gather_expert_stacked(value):
    held, places = value[None], [0]
    for bit in reversed(range(bits_of(lax.axis_size("expert")))):
        held = jnp.concatenate([held, swap_expert(held, bit)])
        places += [place | (1 << bit) for place in places]
    return jnp.concatenate([held[places.index(r)][None] for r in range(len(places))])


def scatter_expert(parts, first_bit=0):
    parts = [[part] for part in parts]
    for bit in range(first_bit, bits_of(lax.axis_size("expert"))):
        left = []
        for kept, away in zip(parts[::2], parts[1::2]):
            away = away[0].astype(jnp.bfloat16) if len(away) == 1 else added(away).astype(jnp.bfloat16)
            kept = kept if len(kept) == 1 else [added(kept).astype(jnp.bfloat16)]
            left.append([*kept, swap_expert(away, bit)])
        parts = left
    return parts[0]


def gather_dp_step(value, bit):
    return jnp.concatenate([value, swap_dp(value, bit)], axis=0)


def gather_dp(value):
    for bit in range(bits_of(lax.axis_size("dp"))):
        value = gather_dp_step(value, bit)
    return value


LINE, PAIR = 4, 2
CORE, CHIP, AHEAD = 8, 10, 12


def tuned(mesh_dp, experts):
    return mesh_dp == LINE * PAIR and experts == 4


def shard_table():
    dp, expert = lax.axis_index("dp"), lax.axis_index("expert")
    relative = jnp.arange(LINE * PAIR, dtype=jnp.int32)
    place, along, across = dp // PAIR, relative // PAIR, dp % PAIR ^ relative % PAIR
    inwards = jnp.where(place < LINE // 2, place + along, place - along + LINE) % LINE
    ahead = (place + along) % LINE
    core, chip = expert & 1, expert >> 1
    return jnp.concatenate(
        [inwards * PAIR + across, jnp.stack([core, 1 - core, chip, 1 - chip]), ahead * PAIR + across]
    ).astype(jnp.int32)


def relatives():
    return [(2 * along + across, along, across) for along in range(LINE) for across in range(PAIR)]


def by_shard(shard, first, moves):
    return (shard, False, lambda j, t: (0, t[first + j]), lambda j, t: (0, 0), moves)


def halves_map(half_steps):
    return lambda j, t: (
        0,
        jnp.where(j < half_steps, t[CORE + 1] * half_steps + j, (t[CORE] - 1) * half_steps + j),
    )


def expert_down_plan(width, hidden):
    shard = hidden // 8
    moves = [
        (relative, along, across * shard, shard, (0,), 0, width)
        for relative, along, across in relatives()
    ]
    return by_shard(shard, 0, moves), [(PAIR * shard, width)] * LINE


def expert_up_plan(width, hidden):
    shard = width // 8
    steps = hidden // width
    moves = [
        (step, across, (along * steps + step) * shard, shard, (0, (relative, shard)), 0, width)
        for step in range(steps)
        for relative, along, across in relatives()
    ]
    plan = (width, True, lambda j, t: (0, 0), lambda j, t: (0, j), moves)
    return plan, [(LINE * steps * shard, width)] * PAIR


def dense_place(chip_first, chip, along, across):
    outer, inner = (chip, across) if chip_first else (across, chip)
    return (2 * outer + inner) * LINE + along


def dense_up_plan(width, hidden):
    cols, shard = width // 2, width // 8
    rows = shard // 2
    unit = rows * (hidden // width)
    half_steps = hidden // width // 2
    moves = []
    for step in range(2 * half_steps):
        for block in range(2):
            column = 2 * (step % half_steps) + block
            for relative, along, across in relatives():
                for chip in range(2):
                    row = dense_place(True, chip, along, across) * unit + column * rows
                    source = (0, (AHEAD + relative, shard), (CHIP + chip, rows))
                    moves.append((step, step // half_steps, row, rows, source, block * cols, cols))
    return (width, True, lambda j, t: (0, 0), halves_map(half_steps), moves)


def dense_down_plan(width, hidden):
    cols = width // 2
    unit = hidden // 8 // 2
    moves = []
    for relative, along, across in relatives():
        for out in range(2):
            for chip in range(2):
                row = (16 + dense_place(False, chip, along, across)) * unit
                source = (0, (CHIP + chip, unit))
                moves.append((relative, out, row, unit, source, (CORE + 1 - out, cols), cols))
    return by_shard(hidden // 8, AHEAD, moves)


def tail_plan(width, first, count):
    cols, shard = width // 2, width // 8
    rows = shard // 2
    moves = []
    for step in range(2):
        for block in range(count):
            for relative, along, across in relatives():
                for chip in range(2):
                    row = (dense_place(True, chip, along, across) * 4 + first + block) * rows
                    source = (0, (AHEAD + relative, shard), (CHIP + chip, rows))
                    moves.append((step, step, row, rows, source, block * cols, cols))
    return (count * cols, True, lambda j, t: (0, 0), halves_map(1), moves)


def low(parts):
    return added(parts).astype(jnp.bfloat16)


class View:
    def __init__(self, array, start, rows):
        self.array, self.start, self.rows = array, start, rows


def view(value):
    return value if isinstance(value, View) else View(value, 0, value.shape[0])


def sum_many(stacks):
    stacks = [[[view(value) for value in addends] for addends in stack] for stack in stacks]
    rows = stacks[0][0][0].rows
    block = 192 if rows % 192 == 0 and rows > 192 else 96
    steps = rows // block
    depth = len(stacks[0])
    arrays, specs, shapes = [], [], []
    for stack in stacks:
        width = stack[0][0].array.shape[1]
        shapes.append(jax.ShapeDtypeStruct((depth * rows, width), jnp.bfloat16))
        for level, addends in enumerate(stack):
            for value in addends:
                first = value.start // block
                arrays.append(value.array)
                specs.append(
                    pl.BlockSpec(
                        (block, width),
                        lambda i, f=first, l=level: (f + jnp.clip(i - l * steps, 0, steps - 1), 0),
                    )
                )

    def kernel(*refs):
        outs = refs[len(arrays) :]
        for level in range(depth):

            @pl.when(pl.program_id(0) // steps == level)
            def _(level=level):
                at = 0
                for out, stack in zip(outs, stacks):
                    for here, addends in enumerate(stack):
                        if here == level:
                            total = refs[at][...].astype(jnp.float32)
                            for extra in range(1, len(addends)):
                                total = total + refs[at + extra][...].astype(jnp.float32)
                            out[...] = total.astype(jnp.bfloat16)
                        at += len(addends)

    return pl.pallas_call(
        kernel,
        grid=(depth * steps,),
        in_specs=specs,
        out_specs=[pl.BlockSpec((block, s.shape[1]), lambda i: (i, 0)) for s in shapes],
        out_shape=shapes,
        compiler_params=pltpu.CompilerParams(vmem_limit_bytes=VMEM_BYTES),
        name="sum_many",
    )(*arrays)


def sync(*values):
    return lax.optimization_barrier(values)


def cut(addends, count):
    views = [view(value) for value in addends]
    left = views[0].rows // count
    return [[View(v.array, v.start + i * left, left) for v in views] for i in range(count)]


def swap_pair(value):
    return lax.ppermute(value, "dp", [(i, i ^ 1) for i in range(LINE * PAIR)])


def move_line(value, pairs):
    return lax.ppermute(
        value, "dp", [(a * PAIR + i, b * PAIR + i) for a, b in pairs for i in range(PAIR)]
    )


OUTSIDE = [(0, 1), (1, 0), (2, 3), (3, 2)]


def at_end():
    place = lax.axis_index("dp") // PAIR
    return (place == 0) | (place == LINE - 1)


def line_first(outer):
    return move_line(outer, OUTSIDE)


def move_inside(value):
    experts = lax.axis_size("expert")
    pairs = []
    for place in range(LINE):
        for rest in range(PAIR * experts):
            here = place * PAIR * experts + rest
            there = here ^ 1 if place in (0, LINE - 1) else (LINE - 1 - place) * PAIR * experts + rest
            pairs.append((here, there))
    return lax.ppermute(value, ("dp", "expert"), pairs)


def line_second(outside, inside):
    return move_line(outside, OUTSIDE), move_inside(inside)


def third_parts(inner, outside, inside):
    return jnp.where(at_end(), low(inner), inside), low([*inner, outside])


def line_third(outside, inside):
    return move_line(outside, OUTSIDE), move_inside(inside)


def line_last(own, first, outside, inside):
    return [*own, outside, jnp.where(at_end(), plain(first), inside)]


def line_direct(aways):
    return [
        move_line(away, [(i, (i + ahead) % LINE) for i in range(LINE)])
        for ahead, away in enumerate(aways, 1)
    ]


def swap_both(value, dp_step, expert_step):
    experts = lax.axis_size("expert")
    pairs = [
        (dp * experts + expert, (dp ^ dp_step) * experts + (expert ^ expert_step))
        for dp in range(LINE * PAIR)
        for expert in range(experts)
    ]
    return lax.ppermute(value, ("dp", "expert"), pairs)


def swap_plane(aways):
    return [swap_pair(aways[0]), swap_expert(aways[1], 1), swap_both(aways[2], 1, 2)]


def share_quarters(total):
    return [swap_expert(total, 0), swap_expert(total, 1), swap_expert(total, None)]


def order_quarters(total, cames):
    core, chip, both = cames
    expert = lax.axis_index("expert")
    right, upper = (expert & 1) == 1, (expert >> 1) == 1
    mine = jnp.where(upper, chip, total), jnp.where(upper, total, chip)
    other = jnp.where(upper, both, core), jnp.where(upper, core, both)
    return [
        [jnp.where(right, o, s) for o, s in zip(other, mine)],
        [jnp.where(right, s, o) for o, s in zip(other, mine)],
    ]


def swap_stack(held, bit):
    return jnp.concatenate([held, swap_expert(held, bit)])


def stack_order(held):
    places = [0]
    for bit in reversed(range(bits_of(held.shape[0]))):
        places += [place | (1 << bit) for place in places]
    return jnp.concatenate([held[places.index(r)][None] for r in range(len(places))])


def gather_chips(value):
    parts = {0: value}
    for bit in reversed(range(1, bits_of(lax.axis_size("expert")))):
        for r in list(parts):
            parts[r | (1 << bit)] = swap_expert(parts[r], bit)
    return parts


def rows_to_columns(stacked, count):
    rows = stacked.shape[0] // count
    return jnp.concatenate([stacked[i * rows : (i + 1) * rows] for i in range(count)], axis=1)


def plain(value):
    if isinstance(value, View):
        return value.array[value.start : value.start + value.rows]
    return value


def added(parts):
    total = plain(parts[0]).astype(jnp.float32)
    for part in parts[1:]:
        total = total + plain(part).astype(jnp.float32)
    return total


def scatter_far(parts):
    came = []
    for bit in range(1, bits_of(lax.axis_size("expert"))):
        left = []
        for kept, away in zip(parts[::2], parts[1::2]):
            moved = swap_expert(away, bit)
            if kept is None:
                came.append(moved)
                left.append(None)
            else:
                left.append(added([kept, moved]).astype(jnp.bfloat16))
        parts = left
    return came


def on_device(
    patches,
    time_embed,
    ada_weight,
    ada_bias,
    qkv_weight,
    out_weight,
    up_weight,
    down_weight,
    expert_up,
    expert_down,
    routes,
    gate_weights,
    cotangent,
):
    tokens, width = patches.shape
    latents = time_embed.shape[0]
    seq_len = tokens // latents
    experts = lax.axis_size("expert")
    dp_size = lax.axis_size("dp")
    dp_index = lax.axis_index("dp")
    expert_index = lax.axis_index("expert")
    capacity = 5 * tokens // (2 * experts)

    hidden = up_weight.shape[1]
    blocks = 2
    groups = experts // blocks
    table = shard_table()

    info = jnp.concatenate(
        [
            routes.T.astype(jnp.float32),
            gate_weights.T,
            time_embed.astype(jnp.float32).reshape(-1, tokens),
        ],
        axis=0,
    )
    info = swap_stack(info[None], bits_of(experts) - 1)
    info, cotangent = sync(info, cotangent)
    cots = gather_chips(cotangent)
    cots[1] = swap_expert(cotangent, 0)
    for bit in reversed(range(bits_of(experts) - 1)):
        info = swap_stack(info, bit)
    info_all = stack_order(info)
    cond = jax.nn.silu(time_embed.astype(jnp.float32)).astype(jnp.bfloat16)
    modulation = jnp.dot(cond, ada_weight, preferred_element_type=jnp.float32) + ada_bias
    mod = modulation.reshape(latents, 6, width)
    first_in, qkv_all, log_total, attended, attn_proj, second_in = attn_forward(
        patches, mod, qkv_weight, out_weight
    )
    second_in, info_all, cots = sync(second_in, info_all, cots)

    seconds = gather_chips(second_in)
    seconds[1] = swap_expert(second_in, 0)
    routed = route(
        expert_index[None], info_all[:, :4], info_all[:, 4:].reshape(experts * latents, width),
        ada_weight, ada_bias, tokens,
    )
    routed, seconds[1] = sync(routed, seconds[1])
    for r in range(2, experts, 2):
        cots[r + 1] = swap_expert(cots[r], 0)

    def run_group(group, carried):
        span = range(group * blocks, (group + 1) * blocks)
        results = expert_forward_backward(
            [seconds[r] for r in span], [cots[r] for r in span], *routed, expert_up[0], expert_down[0],
            capacity, groups, group, carried,
        )
        return results[: 4 + blocks], results[4 + blocks :]

    carried, near = run_group(0, [])
    carried, near, seconds, cots = sync(carried, near, seconds, cots)
    for r in range(2, experts, 2):
        seconds[r + 1] = swap_expert(seconds[r], 0)
    near_came = swap_expert(near[1], 0)
    backs = {}
    for group in range(1, groups):
        carried, backs[group] = run_group(group, carried)
    carried, backs, near_came = sync(carried, backs, near_came)
    act_rows, grad_pre_rows, rows_in, grad_rows, mix_even, mix_odd = carried

    fast = tuned(dp_size, experts)
    backs_came = {group: swap_expert(backs[group][1], 0) for group in backs}
    ups, downs, first_downs = (), (), ()
    if fast:
        plan, shapes = expert_down_plan(width, hidden)
        downs = weight_grad(act_rows, grad_rows, table, plan, shapes, [], "grad_expert_down")
    downs, backs_came, rows_in = sync(downs, backs_came, rows_in)
    far = [None] + [low([backs[group][0], backs_came[group]]) for group in range(1, groups)]
    far_sum = scatter_far(far)
    if fast:
        first_downs = line_first(downs[3])
        plan, shapes = expert_up_plan(width, hidden)
        ups = weight_grad(rows_in, grad_pre_rows, table, plan, shapes, [], "grad_expert_up")
    ups, second_in = sync(ups, second_in)

    mix_came = swap_expert(mix_odd, 0)
    if fast:
        up_came = swap_pair(ups[1])
    shared = shared_forward_backward(second_in, cotangent, mod[:, 5], up_weight, down_weight)
    shared, far_sum, mix_came, first_downs = sync(shared, far_sum, mix_came, first_downs)
    shared_act, grad_shared_pre, grad_shared, shared_out, grad_second = shared
    mix = added([mix_even, mix_came])
    mix = scatter_expert([mix[i * tokens : (i + 1) * tokens] for i in range(groups)], 1)
    if fast:
        second_downs = line_second(downs[2], low([downs[2], first_downs]))
        dense_shapes = [(2 * hidden, width // 2)] * 2
        dense = weight_grad(
            second_in, grad_shared_pre, table, dense_up_plan(width, hidden), dense_shapes, [], "grad_up"
        )
        dense = weight_grad(
            shared_act, grad_shared, table, dense_down_plan(width, hidden), dense_shapes, dense,
            "grad_down",
        )
        dense, attn_proj, mix, second_downs, up_came = sync(
            dense, attn_proj, mix, second_downs, up_came
        )
        dense_came = swap_expert(dense[0], 0)
        third = third_parts([downs[1]], *second_downs)
        ups = cut([ups[0], up_came], LINE)
        up_outer = low(ups[3])
        third, up_outer, dense_came, attn_proj = sync(third, up_outer, dense_came, attn_proj)
        third_downs = line_third(*third)
        up_first = line_first(up_outer)
        first, second = cut([dense[1], dense_came], 2)
        first, second = cut(first, 2), cut(second, 2)
        aways = low(first[1]), low(second[1])
        aways, attn_proj = sync(aways, attn_proj)
        first_came = swap_expert(aways[0], 1)
        second_came = swap_pair(aways[1])

    backward = attn_backward(
        patches, mod, attn_proj, qkv_all, log_total, cotangent, out_weight,
        [grad_second, near[0], near_came, *far_sum],
    )
    grad_qkv_rows, grad_attn, grad_middle, grad_mod_early = backward
    if fast:
        tail_shapes = [(4 * width, width // 2)] * 2
        tail = weight_grad(
            first_in, grad_qkv_rows, table, tail_plan(width, 0, 3), tail_shapes, [], "grad_qkv"
        )
        tail = weight_grad(
            attended, grad_attn, table, tail_plan(width, 3, 1), tail_shapes, tail, "grad_out"
        )
        tail, third_downs, first_came, second_came, grad_middle = sync(
            tail, third_downs, first_came, second_came, grad_middle
        )
        tail_came = swap_expert(tail[0], 0)
        second = cut([*second[0], second_came], 2)
        first = cut([*first[0], first_came], 2)
        aways = sum_many([[first[1]], [second[1]]])
        aways, grad_middle = sync(aways, grad_middle)
        first_came = swap_pair(aways[0])
        second_came = swap_expert(aways[1], 1)
    inner = input_backward(patches, mod, grad_qkv_rows, grad_middle, qkv_weight)
    if fast:
        inner, tail_came = sync(inner, tail_came)
        tail_base, *away = cut([tail[1], tail_came], 4)
        away = sum_many([[addends] for addends in away])
        away, inner, mix, first_came, second_came = sync(away, inner, mix, first_came, second_came)
        third_cames = swap_plane(away)
        first = cut([*first[0], first_came], LINE)
        second = cut([*second[0], second_came], LINE)
        aways = sum_many([[f, s] for f, s in zip(first[1:], second[1:])])
        own, away = cut(line_last([downs[0]], first_downs, *third_downs), 2)
        away = low(away)
        aways, away, mix, up_first = sync(aways, away, mix, up_first)
        up_second = sum_many([[ups[2]], [[*ups[2], up_first]]])
        up_second, mix = sync(up_second, mix)
        up_cames = line_second(*up_second)
    grad_input, grad_mod_late = inner

    middle = patches.astype(jnp.float32).reshape(latents, seq_len, width) + mod[
        :, 2:3
    ] * attn_proj.reshape(latents, seq_len, width)
    branch = (shared_out + added(mix)).reshape(latents, seq_len, width)
    block_out = (middle + mod[:, 5:6] * branch).reshape(tokens, width).astype(jnp.bfloat16)
    grad_gate_two = jnp.sum(
        cotangent.astype(jnp.float32).reshape(latents, seq_len, width) * branch, axis=1
    )
    local_counts = jnp.sum(
        (routes[:, :, None] == jnp.arange(experts, dtype=jnp.int32)).astype(jnp.int32),
        axis=(0, 1),
    )
    count_parts = jnp.concatenate([local_counts // 128, local_counts % 128]).astype(jnp.bfloat16)
    count_rows = jnp.zeros((latents, 128), jnp.bfloat16).at[0, : 2 * experts].set(count_parts)
    mods = jnp.concatenate(
        [
            grad_mod_late.reshape(latents, 2 * width).astype(jnp.bfloat16),
            grad_mod_early.reshape(latents, 3 * width).astype(jnp.bfloat16),
            grad_gate_two.astype(jnp.bfloat16),
            cond,
            count_rows,
        ],
        axis=1,
    )

    if fast:
        line_cames = line_direct(aways)
        third_cames, mods, block_out, up_cames = sync(third_cames, mods, block_out, up_cames)
        third = cut([*tail_base, *third_cames], LINE)
        tail_aways = sum_many([[addends] for addends in third[1:]])
        up_third = third_parts(ups[1], *up_cames)
        tail_aways, line_cames, mods = sync(tail_aways, line_cames, mods)
        third_cames = line_direct(tail_aways)
        mods_all = gather_ordered(mods)
        up_cames = line_third(*up_third)
        third_cames, away, mods_all = sync(third_cames, away, mods_all)
        down_came = swap_pair(away)
        dense_total = low([jnp.concatenate([added(first[0]), added(second[0])]), *line_cames])
        tail_total = low([*third[0], *third_cames])
        totals = jnp.concatenate([dense_total, tail_total], axis=0)
        totals, mods_all = sync(totals, mods_all)
        cames = share_quarters(totals)
        for bit in range(bits_of(dp_size)):
            mods_all = gather_dp_step(mods_all, bit)
        quarters = order_quarters(totals, cames)
        sum_e_up = rows_to_columns(added(line_last(ups[0], up_first, *up_cames)), hidden // width)
        sum_e_down = added([*own, down_came])
        rows = dense_total.shape[0]
        dense_sums = [jnp.concatenate([q[:rows] for q in chips]) for chips in quarters]
        tail_sums = [jnp.concatenate([q[rows:] for q in chips]) for chips in quarters]

        def columns(arrays):
            return jnp.concatenate(arrays, axis=1).astype(jnp.float32)

        half = hidden // 16
        sum_w_up, sum_w_down = [], []
        for chip in range(2):
            at = 2 * half * chip
            sum_w_up.append(
                columns([rows_to_columns(s[at : at + half], hidden // width) for s in dense_sums])
            )
            sum_w_down.append(columns([s[at + half : at + 2 * half] for s in dense_sums]))
        sum_w_up, sum_w_down = jnp.concatenate(sum_w_up), jnp.concatenate(sum_w_down)
        half = width // 16
        sum_w_qkv, sum_w_out = [], []
        for chip in range(2):
            at = 4 * half * chip
            sum_w_qkv.append(
                columns([rows_to_columns(s[at : at + 3 * half], 3) for s in tail_sums])
            )
            sum_w_out.append(columns([s[at + 3 * half : at + 4 * half] for s in tail_sums]))
        sum_w_qkv, sum_w_out = jnp.concatenate(sum_w_qkv), jnp.concatenate(sum_w_out)
    else:
        mods_all = gather_dp(gather_ordered(mods))

        def summed(left, right, axes):
            share = lax.psum_scatter(
                tn(left, right).astype(jnp.bfloat16), "dp", scatter_dimension=0, tiled=True
            )
            return (lax.psum(share, axes) if axes else share).astype(jnp.float32)

        sum_w_up = summed(second_in, grad_shared_pre, "expert")
        sum_w_down = summed(shared_act, grad_shared, "expert")
        sum_w_qkv = summed(first_in, grad_qkv_rows, "expert")
        sum_w_out = summed(attended, grad_attn, "expert")
        sum_e_up = summed(rows_in, grad_pre_rows, None)
        sum_e_down = summed(act_rows, grad_rows, None)

    grad_mod_all = mods_all[:, : 6 * width]
    count_sums = jnp.sum(mods_all[:, 7 * width :].astype(jnp.float32), axis=0).astype(jnp.int32)
    counts = count_sums[:experts] * 128 + count_sums[experts : 2 * experts]
    ada_rows = width // dp_size
    cond_mine = lax.dynamic_slice_in_dim(
        mods_all[:, 6 * width : 7 * width].T, dp_index * ada_rows, ada_rows, axis=0
    )
    sum_ada = jnp.dot(cond_mine, grad_mod_all, preferred_element_type=jnp.float32)
    bias_all = jnp.sum(grad_mod_all.astype(jnp.float32), axis=0)
    bias_size = bias_all.shape[0] // dp_size
    sum_bias = lax.dynamic_slice_in_dim(bias_all, dp_index * bias_size, bias_size)
    return (
        block_out,
        grad_input,
        sum_ada,
        sum_bias,
        sum_w_qkv,
        sum_w_out,
        sum_w_up,
        sum_w_down,
        sum_e_up[None],
        sum_e_down[None],
        counts,
    )


def solution(mesh):
    in_specs = (
        P(("dp", "expert"), None),
        P(("dp", "expert"), None),
        P(),
        P(),
        P(),
        P(),
        P(),
        P(),
        P("expert", None, None),
        P("expert", None, None),
        P(("dp", "expert"), None),
        P(("dp", "expert"), None),
        P(("dp", "expert"), None),
    )
    out_specs = (
        P(("dp", "expert"), None),
        P(("dp", "expert"), None),
        P("dp", None),
        P("dp"),
        P("dp", None),
        P("dp", None),
        P("dp", None),
        P("dp", None),
        P("expert", "dp", None),
        P("expert", "dp", None),
        P(),
    )
    return jax.shard_map(
        on_device, mesh=mesh, in_specs=in_specs, out_specs=out_specs, check_vma=False
    )
```

```python
import functools
import math

import jax
import jax.numpy as jnp
import numpy as np
from jax import lax
from jax.experimental import pallas as pl
from jax.experimental.pallas import tpu as pltpu
from jax.sharding import PartitionSpec as P

HEAD_DIM = 64
VMEM_BYTES = 56 << 20
SHRINK = 1
SQRT_TWO_OVER_PI = math.sqrt(2.0 / math.pi)


def nt(a,b): return lax.dot_general(a,b,(((1,),(1,)),((),())),preferred_element_type=jnp.float32)
def nn(a,b): return lax.dot_general(a,b,(((1,),(0,)),((),())),preferred_element_type=jnp.float32)
def tn(a,b): return lax.dot_general(a,b,(((0,),(0,)),((),())),preferred_element_type=jnp.float32)

def normalized(values_in):
    row_mean = jnp.mean(values_in, axis=-1, keepdims=True)
    centered = values_in - row_mean
    row_var = jnp.mean(centered * centered, axis=-1, keepdims=True)
    inverse = lax.rsqrt(row_var + 1e-06)
    return centered * inverse, inverse

def norm_back(grad_out, scale, normal, inverse):
    inner = grad_out * (1.0 + scale)
    mean_inner = jnp.mean(inner, axis=-1, keepdims=True)
    mean_cross = jnp.mean(inner * normal, axis=-1, keepdims=True)
    return inverse * (inner - mean_inner - normal * mean_cross)

def head_lanes(pair, head):
    lane = lax.broadcasted_iota(jnp.int32, pair.shape, 1)
    return jnp.where(lane // HEAD_DIM == head, pair, jnp.zeros_like(pair))

def attn_forward_kernel(x_ref, mod_ref, wqkv_ref, wout_ref, first_ref, qkv_ref, lse_ref, att_ref, proj_ref, second_ref):
    width = x_ref.shape[1]
    x = x_ref[...].astype(jnp.float32)
    mod = mod_ref[0]
    normal, _ = normalized(x)
    first_ref[...] = (normal * (1.0 + mod[1:2]) + mod[0:1]).astype(jnp.bfloat16)
    qkv_ref[...] = nn(first_ref[...], wqkv_ref[...]).astype(jnp.bfloat16)
    lane = 2 * HEAD_DIM
    for pair in range(width // lane):
        q2 = qkv_ref[:, pair * lane : (pair + 1) * lane]
        k2 = qkv_ref[:, width + pair * lane : width + (pair + 1) * lane]
        v2 = qkv_ref[:, 2 * width + pair * lane : 2 * width + (pair + 1) * lane]
        v2t = v2.T
        outs = []
        for head in range(2):
            scores = nt(head_lanes(k2, head), q2) * HEAD_DIM ** (-0.5)
            peak = jnp.max(scores, axis=0, keepdims=True)
            powers = jnp.exp(scores - peak)
            total = jnp.sum(powers, axis=0, keepdims=True)
            lse_ref[0, 2 * pair + head : 2 * pair + head + 1, :] = peak + jnp.log(total)
            probs = (powers * (1.0 / total)).astype(jnp.bfloat16)
            outs.append(nn(v2t[head * HEAD_DIM : (head + 1) * HEAD_DIM], probs))
        both = jnp.concatenate(outs, axis=0).astype(jnp.bfloat16)
        att_ref[:, pair * lane : (pair + 1) * lane] = both.T
    proj = nn(att_ref[...], wout_ref[...])
    proj_ref[...] = proj
    middle = x + mod[2:3] * proj
    normal2, _ = normalized(middle)
    second_ref[...] = (normal2 * (1.0 + mod[4:5]) + mod[3:4]).astype(jnp.bfloat16)

def attn_forward(patches, mod, wqkv, wout):
    tokens, width = patches.shape
    latents = mod.shape[0]
    seq = tokens // latents
    heads = width // HEAD_DIM
    rows = lambda cols: pl.BlockSpec((seq, cols), lambda i: (i, 0))
    whole = lambda a: pl.BlockSpec(a.shape, lambda i: (0, 0), pipeline_mode=pl.Buffered(1))
    return pl.pallas_call(
        attn_forward_kernel, grid=(latents,),
        in_specs=[rows(width), pl.BlockSpec((1,) + mod.shape[1:], lambda i: (i, 0, 0)), whole(wqkv), whole(wout)],
        out_specs=[rows(width), rows(3 * width), pl.BlockSpec((1, heads, seq), lambda i: (i, 0, 0)), rows(width), rows(width), rows(width)],
        out_shape=[jax.ShapeDtypeStruct((tokens, width), jnp.bfloat16), jax.ShapeDtypeStruct((tokens, 3 * width), jnp.bfloat16),
            jax.ShapeDtypeStruct((latents, heads, seq), jnp.float32), jax.ShapeDtypeStruct((tokens, width), jnp.bfloat16),
            jax.ShapeDtypeStruct((tokens, width), jnp.float32), jax.ShapeDtypeStruct((tokens, width), jnp.bfloat16)],
        compiler_params=pltpu.CompilerParams(vmem_limit_bytes=VMEM_BYTES), cost_estimate=cost(8 * tokens * width * width, 8 * width * width), name="attn_forward")(patches, mod, wqkv, wout)

def attn_backward_kernel(extra, x_ref, mod_ref, proj_ref, qkv_ref, lse_ref, cot_ref, wout_ref, *rest):
    adds = rest[:extra]
    gqkv_ref, gattn_ref, gmid_ref, gmod_ref = rest[extra:]
    width = x_ref.shape[1]
    x = x_ref[...].astype(jnp.float32)
    mod = mod_ref[0]
    proj = proj_ref[...]
    normal, inverse = normalized(x + mod[2:3] * proj)
    grad_second = adds[0][...].astype(jnp.float32)
    for a in adds[1:]:
        grad_second = grad_second + a[...].astype(jnp.float32)
    gmod_ref[0, 1:2, :] = jnp.sum(grad_second, axis=0, keepdims=True)
    gmod_ref[0, 2:3, :] = jnp.sum(grad_second * normal, axis=0, keepdims=True)
    grad_middle = cot_ref[...].astype(jnp.float32) + norm_back(grad_second, mod[4:5], normal, inverse)
    gmid_ref[...] = grad_middle
    gmod_ref[0, 0:1, :] = jnp.sum(grad_middle * proj, axis=0, keepdims=True)
    gattn_ref[...] = (mod[2:3] * grad_middle).astype(jnp.bfloat16)
    grad_att = nt(gattn_ref[...], wout_ref[...]).astype(jnp.bfloat16)
    lane = 2 * HEAD_DIM
    scale = HEAD_DIM ** (-0.5)
    for pair in range(width // lane):
        sl = slice(pair * lane, (pair + 1) * lane)
        q2 = qkv_ref[:, pair * lane : (pair + 1) * lane]
        k2 = qkv_ref[:, width + pair * lane : width + (pair + 1) * lane]
        v2 = qkv_ref[:, 2 * width + pair * lane : 2 * width + (pair + 1) * lane]
        do2 = grad_att[:, sl]
        k2t = k2.T
        gq, gk, gv = [], [], []
        for head in range(2):
            scores = nt(head_lanes(k2, head), q2) * scale
            probs = jnp.exp(scores - lse_ref[0, 2 * pair + head : 2 * pair + head + 1, :])
            grad_probs = nt(head_lanes(v2, head), do2)
            inner = jnp.sum(probs * grad_probs, axis=0, keepdims=True)
            grad_scores = (probs * (grad_probs - inner)).astype(jnp.bfloat16)
            gv.append(nn(probs.astype(jnp.bfloat16), do2))
            gk.append(nn(grad_scores, q2))
            gq.append(nn(k2t[head * HEAD_DIM : (head + 1) * HEAD_DIM], grad_scores))
        low = lax.broadcasted_iota(jnp.int32, gv[0].shape, 1) < HEAD_DIM
        gqt = (jnp.concatenate(gq, axis=0) * scale).astype(jnp.bfloat16)
        gqkv_ref[:, pair * lane : (pair + 1) * lane] = gqt.T
        gqkv_ref[:, width + pair * lane : width + (pair + 1) * lane] = (jnp.where(low, gk[0], gk[1]) * scale).astype(jnp.bfloat16)
        gqkv_ref[:, 2 * width + pair * lane : 2 * width + (pair + 1) * lane] = jnp.where(low, gv[0], gv[1]).astype(jnp.bfloat16)

def attn_backward(patches, mod, proj, qkv, lse, cot, wout, adds):
    tokens, width = patches.shape
    latents = mod.shape[0]
    seq = tokens // latents
    rows = lambda cols: pl.BlockSpec((seq, cols), lambda i: (i, 0))
    per = lambda a: pl.BlockSpec((1,) + a.shape[1:], lambda i: (i, 0, 0))
    whole = lambda a: pl.BlockSpec(a.shape, lambda i: (0, 0), pipeline_mode=pl.Buffered(1))
    return pl.pallas_call(
        functools.partial(attn_backward_kernel, len(adds)), grid=(latents,),
        in_specs=[rows(width), per(mod), rows(width), rows(3 * width), per(lse), rows(width), whole(wout)] + [rows(width)] * len(adds),
        out_specs=[rows(3 * width), rows(width), rows(width), pl.BlockSpec((1, 3, width), lambda i: (i, 0, 0))],
        out_shape=[jax.ShapeDtypeStruct((tokens, 3 * width), jnp.bfloat16), jax.ShapeDtypeStruct((tokens, width), jnp.bfloat16),
            jax.ShapeDtypeStruct((tokens, width), jnp.float32), jax.ShapeDtypeStruct((latents, 3, width), jnp.float32)],
        compiler_params=pltpu.CompilerParams(vmem_limit_bytes=VMEM_BYTES), cost_estimate=cost(8 * tokens * width * width, 8 * width * width), name="attn_backward")(patches, mod, proj, qkv, lse, cot, wout, *adds)

def input_backward_kernel(x_ref, mod_ref, gqkv_ref, gmid_ref, wqkv_ref, gin_ref, gmod_ref):
    mod = mod_ref[0]
    normal, inverse = normalized(x_ref[...].astype(jnp.float32))
    grad_first = nt(gqkv_ref[...], wqkv_ref[...])
    gmod_ref[0, 0:1, :] = jnp.sum(grad_first, axis=0, keepdims=True)
    gmod_ref[0, 1:2, :] = jnp.sum(grad_first * normal, axis=0, keepdims=True)
    gin_ref[...] = gmid_ref[...] + norm_back(grad_first, mod[1:2], normal, inverse)

def input_backward(patches, mod, gqkv, gmid, wqkv):
    tokens, width = patches.shape
    latents = mod.shape[0]
    seq = tokens // latents
    rows = lambda cols: pl.BlockSpec((seq, cols), lambda i: (i, 0))
    per = lambda a: pl.BlockSpec((1,) + a.shape[1:], lambda i: (i, 0, 0))
    whole = lambda a: pl.BlockSpec(a.shape, lambda i: (0, 0), pipeline_mode=pl.Buffered(1))
    return pl.pallas_call(
        input_backward_kernel, grid=(latents,),
        in_specs=[rows(width), per(mod), rows(3 * width), rows(width), whole(wqkv)],
        out_specs=[rows(width), pl.BlockSpec((1, 2, width), lambda i: (i, 0, 0))],
        out_shape=[jax.ShapeDtypeStruct((tokens, width), jnp.float32), jax.ShapeDtypeStruct((latents, 2, width), jnp.float32)],
        compiler_params=pltpu.CompilerParams(vmem_limit_bytes=VMEM_BYTES), cost_estimate=cost(6 * tokens * width * width, 6 * width * width), name="input_backward")(patches, mod, gqkv, gmid, wqkv)


def cost(flops, size):
    return pl.CostEstimate(flops=int(flops) // SHRINK, bytes_accessed=int(size) // SHRINK, transcendentals=0)


def feed_forward_step(x_ref, g_ref, up_ref, down_ref, act_ref, gpre_ref, out_acc, grad_acc):
    inner_scale = SQRT_TWO_OVER_PI
    cubic = 0.044715
    pre = nn(x_ref[...], up_ref[...])
    grad_act = nt(g_ref[...], down_ref[...])
    squared = pre * pre
    bent = jnp.tanh(pre * (inner_scale + (inner_scale * cubic) * squared))
    half = 0.5 + 0.5 * bent
    act = (pre * half).astype(jnp.bfloat16)
    slope = half + (0.5 * pre) * (1.0 - bent * bent) * (
        inner_scale + (3.0 * cubic * inner_scale) * squared
    )
    grad_pre = (grad_act * slope).astype(jnp.bfloat16)
    act_ref[...] = act
    gpre_ref[...] = grad_pre
    out_acc[...] += nn(act, down_ref[...])
    grad_acc[...] += nt(grad_pre, up_ref[...])


def shared_kernel(
    x_ref, cot_ref, gate_ref, up_ref, down_ref,
    act_ref, gpre_ref, g_ref, out_ref, grad_ref,
    out_acc, grad_acc,
):
    step = pl.program_id(0)
    latents = gate_ref.shape[0]
    seq = x_ref.shape[0] // latents

    @pl.when(step == 0)
    def _():
        out_acc[...] = jnp.zeros_like(out_acc)
        grad_acc[...] = jnp.zeros_like(grad_acc)
        for i in range(latents):
            rows = slice(i * seq, (i + 1) * seq)
            g_ref[rows, :] = (gate_ref[i : i + 1, :] * cot_ref[rows, :].astype(jnp.float32)).astype(
                jnp.bfloat16
            )

    feed_forward_step(x_ref, g_ref, up_ref, down_ref, act_ref, gpre_ref, out_acc, grad_acc)

    @pl.when(step == pl.num_programs(0) - 1)
    def _():
        out_ref[...] = out_acc[...]
        grad_ref[...] = grad_acc[...]


def tile_of(width):
    return width // 4 if width % 512 == 0 else width


def still(array):
    return pl.BlockSpec(
        array.shape, lambda j, n=len(array.shape): (0,) * n, pipeline_mode=pl.Buffered(1)
    )


def shared_forward_backward(x, cot, gate, up, down):
    rows, width = x.shape
    hidden = up.shape[1]
    tile = tile_of(hidden)
    out = jax.ShapeDtypeStruct((rows, width), jnp.float32)
    wide = jax.ShapeDtypeStruct((rows, hidden), jnp.bfloat16)
    fixed = pl.BlockSpec((rows, width), lambda j: (0, 0))
    column = pl.BlockSpec((rows, tile), lambda j: (0, j))
    return pl.pallas_call(
        shared_kernel,
        grid=(hidden // tile,),
        in_specs=[
            still(x), still(cot), still(gate),
            pl.BlockSpec((width, tile), lambda j: (0, j)),
            pl.BlockSpec((tile, width), lambda j: (j, 0)),
        ],
        out_specs=[column, column, fixed, fixed, fixed],
        out_shape=[wide, wide, jax.ShapeDtypeStruct((rows, width), jnp.bfloat16), out, out],
        scratch_shapes=[pltpu.VMEM((rows, width), jnp.float32)] * 2,
        compiler_params=pltpu.CompilerParams(vmem_limit_bytes=VMEM_BYTES),
        cost_estimate=cost(8 * rows * width * hidden, 4 * width * hidden + 4 * rows * hidden),
        name="shared_ffn",
    )(x, cot, gate, up, down)


def expert_kernel(blocks, carried, *refs):
    xs, cots = refs[:blocks], refs[blocks : 2 * blocks]
    slot_row, slot_col, gate_col, gate_two, up_ref, down_ref = refs[2 * blocks : 2 * blocks + 6]
    rest = refs[2 * blocks + 6 + carried :]
    act_ref, gpre_ref, x_ref, g_ref = rest[:4]
    mixes, backs = rest[4 : 4 + blocks], rest[4 + blocks : 4 + 2 * blocks]
    out_acc, grad_acc = rest[4 + 2 * blocks :]
    step = pl.program_id(0)
    tokens = xs[0].shape[0]
    capacity = x_ref.shape[0] // blocks
    latents = gate_two.shape[1]
    seq = tokens // latents

    @pl.when(step == 0)
    def _():
        out_acc[...] = jnp.zeros_like(out_acc)
        grad_acc[...] = jnp.zeros_like(grad_acc)
        for b in range(blocks):
            rows = slice(b * capacity, (b + 1) * capacity)
            places = lax.broadcasted_iota(jnp.int32, (capacity, tokens), 0)
            pick = (places == slot_row[b]).astype(jnp.float32).astype(jnp.bfloat16)
            x_ref[rows, :] = nn(pick, xs[b][...]).astype(jnp.bfloat16)
            grads = []
            for i in range(latents):
                part = slice(i * seq, (i + 1) * seq)
                branch = gate_two[b, i : i + 1, :] * cots[b][part, :].astype(jnp.float32)
                grads.append((gate_col[b, part, :] * branch).astype(jnp.bfloat16))
            grad = jnp.concatenate(grads, axis=0)
            g_ref[rows, :] = nn(pick, grad).astype(jnp.bfloat16)

    feed_forward_step(x_ref, g_ref, up_ref, down_ref, act_ref, gpre_ref, out_acc, grad_acc)

    @pl.when(step == pl.num_programs(0) - 1)
    def _():
        for b in range(blocks):
            rows = slice(b * capacity, (b + 1) * capacity)
            places = lax.broadcasted_iota(jnp.int32, (tokens, capacity), 1)
            pick = (places == slot_col[b]).astype(jnp.float32).astype(jnp.bfloat16)
            backs[b][...] = nn(pick, grad_acc[rows, :].astype(jnp.bfloat16)).astype(jnp.bfloat16)
            mixed = nn(pick, out_acc[rows, :].astype(jnp.bfloat16))
            mixes[b][...] = (gate_col[b] * mixed).astype(jnp.bfloat16)


def expert_forward_backward(
    xs, cots, slot_row, slot_col, gate_col, gate_two, up, down, capacity, groups, group, carried
):
    blocks = len(xs)
    tokens, width = xs[0].shape
    hidden = up.shape[1]
    tile = tile_of(hidden)
    rows = blocks * capacity
    wide = jax.ShapeDtypeStruct((rows * groups, hidden), jnp.bfloat16)
    slim = jax.ShapeDtypeStruct((rows * groups, width), jnp.bfloat16)
    mixture = jax.ShapeDtypeStruct((tokens * groups, width), jnp.bfloat16)
    token = jax.ShapeDtypeStruct((tokens, width), jnp.bfloat16)
    column = pl.BlockSpec((rows, tile), lambda j: (group, j))
    own = pl.BlockSpec((rows, width), lambda j: (group, 0))
    mixed = pl.BlockSpec((tokens, width), lambda j: (group, 0))
    fixed = pl.BlockSpec((tokens, width), lambda j: (0, 0))
    small = [slot_row, slot_col, gate_col, gate_two]
    first = 2 * blocks + 6
    return pl.pallas_call(
        functools.partial(expert_kernel, blocks, len(carried)),
        grid=(hidden // tile,),
        in_specs=[still(a) for a in (*xs, *cots)]
        + [
            pl.BlockSpec(
                (blocks,) + a.shape[1:], lambda j, n=len(a.shape) - 1: (group,) + (0,) * n,
                pipeline_mode=pl.Buffered(1),
            )
            for a in small
        ]
        + [
            pl.BlockSpec((width, tile), lambda j: (0, j)),
            pl.BlockSpec((tile, width), lambda j: (j, 0)),
        ]
        + [pl.BlockSpec(memory_space=pl.ANY)] * len(carried),
        out_specs=[column, column, own, own] + [mixed] * blocks + [fixed] * blocks,
        scratch_shapes=[pltpu.VMEM((rows, width), jnp.float32)] * 2,
        out_shape=[wide, wide, slim, slim] + [mixture] * blocks + [token] * blocks,
        input_output_aliases={first + i: i for i in range(len(carried))},
        compiler_params=pltpu.CompilerParams(vmem_limit_bytes=VMEM_BYTES),
        cost_estimate=cost(8 * rows * width * hidden, 4 * width * hidden + 4 * rows * hidden),
        name="expert_ffn",
    )(*xs, *cots, *small, up, down, *carried)


def route_kernel(index_ref, info_ref, time_ref, ada_ref, bias_ref, row_ref, col_ref, gate_ref, two_ref):
    experts, _, tokens = row_ref.shape
    latents = time_ref.shape[0] // experts
    expert = index_ref[0]
    slots, gates = [], []
    before = (
        lax.broadcasted_iota(jnp.int32, (tokens, tokens), 0)
        < lax.broadcasted_iota(jnp.int32, (tokens, tokens), 1)
    ).astype(jnp.float32).astype(jnp.bfloat16)
    for r in range(experts):
        routes = info_ref[r, 0:2, :].astype(jnp.int32)
        named = routes == expert
        member = jnp.sum(named.astype(jnp.float32), axis=0, keepdims=True)
        earlier = nn(member.astype(jnp.bfloat16), before)
        slot = jnp.where(member > 0.5, earlier, float(tokens))
        row_ref[r] = slot.astype(jnp.int32)
        slots.append(slot)
        gates.append(
            jnp.sum(jnp.where(named, info_ref[r, 2:4, :], 0.0), axis=0, keepdims=True)
        )
    turned = jnp.concatenate(slots + gates, axis=0).T
    for r in range(experts):
        col_ref[r] = turned[:, r : r + 1].astype(jnp.int32)
        gate_ref[r] = turned[:, experts + r : experts + r + 1]
    times = time_ref[...]
    cond = (times / (1.0 + jnp.exp(-times))).astype(jnp.bfloat16)
    gate_two = nn(cond, ada_ref[...]) + bias_ref[...]
    for r in range(experts):
        two_ref[r] = gate_two[r * latents : (r + 1) * latents]


def route(expert, info, times, ada_weight, ada_bias, tokens):
    experts = info.shape[0]
    width = times.shape[1]
    latents = times.shape[0] // experts
    vmem = pl.BlockSpec(memory_space=pltpu.VMEM)
    return pl.pallas_call(
        route_kernel,
        grid=(1,),
        in_specs=[
            pl.BlockSpec(memory_space=pltpu.SMEM), still(info), still(times),
            pl.BlockSpec((width, width), lambda j: (0, 5)),
            pl.BlockSpec((1, width), lambda j: (0, 5)),
        ],
        out_specs=[vmem] * 4,
        out_shape=[
            jax.ShapeDtypeStruct((experts, 1, tokens), jnp.int32),
            jax.ShapeDtypeStruct((experts, tokens, 1), jnp.int32),
            jax.ShapeDtypeStruct((experts, tokens, 1), jnp.float32),
            jax.ShapeDtypeStruct((experts, latents, width), jnp.float32),
        ],
        compiler_params=pltpu.CompilerParams(vmem_limit_bytes=VMEM_BYTES),
        name="route",
    )(expert, info, times, ada_weight, ada_bias[None])


def weight_grad_kernel(steps, by_columns, moves, outs, carried, table, a_ref, b_ref, *rest):
    rest = rest[carried:]
    out_refs = rest[:outs]
    sum_ref, sems = rest[outs], rest[outs + 1]
    step = pl.program_id(0)
    if by_columns:
        turned = rest[outs + 2]

        @pl.when(step == 0)
        def _():
            turned[...] = a_ref[...].T

        sum_ref[step] = nn(turned[...], b_ref[...]).astype(jnp.bfloat16)
    else:
        sum_ref[step] = tn(a_ref[...], b_ref[...]).astype(jnp.bfloat16)

    def copies(at):
        for i, (when, out, row, rows, terms, col_from, cols) in enumerate(moves):
            if at is not None and when != at:
                continue
            start = terms[0]
            for entry, scale in terms[1:]:
                start = start + table[entry] * scale
            if len(terms) > 1:
                start = pl.multiple_of(start, 8)
            if isinstance(col_from, tuple):
                chooser, half = col_from
                column = pl.multiple_of(table[chooser] * half, 128)
            else:
                column = col_from
            yield pltpu.make_async_copy(
                sum_ref.at[when, pl.ds(start, rows), pl.ds(column, cols)],
                out_refs[out].at[pl.ds(row, rows), :],
                sems.at[i],
            )

    for at in range(steps):

        @pl.when(step == at)
        def _(at=at):
            for copy in copies(at):
                copy.start()

    @pl.when(step == steps - 1)
    def _():
        for copy in copies(None):
            copy.wait()


def weight_grad(a, b, table, plan, shapes, carried, name):
    tile, by_columns, a_map, b_map, moves = plan
    rows, left = a.shape
    right = b.shape[1]
    if by_columns:
        steps = right // tile
        specs = [
            pl.BlockSpec((rows, left), a_map, pipeline_mode=pl.Buffered(1)),
            pl.BlockSpec((rows, tile), b_map),
        ]
        scratch = [pltpu.VMEM((steps, left, tile), jnp.bfloat16)]
        extra = [pltpu.VMEM((left, rows), jnp.bfloat16)]
    else:
        steps = left // tile
        specs = [
            pl.BlockSpec((rows, tile), a_map),
            pl.BlockSpec((rows, right), b_map, pipeline_mode=pl.Buffered(1)),
        ]
        scratch = [pltpu.VMEM((steps, tile, right), jnp.bfloat16)]
        extra = []
    anywhere = pl.BlockSpec(memory_space=pl.ANY)
    return pl.pallas_call(
        functools.partial(
            weight_grad_kernel, steps, by_columns, moves, len(shapes), len(carried)
        ),
        grid_spec=pltpu.PrefetchScalarGridSpec(
            num_scalar_prefetch=1,
            grid=(steps,),
            in_specs=specs + [anywhere] * len(carried),
            out_specs=[anywhere] * len(shapes),
            scratch_shapes=[*scratch, pltpu.SemaphoreType.DMA((len(moves),)), *extra],
        ),
        out_shape=[jax.ShapeDtypeStruct(s, jnp.bfloat16) for s in shapes],
        input_output_aliases={3 + i: i for i in range(len(carried))},
        compiler_params=pltpu.CompilerParams(vmem_limit_bytes=VMEM_BYTES),
        cost_estimate=cost(2 * rows * left * right, 2 * left * right + 2 * rows * (left + right)),
        name=name,
    )(table, a, b, *carried)


def bits_of(size):
    return size.bit_length() - 1


def label_of(index):
    upper = index >> 1
    return ((upper ^ (upper >> 1)) << 1) | (index & 1)


def index_of(label):
    upper = label >> 1
    shift = 1
    while shift < 32:
        upper = upper ^ (upper >> shift)
        shift *= 2
    return (upper << 1) | (label & 1)


def swap_dp(value, bit):
    size = lax.axis_size("dp")
    return lax.ppermute(
        value, "dp", [(i, index_of(label_of(i) ^ (1 << bit))) for i in range(size)]
    )


def swap_expert(value, bit):
    size = lax.axis_size("expert")
    step = size - 1 if bit is None else 1 << bit
    return lax.ppermute(value, "expert", [(i, i ^ step) for i in range(size)])


def gather_expert(value):
    bits = bits_of(lax.axis_size("expert"))
    parts = {0: value}
    for bit in reversed(range(bits)):
        for r in list(parts):
            parts[r | (1 << bit)] = swap_expert(parts[r], bit)
    return [parts[r] for r in range(1 << bits)]


def gather_ordered(value):
    mine = lax.axis_index("expert")
    for bit in range(bits_of(lax.axis_size("expert"))):
        other = swap_expert(value, bit)
        upper = (mine >> bit & 1) == 1
        value = jnp.concatenate(
            [jnp.where(upper, other, value), jnp.where(upper, value, other)], axis=0
        )
    return value


def gather_expert_stacked(value):
    held, places = value[None], [0]
    for bit in reversed(range(bits_of(lax.axis_size("expert")))):
        held = jnp.concatenate([held, swap_expert(held, bit)])
        places += [place | (1 << bit) for place in places]
    return jnp.concatenate([held[places.index(r)][None] for r in range(len(places))])


def scatter_expert(parts, first_bit=0):
    parts = [[part] for part in parts]
    for bit in range(first_bit, bits_of(lax.axis_size("expert"))):
        left = []
        for kept, away in zip(parts[::2], parts[1::2]):
            away = away[0].astype(jnp.bfloat16) if len(away) == 1 else added(away).astype(jnp.bfloat16)
            kept = kept if len(kept) == 1 else [added(kept).astype(jnp.bfloat16)]
            left.append([*kept, swap_expert(away, bit)])
        parts = left
    return parts[0]


def gather_dp_step(value, bit):
    return jnp.concatenate([value, swap_dp(value, bit)], axis=0)


def gather_dp(value):
    for bit in range(bits_of(lax.axis_size("dp"))):
        value = gather_dp_step(value, bit)
    return value


LINE, PAIR = 4, 2
CORE, CHIP, AHEAD = 8, 10, 12


def tuned(mesh_dp, experts):
    return mesh_dp == LINE * PAIR and experts == 4


def shard_table():
    dp, expert = lax.axis_index("dp"), lax.axis_index("expert")
    relative = jnp.arange(LINE * PAIR, dtype=jnp.int32)
    place, along, across = dp // PAIR, relative // PAIR, dp % PAIR ^ relative % PAIR
    inwards = jnp.where(place < LINE // 2, place + along, place - along + LINE) % LINE
    ahead = (place + along) % LINE
    core, chip = expert & 1, expert >> 1
    return jnp.concatenate(
        [inwards * PAIR + across, jnp.stack([core, 1 - core, chip, 1 - chip]), ahead * PAIR + across]
    ).astype(jnp.int32)


def relatives():
    return [(2 * along + across, along, across) for along in range(LINE) for across in range(PAIR)]


def by_shard(shard, first, moves):
    return (shard, False, lambda j, t: (0, t[first + j]), lambda j, t: (0, 0), moves)


def halves_map(half_steps):
    return lambda j, t: (
        0,
        jnp.where(j < half_steps, t[CORE + 1] * half_steps + j, (t[CORE] - 1) * half_steps + j),
    )


def expert_down_plan(width, hidden):
    shard = hidden // 8
    moves = [
        (relative, along, across * shard, shard, (0,), 0, width)
        for relative, along, across in relatives()
    ]
    return by_shard(shard, 0, moves), [(PAIR * shard, width)] * LINE


def expert_up_plan(width, hidden):
    shard = width // 8
    steps = hidden // width
    moves = [
        (step, across, (along * steps + step) * shard, shard, (0, (relative, shard)), 0, width)
        for step in range(steps)
        for relative, along, across in relatives()
    ]
    plan = (width, True, lambda j, t: (0, 0), lambda j, t: (0, j), moves)
    return plan, [(LINE * steps * shard, width)] * PAIR


def dense_place(chip_first, chip, along, across):
    outer, inner = (chip, across) if chip_first else (across, chip)
    return (2 * outer + inner) * LINE + along


def dense_up_plan(width, hidden):
    cols, shard = width // 2, width // 8
    rows = shard // 2
    unit = rows * (hidden // width)
    half_steps = hidden // width // 2
    moves = []
    for step in range(2 * half_steps):
        for block in range(2):
            column = 2 * (step % half_steps) + block
            for relative, along, across in relatives():
                for chip in range(2):
                    row = dense_place(True, chip, along, across) * unit + column * rows
                    source = (0, (AHEAD + relative, shard), (CHIP + chip, rows))
                    moves.append((step, step // half_steps, row, rows, source, block * cols, cols))
    return (width, True, lambda j, t: (0, 0), halves_map(half_steps), moves)


def dense_down_plan(width, hidden):
    cols = width // 2
    unit = hidden // 8 // 2
    moves = []
    for relative, along, across in relatives():
        for out in range(2):
            for chip in range(2):
                row = (16 + dense_place(False, chip, along, across)) * unit
                source = (0, (CHIP + chip, unit))
                moves.append((relative, out, row, unit, source, (CORE + 1 - out, cols), cols))
    return by_shard(hidden // 8, AHEAD, moves)


def tail_plan(width, first, count):
    cols, shard = width // 2, width // 8
    rows = shard // 2
    moves = []
    for step in range(2):
        for block in range(count):
            for relative, along, across in relatives():
                for chip in range(2):
                    row = (dense_place(True, chip, along, across) * 4 + first + block) * rows
                    source = (0, (AHEAD + relative, shard), (CHIP + chip, rows))
                    moves.append((step, step, row, rows, source, block * cols, cols))
    return (count * cols, True, lambda j, t: (0, 0), halves_map(1), moves)


def low(parts):
    return added(parts).astype(jnp.bfloat16)


class View:
    def __init__(self, array, start, rows):
        self.array, self.start, self.rows = array, start, rows


def view(value):
    return value if isinstance(value, View) else View(value, 0, value.shape[0])


def sum_many(stacks):
    stacks = [[[view(value) for value in addends] for addends in stack] for stack in stacks]
    rows = stacks[0][0][0].rows
    block = 192 if rows % 192 == 0 and rows > 192 else 96
    steps = rows // block
    depth = len(stacks[0])
    arrays, specs, shapes = [], [], []
    for stack in stacks:
        width = stack[0][0].array.shape[1]
        shapes.append(jax.ShapeDtypeStruct((depth * rows, width), jnp.bfloat16))
        for level, addends in enumerate(stack):
            for value in addends:
                first = value.start // block
                arrays.append(value.array)
                specs.append(
                    pl.BlockSpec(
                        (block, width),
                        lambda i, f=first, l=level: (f + jnp.clip(i - l * steps, 0, steps - 1), 0),
                    )
                )

    def kernel(*refs):
        outs = refs[len(arrays) :]
        for level in range(depth):

            @pl.when(pl.program_id(0) // steps == level)
            def _(level=level):
                at = 0
                for out, stack in zip(outs, stacks):
                    for here, addends in enumerate(stack):
                        if here == level:
                            total = refs[at][...].astype(jnp.float32)
                            for extra in range(1, len(addends)):
                                total = total + refs[at + extra][...].astype(jnp.float32)
                            out[...] = total.astype(jnp.bfloat16)
                        at += len(addends)

    return pl.pallas_call(
        kernel,
        grid=(depth * steps,),
        in_specs=specs,
        out_specs=[pl.BlockSpec((block, s.shape[1]), lambda i: (i, 0)) for s in shapes],
        out_shape=shapes,
        compiler_params=pltpu.CompilerParams(vmem_limit_bytes=VMEM_BYTES),
        name="sum_many",
    )(*arrays)


def sync(*values):
    return lax.optimization_barrier(values)


def cut(addends, count):
    views = [view(value) for value in addends]
    left = views[0].rows // count
    return [[View(v.array, v.start + i * left, left) for v in views] for i in range(count)]


def swap_pair(value):
    return lax.ppermute(value, "dp", [(i, i ^ 1) for i in range(LINE * PAIR)])


def move_line(value, pairs):
    return lax.ppermute(
        value, "dp", [(a * PAIR + i, b * PAIR + i) for a, b in pairs for i in range(PAIR)]
    )


OUTSIDE = [(0, 1), (1, 0), (2, 3), (3, 2)]


def at_end():
    place = lax.axis_index("dp") // PAIR
    return (place == 0) | (place == LINE - 1)


def line_first(outer):
    return move_line(outer, OUTSIDE)


def move_inside(value):
    experts = lax.axis_size("expert")
    pairs = []
    for place in range(LINE):
        for rest in range(PAIR * experts):
            here = place * PAIR * experts + rest
            there = here ^ 1 if place in (0, LINE - 1) else (LINE - 1 - place) * PAIR * experts + rest
            pairs.append((here, there))
    return lax.ppermute(value, ("dp", "expert"), pairs)


def line_second(outside, inside):
    return move_line(outside, OUTSIDE), move_inside(inside)


def third_parts(inner, outside, inside):
    return jnp.where(at_end(), low(inner), inside), low([*inner, outside])


def line_third(outside, inside):
    return move_line(outside, OUTSIDE), move_inside(inside)


def line_last(own, first, outside, inside):
    return [*own, outside, jnp.where(at_end(), plain(first), inside)]


def line_direct(aways):
    return [
        move_line(away, [(i, (i + ahead) % LINE) for i in range(LINE)])
        for ahead, away in enumerate(aways, 1)
    ]


def swap_both(value, dp_step, expert_step):
    experts = lax.axis_size("expert")
    pairs = [
        (dp * experts + expert, (dp ^ dp_step) * experts + (expert ^ expert_step))
        for dp in range(LINE * PAIR)
        for expert in range(experts)
    ]
    return lax.ppermute(value, ("dp", "expert"), pairs)


def swap_plane(aways):
    return [swap_pair(aways[0]), swap_expert(aways[1], 1), swap_both(aways[2], 1, 2)]


def share_quarters(total):
    return [swap_expert(total, 0), swap_expert(total, 1), swap_expert(total, None)]


def order_quarters(total, cames):
    core, chip, both = cames
    expert = lax.axis_index("expert")
    right, upper = (expert & 1) == 1, (expert >> 1) == 1
    mine = jnp.where(upper, chip, total), jnp.where(upper, total, chip)
    other = jnp.where(upper, both, core), jnp.where(upper, core, both)
    return [
        [jnp.where(right, o, s) for o, s in zip(other, mine)],
        [jnp.where(right, s, o) for o, s in zip(other, mine)],
    ]


def swap_stack(held, bit):
    return jnp.concatenate([held, swap_expert(held, bit)])


def stack_order(held):
    places = [0]
    for bit in reversed(range(bits_of(held.shape[0]))):
        places += [place | (1 << bit) for place in places]
    return jnp.concatenate([held[places.index(r)][None] for r in range(len(places))])


def gather_chips(value):
    parts = {0: value}
    for bit in reversed(range(1, bits_of(lax.axis_size("expert")))):
        for r in list(parts):
            parts[r | (1 << bit)] = swap_expert(parts[r], bit)
    return parts


def rows_to_columns(stacked, count):
    rows = stacked.shape[0] // count
    return jnp.concatenate([stacked[i * rows : (i + 1) * rows] for i in range(count)], axis=1)


def plain(value):
    if isinstance(value, View):
        return value.array[value.start : value.start + value.rows]
    return value


def added(parts):
    total = plain(parts[0]).astype(jnp.float32)
    for part in parts[1:]:
        total = total + plain(part).astype(jnp.float32)
    return total


def scatter_far(parts):
    came = []
    for bit in range(1, bits_of(lax.axis_size("expert"))):
        left = []
        for kept, away in zip(parts[::2], parts[1::2]):
            moved = swap_expert(away, bit)
            if kept is None:
                came.append(moved)
                left.append(None)
            else:
                left.append(added([kept, moved]).astype(jnp.bfloat16))
        parts = left
    return came


def on_device(
    patches,
    time_embed,
    ada_weight,
    ada_bias,
    qkv_weight,
    out_weight,
    up_weight,
    down_weight,
    expert_up,
    expert_down,
    routes,
    gate_weights,
    cotangent,
):
    tokens, width = patches.shape
    latents = time_embed.shape[0]
    seq_len = tokens // latents
    experts = lax.axis_size("expert")
    dp_size = lax.axis_size("dp")
    dp_index = lax.axis_index("dp")
    expert_index = lax.axis_index("expert")
    capacity = 5 * tokens // (2 * experts)

    hidden = up_weight.shape[1]
    blocks = 2
    groups = experts // blocks
    table = shard_table()

    info = jnp.concatenate(
        [
            routes.T.astype(jnp.float32),
            gate_weights.T,
            time_embed.astype(jnp.float32).reshape(-1, tokens),
        ],
        axis=0,
    )
    info = swap_stack(info[None], bits_of(experts) - 1)
    cots = gather_chips(cotangent)
    cots[1] = swap_expert(cotangent, 0)
    for bit in reversed(range(bits_of(experts) - 1)):
        info = swap_stack(info, bit)
    info_all = stack_order(info)
    cond = jax.nn.silu(time_embed.astype(jnp.float32)).astype(jnp.bfloat16)
    modulation = jnp.dot(cond, ada_weight, preferred_element_type=jnp.float32) + ada_bias
    mod = modulation.reshape(latents, 6, width)
    first_in, qkv_all, log_total, attended, attn_proj, second_in = attn_forward(
        patches, mod, qkv_weight, out_weight
    )
    second_in, cots = sync(second_in, cots)

    seconds = gather_chips(second_in)
    seconds[1] = swap_expert(second_in, 0)
    routed = route(
        expert_index[None], info_all[:, :4], info_all[:, 4:].reshape(experts * latents, width),
        ada_weight, ada_bias, tokens,
    )
    routed, seconds[1] = sync(routed, seconds[1])
    for r in range(2, experts, 2):
        cots[r + 1] = swap_expert(cots[r], 0)

    def run_group(group, carried):
        span = range(group * blocks, (group + 1) * blocks)
        results = expert_forward_backward(
            [seconds[r] for r in span], [cots[r] for r in span], *routed, expert_up[0], expert_down[0],
            capacity, groups, group, carried,
        )
        return results[: 4 + blocks], results[4 + blocks :]

    carried, near = run_group(0, [])
    carried, near, seconds, cots = sync(carried, near, seconds, cots)
    for r in range(2, experts, 2):
        seconds[r + 1] = swap_expert(seconds[r], 0)
    near_came = swap_expert(near[1], 0)
    backs = {}
    for group in range(1, groups):
        carried, backs[group] = run_group(group, carried)
    carried, backs, near_came = sync(carried, backs, near_came)
    act_rows, grad_pre_rows, rows_in, grad_rows, mix_even, mix_odd = carried

    fast = tuned(dp_size, experts)
    backs_came = {group: swap_expert(backs[group][1], 0) for group in backs}
    ups, downs, first_downs = (), (), ()
    if fast:
        plan, shapes = expert_down_plan(width, hidden)
        downs = weight_grad(act_rows, grad_rows, table, plan, shapes, [], "grad_expert_down")
    downs, backs_came, rows_in = sync(downs, backs_came, rows_in)
    far = [None] + [low([backs[group][0], backs_came[group]]) for group in range(1, groups)]
    far_sum = scatter_far(far)
    if fast:
        first_downs = line_first(downs[3])
        plan, shapes = expert_up_plan(width, hidden)
        ups = weight_grad(rows_in, grad_pre_rows, table, plan, shapes, [], "grad_expert_up")
    ups, second_in = sync(ups, second_in)

    mix_came = swap_expert(mix_odd, 0)
    if fast:
        up_came = swap_pair(ups[1])
    shared = shared_forward_backward(second_in, cotangent, mod[:, 5], up_weight, down_weight)
    shared, far_sum, mix_came, first_downs = sync(shared, far_sum, mix_came, first_downs)
    shared_act, grad_shared_pre, grad_shared, shared_out, grad_second = shared
    mix = added([mix_even, mix_came])
    mix = scatter_expert([mix[i * tokens : (i + 1) * tokens] for i in range(groups)], 1)
    if fast:
        second_downs = line_second(downs[2], low([downs[2], first_downs]))
        dense_shapes = [(2 * hidden, width // 2)] * 2
        dense = weight_grad(
            second_in, grad_shared_pre, table, dense_up_plan(width, hidden), dense_shapes, [], "grad_up"
        )
        dense = weight_grad(
            shared_act, grad_shared, table, dense_down_plan(width, hidden), dense_shapes, dense,
            "grad_down",
        )
        dense, attn_proj, mix, second_downs, up_came = sync(
            dense, attn_proj, mix, second_downs, up_came
        )
        dense_came = swap_expert(dense[0], 0)
        third = third_parts([downs[1]], *second_downs)
        ups = cut([ups[0], up_came], LINE)
        up_outer = low(ups[3])
        third, up_outer, dense_came, attn_proj = sync(third, up_outer, dense_came, attn_proj)
        third_downs = line_third(*third)
        up_first = line_first(up_outer)
        first, second = cut([dense[1], dense_came], 2)
        first, second = cut(first, 2), cut(second, 2)
        aways = low(first[1]), low(second[1])
        aways, attn_proj = sync(aways, attn_proj)
        first_came = swap_expert(aways[0], 1)
        second_came = swap_pair(aways[1])

    backward = attn_backward(
        patches, mod, attn_proj, qkv_all, log_total, cotangent, out_weight,
        [grad_second, near[0], near_came, *far_sum],
    )
    grad_qkv_rows, grad_attn, grad_middle, grad_mod_early = backward
    if fast:
        tail_shapes = [(4 * width, width // 2)] * 2
        tail = weight_grad(
            first_in, grad_qkv_rows, table, tail_plan(width, 0, 3), tail_shapes, [], "grad_qkv"
        )
        tail = weight_grad(
            attended, grad_attn, table, tail_plan(width, 3, 1), tail_shapes, tail, "grad_out"
        )
        tail, third_downs, first_came, second_came, grad_middle = sync(
            tail, third_downs, first_came, second_came, grad_middle
        )
        tail_came = swap_expert(tail[0], 0)
        second = cut([*second[0], second_came], 2)
        first = cut([*first[0], first_came], 2)
        aways = sum_many([[first[1]], [second[1]]])
        aways, grad_middle = sync(aways, grad_middle)
        first_came = swap_pair(aways[0])
        second_came = swap_expert(aways[1], 1)
        tail_came, grad_middle = sync(tail_came, grad_middle)
        tail_base, *away = cut([tail[1], tail_came], 4)
        away = sum_many([[addends] for addends in away])
        away, grad_middle = sync(away, grad_middle)
    inner = input_backward(patches, mod, grad_qkv_rows, grad_middle, qkv_weight)
    if fast:
        away, inner, mix, first_came, second_came = sync(away, inner, mix, first_came, second_came)
        third_cames = swap_plane(away)
        first = cut([*first[0], first_came], LINE)
        second = cut([*second[0], second_came], LINE)
        aways = sum_many([[f, s] for f, s in zip(first[1:], second[1:])])
        own, away = cut(line_last([downs[0]], first_downs, *third_downs), 2)
        away = low(away)
        aways, away, mix, up_first = sync(aways, away, mix, up_first)
        up_second = sum_many([[ups[2]], [[*ups[2], up_first]]])
        up_second, mix = sync(up_second, mix)
        up_cames = line_second(*up_second)
    grad_input, grad_mod_late = inner

    middle = patches.astype(jnp.float32).reshape(latents, seq_len, width) + mod[
        :, 2:3
    ] * attn_proj.reshape(latents, seq_len, width)
    branch = (shared_out + added(mix)).reshape(latents, seq_len, width)
    block_out = (middle + mod[:, 5:6] * branch).reshape(tokens, width).astype(jnp.bfloat16)
    grad_gate_two = jnp.sum(
        cotangent.astype(jnp.float32).reshape(latents, seq_len, width) * branch, axis=1
    )
    local_counts = jnp.sum(
        (routes[:, :, None] == jnp.arange(experts, dtype=jnp.int32)).astype(jnp.int32),
        axis=(0, 1),
    )
    count_parts = jnp.concatenate([local_counts // 128, local_counts % 128]).astype(jnp.bfloat16)
    count_rows = jnp.zeros((latents, 128), jnp.bfloat16).at[0, : 2 * experts].set(count_parts)
    mods = jnp.concatenate(
        [
            grad_mod_late.reshape(latents, 2 * width).astype(jnp.bfloat16),
            grad_mod_early.reshape(latents, 3 * width).astype(jnp.bfloat16),
            grad_gate_two.astype(jnp.bfloat16),
            cond,
            count_rows,
        ],
        axis=1,
    )

    if fast:
        line_cames = line_direct(aways)
        third_cames, mods, block_out, up_cames = sync(third_cames, mods, block_out, up_cames)
        third = cut([*tail_base, *third_cames], LINE)
        tail_aways = sum_many([[addends] for addends in third[1:]])
        up_third = third_parts(ups[1], *up_cames)
        tail_aways, line_cames[0], mods = sync(tail_aways, line_cames[0], mods)
        third_cames = line_direct(tail_aways)
        mods_all = gather_ordered(mods)
        up_cames = line_third(*up_third)
        third_cames, line_cames, away, mods_all = sync(third_cames, line_cames, away, mods_all)
        down_came = swap_pair(away)
        dense_total = low([jnp.concatenate([added(first[0]), added(second[0])]), *line_cames])
        tail_total = low([*third[0], *third_cames])
        totals = jnp.concatenate([dense_total, tail_total], axis=0)
        totals, mods_all = sync(totals, mods_all)
        cames = share_quarters(totals)
        for bit in range(bits_of(dp_size)):
            mods_all = gather_dp_step(mods_all, bit)
        quarters = order_quarters(totals, cames)
        sum_e_up = rows_to_columns(added(line_last(ups[0], up_first, *up_cames)), hidden // width)
        sum_e_down = added([*own, down_came])
        rows = dense_total.shape[0]
        dense_sums = [jnp.concatenate([q[:rows] for q in chips]) for chips in quarters]
        tail_sums = [jnp.concatenate([q[rows:] for q in chips]) for chips in quarters]

        def columns(arrays):
            return jnp.concatenate(arrays, axis=1).astype(jnp.float32)

        half = hidden // 16
        sum_w_up, sum_w_down = [], []
        for chip in range(2):
            at = 2 * half * chip
            sum_w_up.append(
                columns([rows_to_columns(s[at : at + half], hidden // width) for s in dense_sums])
            )
            sum_w_down.append(columns([s[at + half : at + 2 * half] for s in dense_sums]))
        sum_w_up, sum_w_down = jnp.concatenate(sum_w_up), jnp.concatenate(sum_w_down)
        half = width // 16
        sum_w_qkv, sum_w_out = [], []
        for chip in range(2):
            at = 4 * half * chip
            sum_w_qkv.append(
                columns([rows_to_columns(s[at : at + 3 * half], 3) for s in tail_sums])
            )
            sum_w_out.append(columns([s[at + 3 * half : at + 4 * half] for s in tail_sums]))
        sum_w_qkv, sum_w_out = jnp.concatenate(sum_w_qkv), jnp.concatenate(sum_w_out)
    else:
        mods_all = gather_dp(gather_ordered(mods))

        def summed(left, right, axes):
            share = lax.psum_scatter(
                tn(left, right).astype(jnp.bfloat16), "dp", scatter_dimension=0, tiled=True
            )
            return (lax.psum(share, axes) if axes else share).astype(jnp.float32)

        sum_w_up = summed(second_in, grad_shared_pre, "expert")
        sum_w_down = summed(shared_act, grad_shared, "expert")
        sum_w_qkv = summed(first_in, grad_qkv_rows, "expert")
        sum_w_out = summed(attended, grad_attn, "expert")
        sum_e_up = summed(rows_in, grad_pre_rows, None)
        sum_e_down = summed(act_rows, grad_rows, None)

    grad_mod_all = mods_all[:, : 6 * width]
    count_sums = jnp.sum(mods_all[:, 7 * width :].astype(jnp.float32), axis=0).astype(jnp.int32)
    counts = count_sums[:experts] * 128 + count_sums[experts : 2 * experts]
    ada_rows = width // dp_size
    cond_mine = lax.dynamic_slice_in_dim(
        mods_all[:, 6 * width : 7 * width].T, dp_index * ada_rows, ada_rows, axis=0
    )
    sum_ada = jnp.dot(cond_mine, grad_mod_all, preferred_element_type=jnp.float32)
    bias_all = jnp.sum(grad_mod_all.astype(jnp.float32), axis=0)
    bias_size = bias_all.shape[0] // dp_size
    sum_bias = lax.dynamic_slice_in_dim(bias_all, dp_index * bias_size, bias_size)
    return (
        block_out,
        grad_input,
        sum_ada,
        sum_bias,
        sum_w_qkv,
        sum_w_out,
        sum_w_up,
        sum_w_down,
        sum_e_up[None],
        sum_e_down[None],
        counts,
    )


def solution(mesh):
    in_specs = (
        P(("dp", "expert"), None),
        P(("dp", "expert"), None),
        P(),
        P(),
        P(),
        P(),
        P(),
        P(),
        P("expert", None, None),
        P("expert", None, None),
        P(("dp", "expert"), None),
        P(("dp", "expert"), None),
        P(("dp", "expert"), None),
    )
    out_specs = (
        P(("dp", "expert"), None),
        P(("dp", "expert"), None),
        P("dp", None),
        P("dp"),
        P("dp", None),
        P("dp", None),
        P("dp", None),
        P("dp", None),
        P("expert", "dp", None),
        P("expert", "dp", None),
        P(),
    )
    return jax.shard_map(
        on_device, mesh=mesh, in_specs=in_specs, out_specs=out_specs, check_vma=False
    )
```

```python
import functools
import math

import jax
import jax.numpy as jnp
import numpy as np
from jax import lax
from jax.experimental import pallas as pl
from jax.experimental.pallas import tpu as pltpu
from jax.sharding import PartitionSpec as P

HEAD_DIM = 64
VMEM_BYTES = 56 << 20
SHRINK = 1
SQRT_TWO_OVER_PI = math.sqrt(2.0 / math.pi)


def nt(a,b): return lax.dot_general(a,b,(((1,),(1,)),((),())),preferred_element_type=jnp.float32)
def nn(a,b): return lax.dot_general(a,b,(((1,),(0,)),((),())),preferred_element_type=jnp.float32)
def tn(a,b): return lax.dot_general(a,b,(((0,),(0,)),((),())),preferred_element_type=jnp.float32)

def normalized(values_in):
    row_mean = jnp.mean(values_in, axis=-1, keepdims=True)
    centered = values_in - row_mean
    row_var = jnp.mean(centered * centered, axis=-1, keepdims=True)
    inverse = lax.rsqrt(row_var + 1e-06)
    return centered * inverse, inverse

def norm_back(grad_out, scale, normal, inverse):
    inner = grad_out * (1.0 + scale)
    mean_inner = jnp.mean(inner, axis=-1, keepdims=True)
    mean_cross = jnp.mean(inner * normal, axis=-1, keepdims=True)
    return inverse * (inner - mean_inner - normal * mean_cross)

def head_lanes(pair, head):
    lane = lax.broadcasted_iota(jnp.int32, pair.shape, 1)
    return jnp.where(lane // HEAD_DIM == head, pair, jnp.zeros_like(pair))

def attn_forward_kernel(x_ref, mod_ref, wqkv_ref, wout_ref, first_ref, qkv_ref, lse_ref, att_ref, proj_ref, second_ref):
    width = x_ref.shape[1]
    x = x_ref[...].astype(jnp.float32)
    mod = mod_ref[0]
    normal, _ = normalized(x)
    first_ref[...] = (normal * (1.0 + mod[1:2]) + mod[0:1]).astype(jnp.bfloat16)
    qkv_ref[...] = nn(first_ref[...], wqkv_ref[...]).astype(jnp.bfloat16)
    lane = 2 * HEAD_DIM
    for pair in range(width // lane):
        q2 = qkv_ref[:, pair * lane : (pair + 1) * lane]
        k2 = qkv_ref[:, width + pair * lane : width + (pair + 1) * lane]
        v2 = qkv_ref[:, 2 * width + pair * lane : 2 * width + (pair + 1) * lane]
        v2t = v2.T
        outs = []
        for head in range(2):
            scores = nt(head_lanes(k2, head), q2) * HEAD_DIM ** (-0.5)
            peak = jnp.max(scores, axis=0, keepdims=True)
            powers = jnp.exp(scores - peak)
            total = jnp.sum(powers, axis=0, keepdims=True)
            lse_ref[0, 2 * pair + head : 2 * pair + head + 1, :] = peak + jnp.log(total)
            probs = (powers * (1.0 / total)).astype(jnp.bfloat16)
            outs.append(nn(v2t[head * HEAD_DIM : (head + 1) * HEAD_DIM], probs))
        both = jnp.concatenate(outs, axis=0).astype(jnp.bfloat16)
        att_ref[:, pair * lane : (pair + 1) * lane] = both.T
    proj = nn(att_ref[...], wout_ref[...])
    proj_ref[...] = proj
    middle = x + mod[2:3] * proj
    normal2, _ = normalized(middle)
    second_ref[...] = (normal2 * (1.0 + mod[4:5]) + mod[3:4]).astype(jnp.bfloat16)

def attn_forward(patches, mod, wqkv, wout):
    tokens, width = patches.shape
    latents = mod.shape[0]
    seq = tokens // latents
    heads = width // HEAD_DIM
    rows = lambda cols: pl.BlockSpec((seq, cols), lambda i: (i, 0))
    whole = lambda a: pl.BlockSpec(a.shape, lambda i: (0, 0), pipeline_mode=pl.Buffered(1))
    return pl.pallas_call(
        attn_forward_kernel, grid=(latents,),
        in_specs=[rows(width), pl.BlockSpec((1,) + mod.shape[1:], lambda i: (i, 0, 0)), whole(wqkv), whole(wout)],
        out_specs=[rows(width), rows(3 * width), pl.BlockSpec((1, heads, seq), lambda i: (i, 0, 0)), rows(width), rows(width), rows(width)],
        out_shape=[jax.ShapeDtypeStruct((tokens, width), jnp.bfloat16), jax.ShapeDtypeStruct((tokens, 3 * width), jnp.bfloat16),
            jax.ShapeDtypeStruct((latents, heads, seq), jnp.float32), jax.ShapeDtypeStruct((tokens, width), jnp.bfloat16),
            jax.ShapeDtypeStruct((tokens, width), jnp.float32), jax.ShapeDtypeStruct((tokens, width), jnp.bfloat16)],
        compiler_params=pltpu.CompilerParams(vmem_limit_bytes=VMEM_BYTES), cost_estimate=cost(8 * tokens * width * width, 8 * width * width), name="attn_forward")(patches, mod, wqkv, wout)

def attn_backward_kernel(extra, x_ref, mod_ref, proj_ref, qkv_ref, lse_ref, cot_ref, wout_ref, *rest):
    adds = rest[:extra]
    gqkv_ref, gattn_ref, gmid_ref, gmod_ref = rest[extra:]
    width = x_ref.shape[1]
    x = x_ref[...].astype(jnp.float32)
    mod = mod_ref[0]
    proj = proj_ref[...]
    normal, inverse = normalized(x + mod[2:3] * proj)
    grad_second = adds[0][...].astype(jnp.float32)
    for a in adds[1:]:
        grad_second = grad_second + a[...].astype(jnp.float32)
    gmod_ref[0, 1:2, :] = jnp.sum(grad_second, axis=0, keepdims=True)
    gmod_ref[0, 2:3, :] = jnp.sum(grad_second * normal, axis=0, keepdims=True)
    grad_middle = cot_ref[...].astype(jnp.float32) + norm_back(grad_second, mod[4:5], normal, inverse)
    gmid_ref[...] = grad_middle
    gmod_ref[0, 0:1, :] = jnp.sum(grad_middle * proj, axis=0, keepdims=True)
    gattn_ref[...] = (mod[2:3] * grad_middle).astype(jnp.bfloat16)
    grad_att = nt(gattn_ref[...], wout_ref[...]).astype(jnp.bfloat16)
    lane = 2 * HEAD_DIM
    scale = HEAD_DIM ** (-0.5)
    for pair in range(width // lane):
        sl = slice(pair * lane, (pair + 1) * lane)
        q2 = qkv_ref[:, pair * lane : (pair + 1) * lane]
        k2 = qkv_ref[:, width + pair * lane : width + (pair + 1) * lane]
        v2 = qkv_ref[:, 2 * width + pair * lane : 2 * width + (pair + 1) * lane]
        do2 = grad_att[:, sl]
        k2t = k2.T
        gq, gk, gv = [], [], []
        for head in range(2):
            scores = nt(head_lanes(k2, head), q2) * scale
            probs = jnp.exp(scores - lse_ref[0, 2 * pair + head : 2 * pair + head + 1, :])
            grad_probs = nt(head_lanes(v2, head), do2)
            inner = jnp.sum(probs * grad_probs, axis=0, keepdims=True)
            grad_scores = (probs * (grad_probs - inner)).astype(jnp.bfloat16)
            gv.append(nn(probs.astype(jnp.bfloat16), do2))
            gk.append(nn(grad_scores, q2))
            gq.append(nn(k2t[head * HEAD_DIM : (head + 1) * HEAD_DIM], grad_scores))
        low = lax.broadcasted_iota(jnp.int32, gv[0].shape, 1) < HEAD_DIM
        gqt = (jnp.concatenate(gq, axis=0) * scale).astype(jnp.bfloat16)
        gqkv_ref[:, pair * lane : (pair + 1) * lane] = gqt.T
        gqkv_ref[:, width + pair * lane : width + (pair + 1) * lane] = (jnp.where(low, gk[0], gk[1]) * scale).astype(jnp.bfloat16)
        gqkv_ref[:, 2 * width + pair * lane : 2 * width + (pair + 1) * lane] = jnp.where(low, gv[0], gv[1]).astype(jnp.bfloat16)

def attn_backward(patches, mod, proj, qkv, lse, cot, wout, adds):
    tokens, width = patches.shape
    latents = mod.shape[0]
    seq = tokens // latents
    rows = lambda cols: pl.BlockSpec((seq, cols), lambda i: (i, 0))
    per = lambda a: pl.BlockSpec((1,) + a.shape[1:], lambda i: (i, 0, 0))
    whole = lambda a: pl.BlockSpec(a.shape, lambda i: (0, 0), pipeline_mode=pl.Buffered(1))
    return pl.pallas_call(
        functools.partial(attn_backward_kernel, len(adds)), grid=(latents,),
        in_specs=[rows(width), per(mod), rows(width), rows(3 * width), per(lse), rows(width), whole(wout)] + [rows(width)] * len(adds),
        out_specs=[rows(3 * width), rows(width), rows(width), pl.BlockSpec((1, 3, width), lambda i: (i, 0, 0))],
        out_shape=[jax.ShapeDtypeStruct((tokens, 3 * width), jnp.bfloat16), jax.ShapeDtypeStruct((tokens, width), jnp.bfloat16),
            jax.ShapeDtypeStruct((tokens, width), jnp.float32), jax.ShapeDtypeStruct((latents, 3, width), jnp.float32)],
        compiler_params=pltpu.CompilerParams(vmem_limit_bytes=VMEM_BYTES), cost_estimate=cost(8 * tokens * width * width, 8 * width * width), name="attn_backward")(patches, mod, proj, qkv, lse, cot, wout, *adds)

def input_backward_kernel(x_ref, mod_ref, gqkv_ref, gmid_ref, wqkv_ref, gin_ref, gmod_ref):
    mod = mod_ref[0]
    normal, inverse = normalized(x_ref[...].astype(jnp.float32))
    grad_first = nt(gqkv_ref[...], wqkv_ref[...])
    gmod_ref[0, 0:1, :] = jnp.sum(grad_first, axis=0, keepdims=True)
    gmod_ref[0, 1:2, :] = jnp.sum(grad_first * normal, axis=0, keepdims=True)
    gin_ref[...] = gmid_ref[...] + norm_back(grad_first, mod[1:2], normal, inverse)

def input_backward(patches, mod, gqkv, gmid, wqkv):
    tokens, width = patches.shape
    latents = mod.shape[0]
    seq = tokens // latents
    rows = lambda cols: pl.BlockSpec((seq, cols), lambda i: (i, 0))
    per = lambda a: pl.BlockSpec((1,) + a.shape[1:], lambda i: (i, 0, 0))
    whole = lambda a: pl.BlockSpec(a.shape, lambda i: (0, 0), pipeline_mode=pl.Buffered(1))
    return pl.pallas_call(
        input_backward_kernel, grid=(latents,),
        in_specs=[rows(width), per(mod), rows(3 * width), rows(width), whole(wqkv)],
        out_specs=[rows(width), pl.BlockSpec((1, 2, width), lambda i: (i, 0, 0))],
        out_shape=[jax.ShapeDtypeStruct((tokens, width), jnp.float32), jax.ShapeDtypeStruct((latents, 2, width), jnp.float32)],
        compiler_params=pltpu.CompilerParams(vmem_limit_bytes=VMEM_BYTES), cost_estimate=cost(6 * tokens * width * width, 6 * width * width), name="input_backward")(patches, mod, gqkv, gmid, wqkv)


def cost(flops, size):
    return pl.CostEstimate(flops=int(flops) // SHRINK, bytes_accessed=int(size) // SHRINK, transcendentals=0)


def feed_forward_step(x_ref, g_ref, up_ref, down_ref, act_ref, gpre_ref, out_acc, grad_acc):
    inner_scale = SQRT_TWO_OVER_PI
    cubic = 0.044715
    pre = nn(x_ref[...], up_ref[...])
    grad_act = nt(g_ref[...], down_ref[...])
    squared = pre * pre
    bent = jnp.tanh(pre * (inner_scale + (inner_scale * cubic) * squared))
    half = 0.5 + 0.5 * bent
    act = (pre * half).astype(jnp.bfloat16)
    slope = half + (0.5 * pre) * (1.0 - bent * bent) * (
        inner_scale + (3.0 * cubic * inner_scale) * squared
    )
    grad_pre = (grad_act * slope).astype(jnp.bfloat16)
    act_ref[...] = act
    gpre_ref[...] = grad_pre
    out_acc[...] += nn(act, down_ref[...])
    grad_acc[...] += nt(grad_pre, up_ref[...])


def shared_kernel(
    x_ref, cot_ref, gate_ref, up_ref, down_ref,
    act_ref, gpre_ref, g_ref, out_ref, grad_ref,
    out_acc, grad_acc,
):
    step = pl.program_id(0)
    latents = gate_ref.shape[0]
    seq = x_ref.shape[0] // latents

    @pl.when(step == 0)
    def _():
        out_acc[...] = jnp.zeros_like(out_acc)
        grad_acc[...] = jnp.zeros_like(grad_acc)
        for i in range(latents):
            rows = slice(i * seq, (i + 1) * seq)
            g_ref[rows, :] = (gate_ref[i : i + 1, :] * cot_ref[rows, :].astype(jnp.float32)).astype(
                jnp.bfloat16
            )

    feed_forward_step(x_ref, g_ref, up_ref, down_ref, act_ref, gpre_ref, out_acc, grad_acc)

    @pl.when(step == pl.num_programs(0) - 1)
    def _():
        out_ref[...] = out_acc[...]
        grad_ref[...] = grad_acc[...]


def tile_of(width):
    return width // 4 if width % 512 == 0 else width


def still(array):
    return pl.BlockSpec(
        array.shape, lambda j, n=len(array.shape): (0,) * n, pipeline_mode=pl.Buffered(1)
    )


def shared_forward_backward(x, cot, gate, up, down):
    rows, width = x.shape
    hidden = up.shape[1]
    tile = tile_of(hidden)
    out = jax.ShapeDtypeStruct((rows, width), jnp.float32)
    wide = jax.ShapeDtypeStruct((rows, hidden), jnp.bfloat16)
    fixed = pl.BlockSpec((rows, width), lambda j: (0, 0))
    column = pl.BlockSpec((rows, tile), lambda j: (0, j))
    return pl.pallas_call(
        shared_kernel,
        grid=(hidden // tile,),
        in_specs=[
            still(x), still(cot), still(gate),
            pl.BlockSpec((width, tile), lambda j: (0, j)),
            pl.BlockSpec((tile, width), lambda j: (j, 0)),
        ],
        out_specs=[column, column, fixed, fixed, fixed],
        out_shape=[wide, wide, jax.ShapeDtypeStruct((rows, width), jnp.bfloat16), out, out],
        scratch_shapes=[pltpu.VMEM((rows, width), jnp.float32)] * 2,
        compiler_params=pltpu.CompilerParams(vmem_limit_bytes=VMEM_BYTES),
        cost_estimate=cost(8 * rows * width * hidden, 4 * width * hidden + 4 * rows * hidden),
        name="shared_ffn",
    )(x, cot, gate, up, down)


def expert_kernel(blocks, carried, *refs):
    xs, cots = refs[:blocks], refs[blocks : 2 * blocks]
    slot_row, slot_col, gate_col, gate_two, up_ref, down_ref = refs[2 * blocks : 2 * blocks + 6]
    rest = refs[2 * blocks + 6 + carried :]
    act_ref, gpre_ref, x_ref, g_ref = rest[:4]
    mixes, backs = rest[4 : 4 + blocks], rest[4 + blocks : 4 + 2 * blocks]
    out_acc, grad_acc = rest[4 + 2 * blocks :]
    step = pl.program_id(0)
    tokens = xs[0].shape[0]
    capacity = x_ref.shape[0] // blocks
    latents = gate_two.shape[1]
    seq = tokens // latents

    @pl.when(step == 0)
    def _():
        out_acc[...] = jnp.zeros_like(out_acc)
        grad_acc[...] = jnp.zeros_like(grad_acc)
        for b in range(blocks):
            rows = slice(b * capacity, (b + 1) * capacity)
            places = lax.broadcasted_iota(jnp.int32, (capacity, tokens), 0)
            pick = (places == slot_row[b]).astype(jnp.float32).astype(jnp.bfloat16)
            x_ref[rows, :] = nn(pick, xs[b][...]).astype(jnp.bfloat16)
            grads = []
            for i in range(latents):
                part = slice(i * seq, (i + 1) * seq)
                branch = gate_two[b, i : i + 1, :] * cots[b][part, :].astype(jnp.float32)
                grads.append((gate_col[b, part, :] * branch).astype(jnp.bfloat16))
            grad = jnp.concatenate(grads, axis=0)
            g_ref[rows, :] = nn(pick, grad).astype(jnp.bfloat16)

    feed_forward_step(x_ref, g_ref, up_ref, down_ref, act_ref, gpre_ref, out_acc, grad_acc)

    @pl.when(step == pl.num_programs(0) - 1)
    def _():
        for b in range(blocks):
            rows = slice(b * capacity, (b + 1) * capacity)
            places = lax.broadcasted_iota(jnp.int32, (tokens, capacity), 1)
            pick = (places == slot_col[b]).astype(jnp.float32).astype(jnp.bfloat16)
            backs[b][...] = nn(pick, grad_acc[rows, :].astype(jnp.bfloat16)).astype(jnp.bfloat16)
            mixed = nn(pick, out_acc[rows, :].astype(jnp.bfloat16))
            mixes[b][...] = (gate_col[b] * mixed).astype(jnp.bfloat16)


def expert_forward_backward(
    xs, cots, slot_row, slot_col, gate_col, gate_two, up, down, capacity, groups, group, carried
):
    blocks = len(xs)
    tokens, width = xs[0].shape
    hidden = up.shape[1]
    tile = tile_of(hidden)
    rows = blocks * capacity
    wide = jax.ShapeDtypeStruct((rows * groups, hidden), jnp.bfloat16)
    slim = jax.ShapeDtypeStruct((rows * groups, width), jnp.bfloat16)
    mixture = jax.ShapeDtypeStruct((tokens * groups, width), jnp.bfloat16)
    token = jax.ShapeDtypeStruct((tokens, width), jnp.bfloat16)
    column = pl.BlockSpec((rows, tile), lambda j: (group, j))
    own = pl.BlockSpec((rows, width), lambda j: (group, 0))
    mixed = pl.BlockSpec((tokens, width), lambda j: (group, 0))
    fixed = pl.BlockSpec((tokens, width), lambda j: (0, 0))
    small = [slot_row, slot_col, gate_col, gate_two]
    first = 2 * blocks + 6
    return pl.pallas_call(
        functools.partial(expert_kernel, blocks, len(carried)),
        grid=(hidden // tile,),
        in_specs=[still(a) for a in (*xs, *cots)]
        + [
            pl.BlockSpec(
                (blocks,) + a.shape[1:], lambda j, n=len(a.shape) - 1: (group,) + (0,) * n,
                pipeline_mode=pl.Buffered(1),
            )
            for a in small
        ]
        + [
            pl.BlockSpec((width, tile), lambda j: (0, j)),
            pl.BlockSpec((tile, width), lambda j: (j, 0)),
        ]
        + [pl.BlockSpec(memory_space=pl.ANY)] * len(carried),
        out_specs=[column, column, own, own] + [mixed] * blocks + [fixed] * blocks,
        scratch_shapes=[pltpu.VMEM((rows, width), jnp.float32)] * 2,
        out_shape=[wide, wide, slim, slim] + [mixture] * blocks + [token] * blocks,
        input_output_aliases={first + i: i for i in range(len(carried))},
        compiler_params=pltpu.CompilerParams(vmem_limit_bytes=VMEM_BYTES),
        cost_estimate=cost(8 * rows * width * hidden, 4 * width * hidden + 4 * rows * hidden),
        name="expert_ffn",
    )(*xs, *cots, *small, up, down, *carried)


def route_kernel(index_ref, info_ref, time_ref, ada_ref, bias_ref, row_ref, col_ref, gate_ref, two_ref):
    experts, _, tokens = row_ref.shape
    latents = time_ref.shape[0] // experts
    expert = index_ref[0]
    slots, gates = [], []
    before = (
        lax.broadcasted_iota(jnp.int32, (tokens, tokens), 0)
        < lax.broadcasted_iota(jnp.int32, (tokens, tokens), 1)
    ).astype(jnp.float32).astype(jnp.bfloat16)
    for r in range(experts):
        routes = info_ref[r, 0:2, :].astype(jnp.int32)
        named = routes == expert
        member = jnp.sum(named.astype(jnp.float32), axis=0, keepdims=True)
        earlier = nn(member.astype(jnp.bfloat16), before)
        slot = jnp.where(member > 0.5, earlier, float(tokens))
        row_ref[r] = slot.astype(jnp.int32)
        slots.append(slot)
        gates.append(
            jnp.sum(jnp.where(named, info_ref[r, 2:4, :], 0.0), axis=0, keepdims=True)
        )
    turned = jnp.concatenate(slots + gates, axis=0).T
    for r in range(experts):
        col_ref[r] = turned[:, r : r + 1].astype(jnp.int32)
        gate_ref[r] = turned[:, experts + r : experts + r + 1]
    times = time_ref[...]
    cond = (times / (1.0 + jnp.exp(-times))).astype(jnp.bfloat16)
    gate_two = nn(cond, ada_ref[...]) + bias_ref[...]
    for r in range(experts):
        two_ref[r] = gate_two[r * latents : (r + 1) * latents]


def route(expert, info, times, ada_weight, ada_bias, tokens):
    experts = info.shape[0]
    width = times.shape[1]
    latents = times.shape[0] // experts
    vmem = pl.BlockSpec(memory_space=pltpu.VMEM)
    return pl.pallas_call(
        route_kernel,
        grid=(1,),
        in_specs=[
            pl.BlockSpec(memory_space=pltpu.SMEM), still(info), still(times),
            pl.BlockSpec((width, width), lambda j: (0, 5)),
            pl.BlockSpec((1, width), lambda j: (0, 5)),
        ],
        out_specs=[vmem] * 4,
        out_shape=[
            jax.ShapeDtypeStruct((experts, 1, tokens), jnp.int32),
            jax.ShapeDtypeStruct((experts, tokens, 1), jnp.int32),
            jax.ShapeDtypeStruct((experts, tokens, 1), jnp.float32),
            jax.ShapeDtypeStruct((experts, latents, width), jnp.float32),
        ],
        compiler_params=pltpu.CompilerParams(vmem_limit_bytes=VMEM_BYTES),
        name="route",
    )(expert, info, times, ada_weight, ada_bias[None])


def weight_grad_kernel(steps, by_columns, moves, outs, carried, table, a_ref, b_ref, *rest):
    rest = rest[carried:]
    out_refs = rest[:outs]
    sum_ref, sems = rest[outs], rest[outs + 1]
    step = pl.program_id(0)
    if by_columns:
        turned = rest[outs + 2]

        @pl.when(step == 0)
        def _():
            turned[...] = a_ref[...].T

        sum_ref[step] = nn(turned[...], b_ref[...]).astype(jnp.bfloat16)
    else:
        sum_ref[step] = tn(a_ref[...], b_ref[...]).astype(jnp.bfloat16)

    def copies(at):
        for i, (when, out, row, rows, terms, col_from, cols) in enumerate(moves):
            if at is not None and when != at:
                continue
            start = terms[0]
            for entry, scale in terms[1:]:
                start = start + table[entry] * scale
            if len(terms) > 1:
                start = pl.multiple_of(start, 8)
            if isinstance(col_from, tuple):
                chooser, half = col_from
                column = pl.multiple_of(table[chooser] * half, 128)
            else:
                column = col_from
            yield pltpu.make_async_copy(
                sum_ref.at[when, pl.ds(start, rows), pl.ds(column, cols)],
                out_refs[out].at[pl.ds(row, rows), :],
                sems.at[i],
            )

    for at in range(steps):

        @pl.when(step == at)
        def _(at=at):
            for copy in copies(at):
                copy.start()

    @pl.when(step == steps - 1)
    def _():
        for copy in copies(None):
            copy.wait()


def weight_grad(a, b, table, plan, shapes, carried, name):
    tile, by_columns, a_map, b_map, moves = plan
    rows, left = a.shape
    right = b.shape[1]
    if by_columns:
        steps = right // tile
        specs = [
            pl.BlockSpec((rows, left), a_map, pipeline_mode=pl.Buffered(1)),
            pl.BlockSpec((rows, tile), b_map),
        ]
        scratch = [pltpu.VMEM((steps, left, tile), jnp.bfloat16)]
        extra = [pltpu.VMEM((left, rows), jnp.bfloat16)]
    else:
        steps = left // tile
        specs = [
            pl.BlockSpec((rows, tile), a_map),
            pl.BlockSpec((rows, right), b_map, pipeline_mode=pl.Buffered(1)),
        ]
        scratch = [pltpu.VMEM((steps, tile, right), jnp.bfloat16)]
        extra = []
    anywhere = pl.BlockSpec(memory_space=pl.ANY)
    return pl.pallas_call(
        functools.partial(
            weight_grad_kernel, steps, by_columns, moves, len(shapes), len(carried)
        ),
        grid_spec=pltpu.PrefetchScalarGridSpec(
            num_scalar_prefetch=1,
            grid=(steps,),
            in_specs=specs + [anywhere] * len(carried),
            out_specs=[anywhere] * len(shapes),
            scratch_shapes=[*scratch, pltpu.SemaphoreType.DMA((len(moves),)), *extra],
        ),
        out_shape=[jax.ShapeDtypeStruct(s, jnp.bfloat16) for s in shapes],
        input_output_aliases={3 + i: i for i in range(len(carried))},
        compiler_params=pltpu.CompilerParams(vmem_limit_bytes=VMEM_BYTES),
        cost_estimate=cost(2 * rows * left * right, 2 * left * right + 2 * rows * (left + right)),
        name=name,
    )(table, a, b, *carried)


def bits_of(size):
    return size.bit_length() - 1


def label_of(index):
    upper = index >> 1
    return ((upper ^ (upper >> 1)) << 1) | (index & 1)


def index_of(label):
    upper = label >> 1
    shift = 1
    while shift < 32:
        upper = upper ^ (upper >> shift)
        shift *= 2
    return (upper << 1) | (label & 1)


def swap_dp(value, bit):
    size = lax.axis_size("dp")
    return lax.ppermute(
        value, "dp", [(i, index_of(label_of(i) ^ (1 << bit))) for i in range(size)]
    )


def swap_expert(value, bit):
    size = lax.axis_size("expert")
    step = size - 1 if bit is None else 1 << bit
    return lax.ppermute(value, "expert", [(i, i ^ step) for i in range(size)])


def gather_expert(value):
    bits = bits_of(lax.axis_size("expert"))
    parts = {0: value}
    for bit in reversed(range(bits)):
        for r in list(parts):
            parts[r | (1 << bit)] = swap_expert(parts[r], bit)
    return [parts[r] for r in range(1 << bits)]


def gather_ordered(value):
    mine = lax.axis_index("expert")
    for bit in range(bits_of(lax.axis_size("expert"))):
        other = swap_expert(value, bit)
        upper = (mine >> bit & 1) == 1
        value = jnp.concatenate(
            [jnp.where(upper, other, value), jnp.where(upper, value, other)], axis=0
        )
    return value


def gather_expert_stacked(value):
    held, places = value[None], [0]
    for bit in reversed(range(bits_of(lax.axis_size("expert")))):
        held = jnp.concatenate([held, swap_expert(held, bit)])
        places += [place | (1 << bit) for place in places]
    return jnp.concatenate([held[places.index(r)][None] for r in range(len(places))])


def scatter_expert(parts, first_bit=0):
    parts = [[part] for part in parts]
    for bit in range(first_bit, bits_of(lax.axis_size("expert"))):
        left = []
        for kept, away in zip(parts[::2], parts[1::2]):
            away = away[0].astype(jnp.bfloat16) if len(away) == 1 else added(away).astype(jnp.bfloat16)
            kept = kept if len(kept) == 1 else [added(kept).astype(jnp.bfloat16)]
            left.append([*kept, swap_expert(away, bit)])
        parts = left
    return parts[0]


def gather_dp_step(value, bit):
    return jnp.concatenate([value, swap_dp(value, bit)], axis=0)


def gather_dp(value):
    for bit in range(bits_of(lax.axis_size("dp"))):
        value = gather_dp_step(value, bit)
    return value


LINE, PAIR = 4, 2
CORE, CHIP, AHEAD = 8, 10, 12


def tuned(mesh_dp, experts):
    return mesh_dp == LINE * PAIR and experts == 4


def shard_table():
    dp, expert = lax.axis_index("dp"), lax.axis_index("expert")
    relative = jnp.arange(LINE * PAIR, dtype=jnp.int32)
    place, along, across = dp // PAIR, relative // PAIR, dp % PAIR ^ relative % PAIR
    inwards = jnp.where(place < LINE // 2, place + along, place - along + LINE) % LINE
    ahead = (place + along) % LINE
    core, chip = expert & 1, expert >> 1
    return jnp.concatenate(
        [inwards * PAIR + across, jnp.stack([core, 1 - core, chip, 1 - chip]), ahead * PAIR + across]
    ).astype(jnp.int32)


def relatives():
    return [(2 * along + across, along, across) for along in range(LINE) for across in range(PAIR)]


def by_shard(shard, first, moves):
    return (shard, False, lambda j, t: (0, t[first + j]), lambda j, t: (0, 0), moves)


def halves_map(half_steps):
    return lambda j, t: (
        0,
        jnp.where(j < half_steps, t[CORE + 1] * half_steps + j, (t[CORE] - 1) * half_steps + j),
    )


def expert_down_plan(width, hidden):
    shard = hidden // 8
    moves = [
        (relative, along, across * shard, shard, (0,), 0, width)
        for relative, along, across in relatives()
    ]
    return by_shard(shard, 0, moves), [(PAIR * shard, width)] * LINE


def expert_up_plan(width, hidden):
    shard = width // 8
    steps = hidden // width
    moves = [
        (step, across, (along * steps + step) * shard, shard, (0, (relative, shard)), 0, width)
        for step in range(steps)
        for relative, along, across in relatives()
    ]
    plan = (width, True, lambda j, t: (0, 0), lambda j, t: (0, j), moves)
    return plan, [(LINE * steps * shard, width)] * PAIR


def dense_place(chip_first, chip, along, across):
    outer, inner = (chip, across) if chip_first else (across, chip)
    return (2 * outer + inner) * LINE + along


def dense_up_plan(width, hidden):
    cols, shard = width // 2, width // 8
    rows = shard // 2
    unit = rows * (hidden // width)
    half_steps = hidden // width // 2
    moves = []
    for step in range(2 * half_steps):
        for block in range(2):
            column = 2 * (step % half_steps) + block
            for relative, along, across in relatives():
                for chip in range(2):
                    row = dense_place(True, chip, along, across) * unit + column * rows
                    source = (0, (AHEAD + relative, shard), (CHIP + chip, rows))
                    moves.append((step, step // half_steps, row, rows, source, block * cols, cols))
    return (width, True, lambda j, t: (0, 0), halves_map(half_steps), moves)


def dense_down_plan(width, hidden):
    cols = width // 2
    unit = hidden // 8 // 2
    moves = []
    for relative, along, across in relatives():
        for out in range(2):
            for chip in range(2):
                row = (16 + dense_place(False, chip, along, across)) * unit
                source = (0, (CHIP + chip, unit))
                moves.append((relative, out, row, unit, source, (CORE + 1 - out, cols), cols))
    return by_shard(hidden // 8, AHEAD, moves)


def tail_plan(width, first, count):
    cols, shard = width // 2, width // 8
    rows = shard // 2
    moves = []
    for step in range(2):
        for block in range(count):
            for relative, along, across in relatives():
                for chip in range(2):
                    row = (dense_place(True, chip, along, across) * 4 + first + block) * rows
                    source = (0, (AHEAD + relative, shard), (CHIP + chip, rows))
                    moves.append((step, step, row, rows, source, block * cols, cols))
    return (count * cols, True, lambda j, t: (0, 0), halves_map(1), moves)


def low(parts):
    return added(parts).astype(jnp.bfloat16)


class View:
    def __init__(self, array, start, rows):
        self.array, self.start, self.rows = array, start, rows


def view(value):
    return value if isinstance(value, View) else View(value, 0, value.shape[0])


def sum_many(stacks):
    stacks = [[[view(value) for value in addends] for addends in stack] for stack in stacks]
    rows = stacks[0][0][0].rows
    block = 384 if rows % 384 == 0 else 192 if rows % 192 == 0 else 96
    steps = rows // block
    depth = len(stacks[0])
    arrays, specs, shapes = [], [], []
    for stack in stacks:
        width = stack[0][0].array.shape[1]
        shapes.append(jax.ShapeDtypeStruct((depth * rows, width), jnp.bfloat16))
        for level, addends in enumerate(stack):
            for value in addends:
                first = value.start // block
                arrays.append(value.array)
                specs.append(
                    pl.BlockSpec(
                        (block, width),
                        lambda i, f=first, l=level: (f + jnp.clip(i - l * steps, 0, steps - 1), 0),
                    )
                )

    def kernel(*refs):
        outs = refs[len(arrays) :]
        for level in range(depth):

            @pl.when(pl.program_id(0) // steps == level)
            def _(level=level):
                at = 0
                for out, stack in zip(outs, stacks):
                    for here, addends in enumerate(stack):
                        if here == level:
                            total = refs[at][...].astype(jnp.float32)
                            for extra in range(1, len(addends)):
                                total = total + refs[at + extra][...].astype(jnp.float32)
                            out[...] = total.astype(jnp.bfloat16)
                        at += len(addends)

    return pl.pallas_call(
        kernel,
        grid=(depth * steps,),
        in_specs=specs,
        out_specs=[pl.BlockSpec((block, s.shape[1]), lambda i: (i, 0)) for s in shapes],
        out_shape=shapes,
        compiler_params=pltpu.CompilerParams(vmem_limit_bytes=VMEM_BYTES),
        name="sum_many",
    )(*arrays)


def sync(*values):
    return lax.optimization_barrier(values)


def cut(addends, count):
    views = [view(value) for value in addends]
    left = views[0].rows // count
    return [[View(v.array, v.start + i * left, left) for v in views] for i in range(count)]


def swap_pair(value):
    return lax.ppermute(value, "dp", [(i, i ^ 1) for i in range(LINE * PAIR)])


def move_line(value, pairs):
    return lax.ppermute(
        value, "dp", [(a * PAIR + i, b * PAIR + i) for a, b in pairs for i in range(PAIR)]
    )


OUTSIDE = [(0, 1), (1, 0), (2, 3), (3, 2)]


def at_end():
    place = lax.axis_index("dp") // PAIR
    return (place == 0) | (place == LINE - 1)


def line_first(outer):
    return move_line(outer, OUTSIDE)


def move_inside(value):
    experts = lax.axis_size("expert")
    pairs = []
    for place in range(LINE):
        for rest in range(PAIR * experts):
            here = place * PAIR * experts + rest
            there = here ^ 1 if place in (0, LINE - 1) else (LINE - 1 - place) * PAIR * experts + rest
            pairs.append((here, there))
    return lax.ppermute(value, ("dp", "expert"), pairs)


def line_second(outside, inside):
    return move_line(outside, OUTSIDE), move_inside(inside)


def third_parts(inner, outside, inside):
    return jnp.where(at_end(), low(inner), inside), low([*inner, outside])


def line_third(outside, inside):
    return move_line(outside, OUTSIDE), move_inside(inside)


def line_last(own, first, outside, inside):
    return [*own, outside, jnp.where(at_end(), plain(first), inside)]


def line_direct(aways):
    return [
        move_line(away, [(i, (i + ahead) % LINE) for i in range(LINE)])
        for ahead, away in enumerate(aways, 1)
    ]


def swap_both(value, dp_step, expert_step):
    experts = lax.axis_size("expert")
    pairs = [
        (dp * experts + expert, (dp ^ dp_step) * experts + (expert ^ expert_step))
        for dp in range(LINE * PAIR)
        for expert in range(experts)
    ]
    return lax.ppermute(value, ("dp", "expert"), pairs)


def swap_plane(aways):
    return [swap_pair(aways[0]), swap_expert(aways[1], 1), swap_both(aways[2], 1, 2)]


def share_quarters(total):
    return [swap_expert(total, 0), swap_expert(total, 1), swap_expert(total, None)]


def order_quarters(total, cames):
    core, chip, both = cames
    expert = lax.axis_index("expert")
    right, upper = (expert & 1) == 1, (expert >> 1) == 1
    mine = jnp.where(upper, chip, total), jnp.where(upper, total, chip)
    other = jnp.where(upper, both, core), jnp.where(upper, core, both)
    return [
        [jnp.where(right, o, s) for o, s in zip(other, mine)],
        [jnp.where(right, s, o) for o, s in zip(other, mine)],
    ]


def swap_stack(held, bit):
    return jnp.concatenate([held, swap_expert(held, bit)])


def stack_order(held):
    places = [0]
    for bit in reversed(range(bits_of(held.shape[0]))):
        places += [place | (1 << bit) for place in places]
    return jnp.concatenate([held[places.index(r)][None] for r in range(len(places))])


def gather_chips(value):
    parts = {0: value}
    for bit in reversed(range(1, bits_of(lax.axis_size("expert")))):
        for r in list(parts):
            parts[r | (1 << bit)] = swap_expert(parts[r], bit)
    return parts


def rows_to_columns(stacked, count):
    rows = stacked.shape[0] // count
    return jnp.concatenate([stacked[i * rows : (i + 1) * rows] for i in range(count)], axis=1)


def plain(value):
    if isinstance(value, View):
        return value.array[value.start : value.start + value.rows]
    return value


def added(parts):
    total = plain(parts[0]).astype(jnp.float32)
    for part in parts[1:]:
        total = total + plain(part).astype(jnp.float32)
    return total


def scatter_far(parts):
    came = []
    for bit in range(1, bits_of(lax.axis_size("expert"))):
        left = []
        for kept, away in zip(parts[::2], parts[1::2]):
            moved = swap_expert(away, bit)
            if kept is None:
                came.append(moved)
                left.append(None)
            else:
                left.append(added([kept, moved]).astype(jnp.bfloat16))
        parts = left
    return came


def on_device(
    patches,
    time_embed,
    ada_weight,
    ada_bias,
    qkv_weight,
    out_weight,
    up_weight,
    down_weight,
    expert_up,
    expert_down,
    routes,
    gate_weights,
    cotangent,
):
    tokens, width = patches.shape
    latents = time_embed.shape[0]
    seq_len = tokens // latents
    experts = lax.axis_size("expert")
    dp_size = lax.axis_size("dp")
    dp_index = lax.axis_index("dp")
    expert_index = lax.axis_index("expert")
    capacity = 5 * tokens // (2 * experts)

    hidden = up_weight.shape[1]
    blocks = 2
    groups = experts // blocks
    table = shard_table()

    info = jnp.concatenate(
        [
            routes.T.astype(jnp.float32),
            gate_weights.T,
            time_embed.astype(jnp.float32).reshape(-1, tokens),
        ],
        axis=0,
    )
    info = swap_stack(info[None], bits_of(experts) - 1)
    cots = gather_chips(cotangent)
    cots[1] = swap_expert(cotangent, 0)
    for bit in reversed(range(bits_of(experts) - 1)):
        info = swap_stack(info, bit)
    info_all = stack_order(info)
    cond = jax.nn.silu(time_embed.astype(jnp.float32)).astype(jnp.bfloat16)
    modulation = jnp.dot(cond, ada_weight, preferred_element_type=jnp.float32) + ada_bias
    mod = modulation.reshape(latents, 6, width)
    first_in, qkv_all, log_total, attended, attn_proj, second_in = attn_forward(
        patches, mod, qkv_weight, out_weight
    )
    second_in, cots = sync(second_in, cots)

    seconds = gather_chips(second_in)
    seconds[1] = swap_expert(second_in, 0)
    routed = route(
        expert_index[None], info_all[:, :4], info_all[:, 4:].reshape(experts * latents, width),
        ada_weight, ada_bias, tokens,
    )
    routed, seconds[1] = sync(routed, seconds[1])
    for r in range(2, experts, 2):
        cots[r + 1] = swap_expert(cots[r], 0)

    def run_group(group, carried):
        span = range(group * blocks, (group + 1) * blocks)
        results = expert_forward_backward(
            [seconds[r] for r in span], [cots[r] for r in span], *routed, expert_up[0], expert_down[0],
            capacity, groups, group, carried,
        )
        return results[: 4 + blocks], results[4 + blocks :]

    carried, near = run_group(0, [])
    carried, near, seconds, cots = sync(carried, near, seconds, cots)
    for r in range(2, experts, 2):
        seconds[r + 1] = swap_expert(seconds[r], 0)
    near_came = swap_expert(near[1], 0)
    backs = {}
    for group in range(1, groups):
        carried, backs[group] = run_group(group, carried)
    carried, backs, near_came = sync(carried, backs, near_came)
    act_rows, grad_pre_rows, rows_in, grad_rows, mix_even, mix_odd = carried

    fast = tuned(dp_size, experts)
    backs_came = {group: swap_expert(backs[group][1], 0) for group in backs}
    ups, downs, first_downs = (), (), ()
    if fast:
        plan, shapes = expert_down_plan(width, hidden)
        downs = weight_grad(act_rows, grad_rows, table, plan, shapes, [], "grad_expert_down")
    downs, backs_came, rows_in = sync(downs, backs_came, rows_in)
    far = [None] + [low([backs[group][0], backs_came[group]]) for group in range(1, groups)]
    far_sum = scatter_far(far)
    if fast:
        first_downs = line_first(downs[3])
        plan, shapes = expert_up_plan(width, hidden)
        ups = weight_grad(rows_in, grad_pre_rows, table, plan, shapes, [], "grad_expert_up")
    ups, second_in = sync(ups, second_in)

    mix_came = swap_expert(mix_odd, 0)
    if fast:
        up_came = swap_pair(ups[1])
    shared = shared_forward_backward(second_in, cotangent, mod[:, 5], up_weight, down_weight)
    shared, far_sum, mix_came, first_downs = sync(shared, far_sum, mix_came, first_downs)
    shared_act, grad_shared_pre, grad_shared, shared_out, grad_second = shared
    mix = added([mix_even, mix_came])
    mix = scatter_expert([mix[i * tokens : (i + 1) * tokens] for i in range(groups)], 1)
    if fast:
        second_downs = line_second(downs[2], low([downs[2], first_downs]))
        dense_shapes = [(2 * hidden, width // 2)] * 2
        dense = weight_grad(
            second_in, grad_shared_pre, table, dense_up_plan(width, hidden), dense_shapes, [], "grad_up"
        )
        dense = weight_grad(
            shared_act, grad_shared, table, dense_down_plan(width, hidden), dense_shapes, dense,
            "grad_down",
        )
        dense, attn_proj, mix, second_downs, up_came = sync(
            dense, attn_proj, mix, second_downs, up_came
        )
        dense_came = swap_expert(dense[0], 0)
        third = third_parts([downs[1]], *second_downs)
        ups = cut([ups[0], up_came], LINE)
        up_outer = low(ups[3])
        third, up_outer, dense_came, attn_proj = sync(third, up_outer, dense_came, attn_proj)
        third_downs = line_third(*third)
        up_first = line_first(up_outer)
        first, second = cut([dense[1], dense_came], 2)
        first, second = cut(first, 2), cut(second, 2)
        aways = low(first[1]), low(second[1])
        aways, attn_proj = sync(aways, attn_proj)
        first_came = swap_expert(aways[0], 1)
        second_came = swap_pair(aways[1])

    backward = attn_backward(
        patches, mod, attn_proj, qkv_all, log_total, cotangent, out_weight,
        [grad_second, near[0], near_came, *far_sum],
    )
    grad_qkv_rows, grad_attn, grad_middle, grad_mod_early = backward
    if fast:
        tail_shapes = [(4 * width, width // 2)] * 2
        tail = weight_grad(
            first_in, grad_qkv_rows, table, tail_plan(width, 0, 3), tail_shapes, [], "grad_qkv"
        )
        tail = weight_grad(
            attended, grad_attn, table, tail_plan(width, 3, 1), tail_shapes, tail, "grad_out"
        )
        tail, third_downs, first_came, second_came, grad_middle = sync(
            tail, third_downs, first_came, second_came, grad_middle
        )
        tail_came = swap_expert(tail[0], 0)
        second = cut([*second[0], second_came], 2)
        first = cut([*first[0], first_came], 2)
        aways = sum_many([[first[1]], [second[1]]])
        aways, grad_middle = sync(aways, grad_middle)
        first_came = swap_pair(aways[0])
        second_came = swap_expert(aways[1], 1)
        tail_came, grad_middle = sync(tail_came, grad_middle)
        tail_base, *away = cut([tail[1], tail_came], 4)
        away = sum_many([[addends] for addends in away])
        away, grad_middle = sync(away, grad_middle)
    inner = input_backward(patches, mod, grad_qkv_rows, grad_middle, qkv_weight)
    if fast:
        away, inner, mix, first_came, second_came = sync(away, inner, mix, first_came, second_came)
        third_cames = swap_plane(away)
        first = cut([*first[0], first_came], LINE)
        second = cut([*second[0], second_came], LINE)
        aways = sum_many([[f, s] for f, s in zip(first[1:], second[1:])])
        own, away = cut(line_last([downs[0]], first_downs, *third_downs), 2)
        away = low(away)
        aways, away, mix, up_first = sync(aways, away, mix, up_first)
        up_second = sum_many([[ups[2]], [[*ups[2], up_first]]])
        up_second, mix = sync(up_second, mix)
        up_cames = line_second(*up_second)
    grad_input, grad_mod_late = inner

    middle = patches.astype(jnp.float32).reshape(latents, seq_len, width) + mod[
        :, 2:3
    ] * attn_proj.reshape(latents, seq_len, width)
    branch = (shared_out + added(mix)).reshape(latents, seq_len, width)
    block_out = (middle + mod[:, 5:6] * branch).reshape(tokens, width).astype(jnp.bfloat16)
    grad_gate_two = jnp.sum(
        cotangent.astype(jnp.float32).reshape(latents, seq_len, width) * branch, axis=1
    )
    local_counts = jnp.sum(
        (routes[:, :, None] == jnp.arange(experts, dtype=jnp.int32)).astype(jnp.int32),
        axis=(0, 1),
    )
    count_parts = jnp.concatenate([local_counts // 128, local_counts % 128]).astype(jnp.bfloat16)
    count_rows = jnp.zeros((latents, 128), jnp.bfloat16).at[0, : 2 * experts].set(count_parts)
    mods = jnp.concatenate(
        [
            grad_mod_late.reshape(latents, 2 * width).astype(jnp.bfloat16),
            grad_mod_early.reshape(latents, 3 * width).astype(jnp.bfloat16),
            grad_gate_two.astype(jnp.bfloat16),
            cond,
            count_rows,
        ],
        axis=1,
    )

    if fast:
        line_cames = line_direct(aways)
        third_cames, mods, block_out, up_cames = sync(third_cames, mods, block_out, up_cames)
        third = cut([*tail_base, *third_cames], LINE)
        tail_aways = sum_many([[addends] for addends in third[1:]])
        up_third = third_parts(ups[1], *up_cames)
        tail_aways, line_cames[0], mods = sync(tail_aways, line_cames[0], mods)
        third_cames = line_direct(tail_aways)
        mods_all = gather_ordered(mods)
        up_cames = line_third(*up_third)
        third_cames, line_cames, away, mods_all = sync(third_cames, line_cames, away, mods_all)
        down_came = swap_pair(away)
        dense_total = low([jnp.concatenate([added(first[0]), added(second[0])]), *line_cames])
        tail_total = low([*third[0], *third_cames])
        totals = jnp.concatenate([dense_total, tail_total], axis=0)
        totals, mods_all = sync(totals, mods_all)
        cames = share_quarters(totals)
        for bit in range(bits_of(dp_size)):
            mods_all = gather_dp_step(mods_all, bit)
        quarters = order_quarters(totals, cames)
        sum_e_up = rows_to_columns(added(line_last(ups[0], up_first, *up_cames)), hidden // width)
        sum_e_down = added([*own, down_came])
        rows = dense_total.shape[0]
        dense_sums = [jnp.concatenate([q[:rows] for q in chips]) for chips in quarters]
        tail_sums = [jnp.concatenate([q[rows:] for q in chips]) for chips in quarters]

        def columns(arrays):
            return jnp.concatenate(arrays, axis=1).astype(jnp.float32)

        half = hidden // 16
        sum_w_up, sum_w_down = [], []
        for chip in range(2):
            at = 2 * half * chip
            sum_w_up.append(
                columns([rows_to_columns(s[at : at + half], hidden // width) for s in dense_sums])
            )
            sum_w_down.append(columns([s[at + half : at + 2 * half] for s in dense_sums]))
        sum_w_up, sum_w_down = jnp.concatenate(sum_w_up), jnp.concatenate(sum_w_down)
        half = width // 16
        sum_w_qkv, sum_w_out = [], []
        for chip in range(2):
            at = 4 * half * chip
            sum_w_qkv.append(
                columns([rows_to_columns(s[at : at + 3 * half], 3) for s in tail_sums])
            )
            sum_w_out.append(columns([s[at + 3 * half : at + 4 * half] for s in tail_sums]))
        sum_w_qkv, sum_w_out = jnp.concatenate(sum_w_qkv), jnp.concatenate(sum_w_out)
    else:
        mods_all = gather_dp(gather_ordered(mods))

        def summed(left, right, axes):
            share = lax.psum_scatter(
                tn(left, right).astype(jnp.bfloat16), "dp", scatter_dimension=0, tiled=True
            )
            return (lax.psum(share, axes) if axes else share).astype(jnp.float32)

        sum_w_up = summed(second_in, grad_shared_pre, "expert")
        sum_w_down = summed(shared_act, grad_shared, "expert")
        sum_w_qkv = summed(first_in, grad_qkv_rows, "expert")
        sum_w_out = summed(attended, grad_attn, "expert")
        sum_e_up = summed(rows_in, grad_pre_rows, None)
        sum_e_down = summed(act_rows, grad_rows, None)

    grad_mod_all = mods_all[:, : 6 * width]
    count_sums = jnp.sum(mods_all[:, 7 * width :].astype(jnp.float32), axis=0).astype(jnp.int32)
    counts = count_sums[:experts] * 128 + count_sums[experts : 2 * experts]
    ada_rows = width // dp_size
    cond_mine = lax.dynamic_slice_in_dim(
        mods_all[:, 6 * width : 7 * width].T, dp_index * ada_rows, ada_rows, axis=0
    )
    sum_ada = jnp.dot(cond_mine, grad_mod_all, preferred_element_type=jnp.float32)
    bias_all = jnp.sum(grad_mod_all.astype(jnp.float32), axis=0)
    bias_size = bias_all.shape[0] // dp_size
    sum_bias = lax.dynamic_slice_in_dim(bias_all, dp_index * bias_size, bias_size)
    return (
        block_out,
        grad_input,
        sum_ada,
        sum_bias,
        sum_w_qkv,
        sum_w_out,
        sum_w_up,
        sum_w_down,
        sum_e_up[None],
        sum_e_down[None],
        counts,
    )


def solution(mesh):
    in_specs = (
        P(("dp", "expert"), None),
        P(("dp", "expert"), None),
        P(),
        P(),
        P(),
        P(),
        P(),
        P(),
        P("expert", None, None),
        P("expert", None, None),
        P(("dp", "expert"), None),
        P(("dp", "expert"), None),
        P(("dp", "expert"), None),
    )
    out_specs = (
        P(("dp", "expert"), None),
        P(("dp", "expert"), None),
        P("dp", None),
        P("dp"),
        P("dp", None),
        P("dp", None),
        P("dp", None),
        P("dp", None),
        P("expert", "dp", None),
        P("expert", "dp", None),
        P(),
    )
    return jax.shard_map(
        on_device, mesh=mesh, in_specs=in_specs, out_specs=out_specs, check_vma=False
    )
```

```python
import functools
import math

import jax
import jax.numpy as jnp
import numpy as np
from jax import lax
from jax.experimental import pallas as pl
from jax.experimental.pallas import tpu as pltpu
from jax.sharding import PartitionSpec as P

HEAD_DIM = 64
VMEM_BYTES = 56 << 20
SHRINK = 1
SQRT_TWO_OVER_PI = math.sqrt(2.0 / math.pi)


def nt(a,b): return lax.dot_general(a,b,(((1,),(1,)),((),())),preferred_element_type=jnp.float32)
def nn(a,b): return lax.dot_general(a,b,(((1,),(0,)),((),())),preferred_element_type=jnp.float32)
def tn(a,b): return lax.dot_general(a,b,(((0,),(0,)),((),())),preferred_element_type=jnp.float32)

def normalized(values_in):
    row_mean = jnp.mean(values_in, axis=-1, keepdims=True)
    centered = values_in - row_mean
    row_var = jnp.mean(centered * centered, axis=-1, keepdims=True)
    inverse = lax.rsqrt(row_var + 1e-06)
    return centered * inverse, inverse

def norm_back(grad_out, scale, normal, inverse):
    inner = grad_out * (1.0 + scale)
    mean_inner = jnp.mean(inner, axis=-1, keepdims=True)
    mean_cross = jnp.mean(inner * normal, axis=-1, keepdims=True)
    return inverse * (inner - mean_inner - normal * mean_cross)

def head_lanes(pair, head):
    lane = lax.broadcasted_iota(jnp.int32, pair.shape, 1)
    return jnp.where(lane // HEAD_DIM == head, pair, jnp.zeros_like(pair))

def attn_forward_kernel(x_ref, mod_ref, wqkv_ref, wout_ref, first_ref, qkv_ref, lse_ref, att_ref, proj_ref, second_ref):
    width = x_ref.shape[1]
    x = x_ref[...].astype(jnp.float32)
    mod = mod_ref[0]
    normal, _ = normalized(x)
    first_ref[...] = (normal * (1.0 + mod[1:2]) + mod[0:1]).astype(jnp.bfloat16)
    qkv_ref[...] = nn(first_ref[...], wqkv_ref[...]).astype(jnp.bfloat16)
    lane = 2 * HEAD_DIM
    for pair in range(width // lane):
        q2 = qkv_ref[:, pair * lane : (pair + 1) * lane]
        k2 = qkv_ref[:, width + pair * lane : width + (pair + 1) * lane]
        v2 = qkv_ref[:, 2 * width + pair * lane : 2 * width + (pair + 1) * lane]
        v2t = v2.T
        outs = []
        for head in range(2):
            scores = nt(head_lanes(k2, head), q2) * HEAD_DIM ** (-0.5)
            peak = jnp.max(scores, axis=0, keepdims=True)
            powers = jnp.exp(scores - peak)
            total = jnp.sum(powers, axis=0, keepdims=True)
            lse_ref[0, 2 * pair + head : 2 * pair + head + 1, :] = peak + jnp.log(total)
            probs = (powers * (1.0 / total)).astype(jnp.bfloat16)
            outs.append(nn(v2t[head * HEAD_DIM : (head + 1) * HEAD_DIM], probs))
        both = jnp.concatenate(outs, axis=0).astype(jnp.bfloat16)
        att_ref[:, pair * lane : (pair + 1) * lane] = both.T
    proj = nn(att_ref[...], wout_ref[...])
    proj_ref[...] = proj
    middle = x + mod[2:3] * proj
    normal2, _ = normalized(middle)
    second_ref[...] = (normal2 * (1.0 + mod[4:5]) + mod[3:4]).astype(jnp.bfloat16)

def attn_forward(patches, mod, wqkv, wout):
    tokens, width = patches.shape
    latents = mod.shape[0]
    seq = tokens // latents
    heads = width // HEAD_DIM
    rows = lambda cols: pl.BlockSpec((seq, cols), lambda i: (i, 0))
    whole = lambda a: pl.BlockSpec(a.shape, lambda i: (0, 0), pipeline_mode=pl.Buffered(1))
    return pl.pallas_call(
        attn_forward_kernel, grid=(latents,),
        in_specs=[rows(width), pl.BlockSpec((1,) + mod.shape[1:], lambda i: (i, 0, 0)), whole(wqkv), whole(wout)],
        out_specs=[rows(width), rows(3 * width), pl.BlockSpec((1, heads, seq), lambda i: (i, 0, 0)), rows(width), rows(width), rows(width)],
        out_shape=[jax.ShapeDtypeStruct((tokens, width), jnp.bfloat16), jax.ShapeDtypeStruct((tokens, 3 * width), jnp.bfloat16),
            jax.ShapeDtypeStruct((latents, heads, seq), jnp.float32), jax.ShapeDtypeStruct((tokens, width), jnp.bfloat16),
            jax.ShapeDtypeStruct((tokens, width), jnp.float32), jax.ShapeDtypeStruct((tokens, width), jnp.bfloat16)],
        compiler_params=pltpu.CompilerParams(vmem_limit_bytes=VMEM_BYTES), cost_estimate=cost(8 * tokens * width * width, 8 * width * width), name="attn_forward")(patches, mod, wqkv, wout)

def attn_backward_kernel(extra, x_ref, mod_ref, proj_ref, qkv_ref, lse_ref, cot_ref, wout_ref, *rest):
    adds = rest[:extra]
    gqkv_ref, gattn_ref, gmid_ref, gmod_ref = rest[extra:]
    width = x_ref.shape[1]
    x = x_ref[...].astype(jnp.float32)
    mod = mod_ref[0]
    proj = proj_ref[...]
    normal, inverse = normalized(x + mod[2:3] * proj)
    grad_second = adds[0][...].astype(jnp.float32)
    for a in adds[1:]:
        grad_second = grad_second + a[...].astype(jnp.float32)
    gmod_ref[0, 1:2, :] = jnp.sum(grad_second, axis=0, keepdims=True)
    gmod_ref[0, 2:3, :] = jnp.sum(grad_second * normal, axis=0, keepdims=True)
    grad_middle = cot_ref[...].astype(jnp.float32) + norm_back(grad_second, mod[4:5], normal, inverse)
    gmid_ref[...] = grad_middle
    gmod_ref[0, 0:1, :] = jnp.sum(grad_middle * proj, axis=0, keepdims=True)
    gattn_ref[...] = (mod[2:3] * grad_middle).astype(jnp.bfloat16)
    grad_att = nt(gattn_ref[...], wout_ref[...]).astype(jnp.bfloat16)
    lane = 2 * HEAD_DIM
    scale = HEAD_DIM ** (-0.5)
    for pair in range(width // lane):
        sl = slice(pair * lane, (pair + 1) * lane)
        q2 = qkv_ref[:, pair * lane : (pair + 1) * lane]
        k2 = qkv_ref[:, width + pair * lane : width + (pair + 1) * lane]
        v2 = qkv_ref[:, 2 * width + pair * lane : 2 * width + (pair + 1) * lane]
        do2 = grad_att[:, sl]
        k2t = k2.T
        gq, gk, gv = [], [], []
        for head in range(2):
            scores = nt(head_lanes(k2, head), q2) * scale
            probs = jnp.exp(scores - lse_ref[0, 2 * pair + head : 2 * pair + head + 1, :])
            grad_probs = nt(head_lanes(v2, head), do2)
            inner = jnp.sum(probs * grad_probs, axis=0, keepdims=True)
            grad_scores = (probs * (grad_probs - inner)).astype(jnp.bfloat16)
            gv.append(nn(probs.astype(jnp.bfloat16), do2))
            gk.append(nn(grad_scores, q2))
            gq.append(nn(k2t[head * HEAD_DIM : (head + 1) * HEAD_DIM], grad_scores))
        low = lax.broadcasted_iota(jnp.int32, gv[0].shape, 1) < HEAD_DIM
        gqt = (jnp.concatenate(gq, axis=0) * scale).astype(jnp.bfloat16)
        gqkv_ref[:, pair * lane : (pair + 1) * lane] = gqt.T
        gqkv_ref[:, width + pair * lane : width + (pair + 1) * lane] = (jnp.where(low, gk[0], gk[1]) * scale).astype(jnp.bfloat16)
        gqkv_ref[:, 2 * width + pair * lane : 2 * width + (pair + 1) * lane] = jnp.where(low, gv[0], gv[1]).astype(jnp.bfloat16)

def attn_backward(patches, mod, proj, qkv, lse, cot, wout, adds):
    tokens, width = patches.shape
    latents = mod.shape[0]
    seq = tokens // latents
    rows = lambda cols: pl.BlockSpec((seq, cols), lambda i: (i, 0))
    per = lambda a: pl.BlockSpec((1,) + a.shape[1:], lambda i: (i, 0, 0))
    whole = lambda a: pl.BlockSpec(a.shape, lambda i: (0, 0), pipeline_mode=pl.Buffered(1))
    return pl.pallas_call(
        functools.partial(attn_backward_kernel, len(adds)), grid=(latents,),
        in_specs=[rows(width), per(mod), rows(width), rows(3 * width), per(lse), rows(width), whole(wout)] + [rows(width)] * len(adds),
        out_specs=[rows(3 * width), rows(width), rows(width), pl.BlockSpec((1, 3, width), lambda i: (i, 0, 0))],
        out_shape=[jax.ShapeDtypeStruct((tokens, 3 * width), jnp.bfloat16), jax.ShapeDtypeStruct((tokens, width), jnp.bfloat16),
            jax.ShapeDtypeStruct((tokens, width), jnp.float32), jax.ShapeDtypeStruct((latents, 3, width), jnp.float32)],
        compiler_params=pltpu.CompilerParams(vmem_limit_bytes=VMEM_BYTES), cost_estimate=cost(8 * tokens * width * width, 8 * width * width), name="attn_backward")(patches, mod, proj, qkv, lse, cot, wout, *adds)

def input_backward_kernel(x_ref, mod_ref, gqkv_ref, gmid_ref, wqkv_ref, gin_ref, gmod_ref):
    mod = mod_ref[0]
    normal, inverse = normalized(x_ref[...].astype(jnp.float32))
    grad_first = nt(gqkv_ref[...], wqkv_ref[...])
    gmod_ref[0, 0:1, :] = jnp.sum(grad_first, axis=0, keepdims=True)
    gmod_ref[0, 1:2, :] = jnp.sum(grad_first * normal, axis=0, keepdims=True)
    gin_ref[...] = gmid_ref[...] + norm_back(grad_first, mod[1:2], normal, inverse)

def input_backward(patches, mod, gqkv, gmid, wqkv):
    tokens, width = patches.shape
    latents = mod.shape[0]
    seq = tokens // latents
    rows = lambda cols: pl.BlockSpec((seq, cols), lambda i: (i, 0))
    per = lambda a: pl.BlockSpec((1,) + a.shape[1:], lambda i: (i, 0, 0))
    whole = lambda a: pl.BlockSpec(a.shape, lambda i: (0, 0), pipeline_mode=pl.Buffered(1))
    return pl.pallas_call(
        input_backward_kernel, grid=(latents,),
        in_specs=[rows(width), per(mod), rows(3 * width), rows(width), whole(wqkv)],
        out_specs=[rows(width), pl.BlockSpec((1, 2, width), lambda i: (i, 0, 0))],
        out_shape=[jax.ShapeDtypeStruct((tokens, width), jnp.float32), jax.ShapeDtypeStruct((latents, 2, width), jnp.float32)],
        compiler_params=pltpu.CompilerParams(vmem_limit_bytes=VMEM_BYTES), cost_estimate=cost(6 * tokens * width * width, 6 * width * width), name="input_backward")(patches, mod, gqkv, gmid, wqkv)


def cost(flops, size):
    return pl.CostEstimate(flops=int(flops) // SHRINK, bytes_accessed=int(size) // SHRINK, transcendentals=0)


def feed_forward_step(x_ref, g_ref, up_ref, down_ref, act_ref, gpre_ref, out_acc, grad_acc):
    inner_scale = SQRT_TWO_OVER_PI
    cubic = 0.044715
    pre = nn(x_ref[...], up_ref[...])
    grad_act = nt(g_ref[...], down_ref[...])
    squared = pre * pre
    bent = jnp.tanh(pre * (inner_scale + (inner_scale * cubic) * squared))
    half = 0.5 + 0.5 * bent
    act = (pre * half).astype(jnp.bfloat16)
    slope = half + (0.5 * pre) * (1.0 - bent * bent) * (
        inner_scale + (3.0 * cubic * inner_scale) * squared
    )
    grad_pre = (grad_act * slope).astype(jnp.bfloat16)
    act_ref[...] = act
    gpre_ref[...] = grad_pre
    out_acc[...] += nn(act, down_ref[...])
    grad_acc[...] += nt(grad_pre, up_ref[...])


def shared_kernel(
    x_ref, cot_ref, gate_ref, up_ref, down_ref,
    act_ref, gpre_ref, g_ref, out_ref, grad_ref,
    out_acc, grad_acc,
):
    step = pl.program_id(0)
    latents = gate_ref.shape[0]
    seq = x_ref.shape[0] // latents

    @pl.when(step == 0)
    def _():
        out_acc[...] = jnp.zeros_like(out_acc)
        grad_acc[...] = jnp.zeros_like(grad_acc)
        for i in range(latents):
            rows = slice(i * seq, (i + 1) * seq)
            g_ref[rows, :] = (gate_ref[i : i + 1, :] * cot_ref[rows, :].astype(jnp.float32)).astype(
                jnp.bfloat16
            )

    feed_forward_step(x_ref, g_ref, up_ref, down_ref, act_ref, gpre_ref, out_acc, grad_acc)

    @pl.when(step == pl.num_programs(0) - 1)
    def _():
        out_ref[...] = out_acc[...]
        grad_ref[...] = grad_acc[...]


def tile_of(width):
    return width // 4 if width % 512 == 0 else width


def still(array):
    return pl.BlockSpec(
        array.shape, lambda j, n=len(array.shape): (0,) * n, pipeline_mode=pl.Buffered(1)
    )


def shared_forward_backward(x, cot, gate, up, down):
    rows, width = x.shape
    hidden = up.shape[1]
    tile = tile_of(hidden)
    out = jax.ShapeDtypeStruct((rows, width), jnp.float32)
    wide = jax.ShapeDtypeStruct((rows, hidden), jnp.bfloat16)
    fixed = pl.BlockSpec((rows, width), lambda j: (0, 0))
    column = pl.BlockSpec((rows, tile), lambda j: (0, j))
    return pl.pallas_call(
        shared_kernel,
        grid=(hidden // tile,),
        in_specs=[
            still(x), still(cot), still(gate),
            pl.BlockSpec((width, tile), lambda j: (0, j)),
            pl.BlockSpec((tile, width), lambda j: (j, 0)),
        ],
        out_specs=[column, column, fixed, fixed, fixed],
        out_shape=[wide, wide, jax.ShapeDtypeStruct((rows, width), jnp.bfloat16), out, out],
        scratch_shapes=[pltpu.VMEM((rows, width), jnp.float32)] * 2,
        compiler_params=pltpu.CompilerParams(vmem_limit_bytes=VMEM_BYTES),
        cost_estimate=cost(8 * rows * width * hidden, 4 * width * hidden + 4 * rows * hidden),
        name="shared_ffn",
    )(x, cot, gate, up, down)


def expert_kernel(blocks, carried, *refs):
    xs, cots = refs[:blocks], refs[blocks : 2 * blocks]
    slot_row, slot_col, gate_col, gate_two, up_ref, down_ref = refs[2 * blocks : 2 * blocks + 6]
    rest = refs[2 * blocks + 6 + carried :]
    act_ref, gpre_ref, x_ref, g_ref = rest[:4]
    mixes, backs = rest[4 : 4 + blocks], rest[4 + blocks : 4 + 2 * blocks]
    out_acc, grad_acc = rest[4 + 2 * blocks :]
    step = pl.program_id(0)
    tokens = xs[0].shape[0]
    capacity = x_ref.shape[0] // blocks
    latents = gate_two.shape[1]
    seq = tokens // latents

    @pl.when(step == 0)
    def _():
        out_acc[...] = jnp.zeros_like(out_acc)
        grad_acc[...] = jnp.zeros_like(grad_acc)
        for b in range(blocks):
            rows = slice(b * capacity, (b + 1) * capacity)
            places = lax.broadcasted_iota(jnp.int32, (capacity, tokens), 0)
            pick = (places == slot_row[b]).astype(jnp.float32).astype(jnp.bfloat16)
            x_ref[rows, :] = nn(pick, xs[b][...]).astype(jnp.bfloat16)
            grads = []
            for i in range(latents):
                part = slice(i * seq, (i + 1) * seq)
                branch = gate_two[b, i : i + 1, :] * cots[b][part, :].astype(jnp.float32)
                grads.append((gate_col[b, part, :] * branch).astype(jnp.bfloat16))
            grad = jnp.concatenate(grads, axis=0)
            g_ref[rows, :] = nn(pick, grad).astype(jnp.bfloat16)

    feed_forward_step(x_ref, g_ref, up_ref, down_ref, act_ref, gpre_ref, out_acc, grad_acc)

    @pl.when(step == pl.num_programs(0) - 1)
    def _():
        for b in range(blocks):
            rows = slice(b * capacity, (b + 1) * capacity)
            places = lax.broadcasted_iota(jnp.int32, (tokens, capacity), 1)
            pick = (places == slot_col[b]).astype(jnp.float32).astype(jnp.bfloat16)
            backs[b][...] = nn(pick, grad_acc[rows, :].astype(jnp.bfloat16)).astype(jnp.bfloat16)
            mixed = nn(pick, out_acc[rows, :].astype(jnp.bfloat16))
            mixes[b][...] = (gate_col[b] * mixed).astype(jnp.bfloat16)


def expert_forward_backward(
    xs, cots, slot_row, slot_col, gate_col, gate_two, up, down, capacity, groups, group, carried
):
    blocks = len(xs)
    tokens, width = xs[0].shape
    hidden = up.shape[1]
    tile = tile_of(hidden)
    rows = blocks * capacity
    wide = jax.ShapeDtypeStruct((rows * groups, hidden), jnp.bfloat16)
    slim = jax.ShapeDtypeStruct((rows * groups, width), jnp.bfloat16)
    mixture = jax.ShapeDtypeStruct((tokens * groups, width), jnp.bfloat16)
    token = jax.ShapeDtypeStruct((tokens, width), jnp.bfloat16)
    column = pl.BlockSpec((rows, tile), lambda j: (group, j))
    own = pl.BlockSpec((rows, width), lambda j: (group, 0))
    mixed = pl.BlockSpec((tokens, width), lambda j: (group, 0))
    fixed = pl.BlockSpec((tokens, width), lambda j: (0, 0))
    small = [slot_row, slot_col, gate_col, gate_two]
    first = 2 * blocks + 6
    return pl.pallas_call(
        functools.partial(expert_kernel, blocks, len(carried)),
        grid=(hidden // tile,),
        in_specs=[still(a) for a in (*xs, *cots)]
        + [
            pl.BlockSpec(
                (blocks,) + a.shape[1:], lambda j, n=len(a.shape) - 1: (group,) + (0,) * n,
                pipeline_mode=pl.Buffered(1),
            )
            for a in small
        ]
        + [
            pl.BlockSpec((width, tile), lambda j: (0, j)),
            pl.BlockSpec((tile, width), lambda j: (j, 0)),
        ]
        + [pl.BlockSpec(memory_space=pl.ANY)] * len(carried),
        out_specs=[column, column, own, own] + [mixed] * blocks + [fixed] * blocks,
        scratch_shapes=[pltpu.VMEM((rows, width), jnp.float32)] * 2,
        out_shape=[wide, wide, slim, slim] + [mixture] * blocks + [token] * blocks,
        input_output_aliases={first + i: i for i in range(len(carried))},
        compiler_params=pltpu.CompilerParams(vmem_limit_bytes=VMEM_BYTES),
        cost_estimate=cost(8 * rows * width * hidden, 4 * width * hidden + 4 * rows * hidden),
        name="expert_ffn",
    )(*xs, *cots, *small, up, down, *carried)


def route_kernel(index_ref, info_ref, time_ref, ada_ref, bias_ref, row_ref, col_ref, gate_ref, two_ref):
    experts, _, tokens = row_ref.shape
    latents = time_ref.shape[0] // experts
    expert = index_ref[0]
    slots, gates = [], []
    before = (
        lax.broadcasted_iota(jnp.int32, (tokens, tokens), 0)
        < lax.broadcasted_iota(jnp.int32, (tokens, tokens), 1)
    ).astype(jnp.float32).astype(jnp.bfloat16)
    for r in range(experts):
        routes = info_ref[r, 0:2, :].astype(jnp.int32)
        named = routes == expert
        member = jnp.sum(named.astype(jnp.float32), axis=0, keepdims=True)
        earlier = nn(member.astype(jnp.bfloat16), before)
        slot = jnp.where(member > 0.5, earlier, float(tokens))
        row_ref[r] = slot.astype(jnp.int32)
        slots.append(slot)
        gates.append(
            jnp.sum(jnp.where(named, info_ref[r, 2:4, :], 0.0), axis=0, keepdims=True)
        )
    turned = jnp.concatenate(slots + gates, axis=0).T
    for r in range(experts):
        col_ref[r] = turned[:, r : r + 1].astype(jnp.int32)
        gate_ref[r] = turned[:, experts + r : experts + r + 1]
    times = time_ref[...]
    cond = (times / (1.0 + jnp.exp(-times))).astype(jnp.bfloat16)
    gate_two = nn(cond, ada_ref[...]) + bias_ref[...]
    for r in range(experts):
        two_ref[r] = gate_two[r * latents : (r + 1) * latents]


def route(expert, info, times, ada_weight, ada_bias, tokens):
    experts = info.shape[0]
    width = times.shape[1]
    latents = times.shape[0] // experts
    vmem = pl.BlockSpec(memory_space=pltpu.VMEM)
    return pl.pallas_call(
        route_kernel,
        grid=(1,),
        in_specs=[
            pl.BlockSpec(memory_space=pltpu.SMEM), still(info), still(times),
            pl.BlockSpec((width, width), lambda j: (0, 5)),
            pl.BlockSpec((1, width), lambda j: (0, 5)),
        ],
        out_specs=[vmem] * 4,
        out_shape=[
            jax.ShapeDtypeStruct((experts, 1, tokens), jnp.int32),
            jax.ShapeDtypeStruct((experts, tokens, 1), jnp.int32),
            jax.ShapeDtypeStruct((experts, tokens, 1), jnp.float32),
            jax.ShapeDtypeStruct((experts, latents, width), jnp.float32),
        ],
        compiler_params=pltpu.CompilerParams(vmem_limit_bytes=VMEM_BYTES),
        name="route",
    )(expert, info, times, ada_weight, ada_bias[None])


def weight_grad_kernel(steps, by_columns, moves, outs, carried, table, a_ref, b_ref, *rest):
    rest = rest[carried:]
    out_refs = rest[:outs]
    sum_ref, sems = rest[outs], rest[outs + 1]
    step = pl.program_id(0)
    if by_columns:
        turned = rest[outs + 2]

        @pl.when(step == 0)
        def _():
            turned[...] = a_ref[...].T

        sum_ref[step] = nn(turned[...], b_ref[...]).astype(jnp.bfloat16)
    else:
        sum_ref[step] = tn(a_ref[...], b_ref[...]).astype(jnp.bfloat16)

    def copies(at):
        for i, (when, out, row, rows, terms, col_from, cols) in enumerate(moves):
            if at is not None and when != at:
                continue
            start = terms[0]
            for entry, scale in terms[1:]:
                start = start + table[entry] * scale
            if len(terms) > 1:
                start = pl.multiple_of(start, 8)
            if isinstance(col_from, tuple):
                chooser, half = col_from
                column = pl.multiple_of(table[chooser] * half, 128)
            else:
                column = col_from
            yield pltpu.make_async_copy(
                sum_ref.at[when, pl.ds(start, rows), pl.ds(column, cols)],
                out_refs[out].at[pl.ds(row, rows), :],
                sems.at[i],
            )

    for at in range(steps):

        @pl.when(step == at)
        def _(at=at):
            for copy in copies(at):
                copy.start()

    @pl.when(step == steps - 1)
    def _():
        for copy in copies(None):
            copy.wait()


def weight_grad(a, b, table, plan, shapes, carried, name):
    tile, by_columns, a_map, b_map, moves = plan
    rows, left = a.shape
    right = b.shape[1]
    if by_columns:
        steps = right // tile
        specs = [
            pl.BlockSpec((rows, left), a_map, pipeline_mode=pl.Buffered(1)),
            pl.BlockSpec((rows, tile), b_map),
        ]
        scratch = [pltpu.VMEM((steps, left, tile), jnp.bfloat16)]
        extra = [pltpu.VMEM((left, rows), jnp.bfloat16)]
    else:
        steps = left // tile
        specs = [
            pl.BlockSpec((rows, tile), a_map),
            pl.BlockSpec((rows, right), b_map, pipeline_mode=pl.Buffered(1)),
        ]
        scratch = [pltpu.VMEM((steps, tile, right), jnp.bfloat16)]
        extra = []
    anywhere = pl.BlockSpec(memory_space=pl.ANY)
    return pl.pallas_call(
        functools.partial(
            weight_grad_kernel, steps, by_columns, moves, len(shapes), len(carried)
        ),
        grid_spec=pltpu.PrefetchScalarGridSpec(
            num_scalar_prefetch=1,
            grid=(steps,),
            in_specs=specs + [anywhere] * len(carried),
            out_specs=[anywhere] * len(shapes),
            scratch_shapes=[*scratch, pltpu.SemaphoreType.DMA((len(moves),)), *extra],
        ),
        out_shape=[jax.ShapeDtypeStruct(s, jnp.bfloat16) for s in shapes],
        input_output_aliases={3 + i: i for i in range(len(carried))},
        compiler_params=pltpu.CompilerParams(vmem_limit_bytes=VMEM_BYTES),
        cost_estimate=cost(2 * rows * left * right, 2 * left * right + 2 * rows * (left + right)),
        name=name,
    )(table, a, b, *carried)


def bits_of(size):
    return size.bit_length() - 1


def label_of(index):
    upper = index >> 1
    return ((upper ^ (upper >> 1)) << 1) | (index & 1)


def index_of(label):
    upper = label >> 1
    shift = 1
    while shift < 32:
        upper = upper ^ (upper >> shift)
        shift *= 2
    return (upper << 1) | (label & 1)


def swap_dp(value, bit):
    size = lax.axis_size("dp")
    return lax.ppermute(
        value, "dp", [(i, index_of(label_of(i) ^ (1 << bit))) for i in range(size)]
    )


def swap_expert(value, bit):
    size = lax.axis_size("expert")
    step = size - 1 if bit is None else 1 << bit
    return lax.ppermute(value, "expert", [(i, i ^ step) for i in range(size)])


def gather_expert(value):
    bits = bits_of(lax.axis_size("expert"))
    parts = {0: value}
    for bit in reversed(range(bits)):
        for r in list(parts):
            parts[r | (1 << bit)] = swap_expert(parts[r], bit)
    return [parts[r] for r in range(1 << bits)]


def gather_ordered(value):
    mine = lax.axis_index("expert")
    for bit in range(bits_of(lax.axis_size("expert"))):
        other = swap_expert(value, bit)
        upper = (mine >> bit & 1) == 1
        value = jnp.concatenate(
            [jnp.where(upper, other, value), jnp.where(upper, value, other)], axis=0
        )
    return value


def gather_expert_stacked(value):
    held, places = value[None], [0]
    for bit in reversed(range(bits_of(lax.axis_size("expert")))):
        held = jnp.concatenate([held, swap_expert(held, bit)])
        places += [place | (1 << bit) for place in places]
    return jnp.concatenate([held[places.index(r)][None] for r in range(len(places))])


def scatter_expert(parts, first_bit=0):
    parts = [[part] for part in parts]
    for bit in range(first_bit, bits_of(lax.axis_size("expert"))):
        left = []
        for kept, away in zip(parts[::2], parts[1::2]):
            away = away[0].astype(jnp.bfloat16) if len(away) == 1 else added(away).astype(jnp.bfloat16)
            kept = kept if len(kept) == 1 else [added(kept).astype(jnp.bfloat16)]
            left.append([*kept, swap_expert(away, bit)])
        parts = left
    return parts[0]


def gather_dp_step(value, bit):
    return jnp.concatenate([value, swap_dp(value, bit)], axis=0)


def gather_dp(value):
    for bit in range(bits_of(lax.axis_size("dp"))):
        value = gather_dp_step(value, bit)
    return value


LINE, PAIR = 4, 2
CORE, CHIP, AHEAD = 8, 10, 12


def tuned(mesh_dp, experts):
    return mesh_dp == LINE * PAIR and experts == 4


def shard_table():
    dp, expert = lax.axis_index("dp"), lax.axis_index("expert")
    relative = jnp.arange(LINE * PAIR, dtype=jnp.int32)
    place, along, across = dp // PAIR, relative // PAIR, dp % PAIR ^ relative % PAIR
    inwards = jnp.where(place < LINE // 2, place + along, place - along + LINE) % LINE
    ahead = (place + along) % LINE
    core, chip = expert & 1, expert >> 1
    return jnp.concatenate(
        [inwards * PAIR + across, jnp.stack([core, 1 - core, chip, 1 - chip]), ahead * PAIR + across]
    ).astype(jnp.int32)


def relatives():
    return [(2 * along + across, along, across) for along in range(LINE) for across in range(PAIR)]


def by_shard(shard, first, moves):
    return (shard, False, lambda j, t: (0, t[first + j]), lambda j, t: (0, 0), moves)


def halves_map(half_steps):
    return lambda j, t: (
        0,
        jnp.where(j < half_steps, t[CORE + 1] * half_steps + j, (t[CORE] - 1) * half_steps + j),
    )


def expert_down_plan(width, hidden):
    shard = hidden // 8
    moves = [
        (relative, along, across * shard, shard, (0,), 0, width)
        for relative, along, across in relatives()
    ]
    return by_shard(shard, 0, moves), [(PAIR * shard, width)] * LINE


def expert_up_plan(width, hidden):
    shard = width // 8
    steps = hidden // width
    moves = [
        (step, across, (along * steps + step) * shard, shard, (0, (relative, shard)), 0, width)
        for step in range(steps)
        for relative, along, across in relatives()
    ]
    plan = (width, True, lambda j, t: (0, 0), lambda j, t: (0, j), moves)
    return plan, [(LINE * steps * shard, width)] * PAIR


def dense_place(chip_first, chip, along, across):
    outer, inner = (chip, across) if chip_first else (across, chip)
    return (2 * outer + inner) * LINE + along


def dense_up_plan(width, hidden):
    cols, shard = width // 2, width // 8
    rows = shard // 2
    unit = rows * (hidden // width)
    half_steps = hidden // width // 2
    moves = []
    for step in range(2 * half_steps):
        for block in range(2):
            column = 2 * (step % half_steps) + block
            for relative, along, across in relatives():
                for chip in range(2):
                    row = dense_place(True, chip, along, across) * unit + column * rows
                    source = (0, (AHEAD + relative, shard), (CHIP + chip, rows))
                    moves.append((step, step // half_steps, row, rows, source, block * cols, cols))
    return (width, True, lambda j, t: (0, 0), halves_map(half_steps), moves)


def dense_down_plan(width, hidden):
    cols = width // 2
    unit = hidden // 8 // 2
    moves = []
    for relative, along, across in relatives():
        for out in range(2):
            for chip in range(2):
                row = (16 + dense_place(False, chip, along, across)) * unit
                source = (0, (CHIP + chip, unit))
                moves.append((relative, out, row, unit, source, (CORE + 1 - out, cols), cols))
    return by_shard(hidden // 8, AHEAD, moves)


def tail_plan(width, first, count):
    cols, shard = width // 2, width // 8
    rows = shard // 2
    moves = []
    for step in range(2):
        for block in range(count):
            for relative, along, across in relatives():
                for chip in range(2):
                    row = (dense_place(True, chip, along, across) * 4 + first + block) * rows
                    source = (0, (AHEAD + relative, shard), (CHIP + chip, rows))
                    moves.append((step, step, row, rows, source, block * cols, cols))
    return (count * cols, True, lambda j, t: (0, 0), halves_map(1), moves)


def low(parts):
    return added(parts).astype(jnp.bfloat16)


class View:
    def __init__(self, array, start, rows):
        self.array, self.start, self.rows = array, start, rows


def view(value):
    return value if isinstance(value, View) else View(value, 0, value.shape[0])


def sum_many(stacks):
    stacks = [[[view(value) for value in addends] for addends in stack] for stack in stacks]
    rows = stacks[0][0][0].rows
    block = 384 if rows % 384 == 0 else 192 if rows % 192 == 0 else 96
    steps = rows // block
    depth = len(stacks[0])
    arrays, specs, shapes = [], [], []
    for stack in stacks:
        width = stack[0][0].array.shape[1]
        shapes.append(jax.ShapeDtypeStruct((depth * rows, width), jnp.bfloat16))
        for level, addends in enumerate(stack):
            for value in addends:
                first = value.start // block
                arrays.append(value.array)
                specs.append(
                    pl.BlockSpec(
                        (block, width),
                        lambda i, f=first, l=level: (f + jnp.clip(i - l * steps, 0, steps - 1), 0),
                    )
                )

    def kernel(*refs):
        outs = refs[len(arrays) :]
        for level in range(depth):

            @pl.when(pl.program_id(0) // steps == level)
            def _(level=level):
                at = 0
                for out, stack in zip(outs, stacks):
                    for here, addends in enumerate(stack):
                        if here == level:
                            total = refs[at][...].astype(jnp.float32)
                            for extra in range(1, len(addends)):
                                total = total + refs[at + extra][...].astype(jnp.float32)
                            out[...] = total.astype(jnp.bfloat16)
                        at += len(addends)

    return pl.pallas_call(
        kernel,
        grid=(depth * steps,),
        in_specs=specs,
        out_specs=[pl.BlockSpec((block, s.shape[1]), lambda i: (i, 0)) for s in shapes],
        out_shape=shapes,
        compiler_params=pltpu.CompilerParams(vmem_limit_bytes=24 << 20),
        name="sum_many",
    )(*arrays)


def sync(*values):
    return lax.optimization_barrier(values)


def cut(addends, count):
    views = [view(value) for value in addends]
    left = views[0].rows // count
    return [[View(v.array, v.start + i * left, left) for v in views] for i in range(count)]


def swap_pair(value):
    return lax.ppermute(value, "dp", [(i, i ^ 1) for i in range(LINE * PAIR)])


def move_line(value, pairs):
    return lax.ppermute(
        value, "dp", [(a * PAIR + i, b * PAIR + i) for a, b in pairs for i in range(PAIR)]
    )


OUTSIDE = [(0, 1), (1, 0), (2, 3), (3, 2)]


def at_end():
    place = lax.axis_index("dp") // PAIR
    return (place == 0) | (place == LINE - 1)


def line_first(outer):
    return move_line(outer, OUTSIDE)


def move_inside(value):
    experts = lax.axis_size("expert")
    pairs = []
    for place in range(LINE):
        for rest in range(PAIR * experts):
            here = place * PAIR * experts + rest
            there = here ^ 1 if place in (0, LINE - 1) else (LINE - 1 - place) * PAIR * experts + rest
            pairs.append((here, there))
    return lax.ppermute(value, ("dp", "expert"), pairs)


def line_second(outside, inside):
    return move_line(outside, OUTSIDE), move_inside(inside)


def third_parts(inner, outside, inside):
    return jnp.where(at_end(), low(inner), inside), low([*inner, outside])


def line_third(outside, inside):
    return move_line(outside, OUTSIDE), move_inside(inside)


def line_last(own, first, outside, inside):
    return [*own, outside, jnp.where(at_end(), plain(first), inside)]


def line_direct(aways):
    return [
        move_line(away, [(i, (i + ahead) % LINE) for i in range(LINE)])
        for ahead, away in enumerate(aways, 1)
    ]


def swap_both(value, dp_step, expert_step):
    experts = lax.axis_size("expert")
    pairs = [
        (dp * experts + expert, (dp ^ dp_step) * experts + (expert ^ expert_step))
        for dp in range(LINE * PAIR)
        for expert in range(experts)
    ]
    return lax.ppermute(value, ("dp", "expert"), pairs)


def swap_plane(aways):
    return [swap_pair(aways[0]), swap_expert(aways[1], 1), swap_both(aways[2], 1, 2)]


def share_quarters(total):
    return [swap_expert(total, 0), swap_expert(total, 1), swap_expert(total, None)]


def order_quarters(total, cames):
    core, chip, both = cames
    expert = lax.axis_index("expert")
    right, upper = (expert & 1) == 1, (expert >> 1) == 1
    mine = jnp.where(upper, chip, total), jnp.where(upper, total, chip)
    other = jnp.where(upper, both, core), jnp.where(upper, core, both)
    return [
        [jnp.where(right, o, s) for o, s in zip(other, mine)],
        [jnp.where(right, s, o) for o, s in zip(other, mine)],
    ]


def swap_stack(held, bit):
    return jnp.concatenate([held, swap_expert(held, bit)])


def stack_order(held):
    places = [0]
    for bit in reversed(range(bits_of(held.shape[0]))):
        places += [place | (1 << bit) for place in places]
    return jnp.concatenate([held[places.index(r)][None] for r in range(len(places))])


def gather_chips(value):
    parts = {0: value}
    for bit in reversed(range(1, bits_of(lax.axis_size("expert")))):
        for r in list(parts):
            parts[r | (1 << bit)] = swap_expert(parts[r], bit)
    return parts


def rows_to_columns(stacked, count):
    rows = stacked.shape[0] // count
    return jnp.concatenate([stacked[i * rows : (i + 1) * rows] for i in range(count)], axis=1)


def plain(value):
    if isinstance(value, View):
        return value.array[value.start : value.start + value.rows]
    return value


def added(parts):
    total = plain(parts[0]).astype(jnp.float32)
    for part in parts[1:]:
        total = total + plain(part).astype(jnp.float32)
    return total


def scatter_far(parts):
    came = []
    for bit in range(1, bits_of(lax.axis_size("expert"))):
        left = []
        for kept, away in zip(parts[::2], parts[1::2]):
            moved = swap_expert(away, bit)
            if kept is None:
                came.append(moved)
                left.append(None)
            else:
                left.append(added([kept, moved]).astype(jnp.bfloat16))
        parts = left
    return came


def on_device(
    patches,
    time_embed,
    ada_weight,
    ada_bias,
    qkv_weight,
    out_weight,
    up_weight,
    down_weight,
    expert_up,
    expert_down,
    routes,
    gate_weights,
    cotangent,
):
    tokens, width = patches.shape
    latents = time_embed.shape[0]
    seq_len = tokens // latents
    experts = lax.axis_size("expert")
    dp_size = lax.axis_size("dp")
    dp_index = lax.axis_index("dp")
    expert_index = lax.axis_index("expert")
    capacity = 5 * tokens // (2 * experts)

    hidden = up_weight.shape[1]
    blocks = 2
    groups = experts // blocks
    table = shard_table()

    info = jnp.concatenate(
        [
            routes.T.astype(jnp.float32),
            gate_weights.T,
            time_embed.astype(jnp.float32).reshape(-1, tokens),
        ],
        axis=0,
    )
    info = swap_stack(info[None], bits_of(experts) - 1)
    cots = gather_chips(cotangent)
    cots[1] = swap_expert(cotangent, 0)
    for bit in reversed(range(bits_of(experts) - 1)):
        info = swap_stack(info, bit)
    info_all = stack_order(info)
    cond = jax.nn.silu(time_embed.astype(jnp.float32)).astype(jnp.bfloat16)
    modulation = jnp.dot(cond, ada_weight, preferred_element_type=jnp.float32) + ada_bias
    mod = modulation.reshape(latents, 6, width)
    first_in, qkv_all, log_total, attended, attn_proj, second_in = attn_forward(
        patches, mod, qkv_weight, out_weight
    )
    second_in, cots = sync(second_in, cots)

    seconds = gather_chips(second_in)
    seconds[1] = swap_expert(second_in, 0)
    routed = route(
        expert_index[None], info_all[:, :4], info_all[:, 4:].reshape(experts * latents, width),
        ada_weight, ada_bias, tokens,
    )
    routed, seconds[1] = sync(routed, seconds[1])
    for r in range(2, experts, 2):
        cots[r + 1] = swap_expert(cots[r], 0)

    def run_group(group, carried):
        span = range(group * blocks, (group + 1) * blocks)
        results = expert_forward_backward(
            [seconds[r] for r in span], [cots[r] for r in span], *routed, expert_up[0], expert_down[0],
            capacity, groups, group, carried,
        )
        return results[: 4 + blocks], results[4 + blocks :]

    carried, near = run_group(0, [])
    carried, near, seconds, cots = sync(carried, near, seconds, cots)
    for r in range(2, experts, 2):
        seconds[r + 1] = swap_expert(seconds[r], 0)
    near_came = swap_expert(near[1], 0)
    backs = {}
    for group in range(1, groups):
        carried, backs[group] = run_group(group, carried)
    carried, backs, near_came = sync(carried, backs, near_came)
    act_rows, grad_pre_rows, rows_in, grad_rows, mix_even, mix_odd = carried

    fast = tuned(dp_size, experts)
    backs_came = {group: swap_expert(backs[group][1], 0) for group in backs}
    ups, downs, first_downs = (), (), ()
    if fast:
        plan, shapes = expert_down_plan(width, hidden)
        downs = weight_grad(act_rows, grad_rows, table, plan, shapes, [], "grad_expert_down")
    downs, backs_came, rows_in = sync(downs, backs_came, rows_in)
    far = [None] + [low([backs[group][0], backs_came[group]]) for group in range(1, groups)]
    far_sum = scatter_far(far)
    if fast:
        first_downs = line_first(downs[3])
        plan, shapes = expert_up_plan(width, hidden)
        ups = weight_grad(rows_in, grad_pre_rows, table, plan, shapes, [], "grad_expert_up")
    ups, second_in = sync(ups, second_in)

    mix_came = swap_expert(mix_odd, 0)
    if fast:
        up_came = swap_pair(ups[1])
    shared = shared_forward_backward(second_in, cotangent, mod[:, 5], up_weight, down_weight)
    shared, far_sum, mix_came, first_downs = sync(shared, far_sum, mix_came, first_downs)
    shared_act, grad_shared_pre, grad_shared, shared_out, grad_second = shared
    mix = added([mix_even, mix_came])
    mix = scatter_expert([mix[i * tokens : (i + 1) * tokens] for i in range(groups)], 1)
    if fast:
        second_downs = line_second(downs[2], low([downs[2], first_downs]))
        dense_shapes = [(2 * hidden, width // 2)] * 2
        dense = weight_grad(
            second_in, grad_shared_pre, table, dense_up_plan(width, hidden), dense_shapes, [], "grad_up"
        )
        dense = weight_grad(
            shared_act, grad_shared, table, dense_down_plan(width, hidden), dense_shapes, dense,
            "grad_down",
        )
        dense, attn_proj, mix, second_downs, up_came = sync(
            dense, attn_proj, mix, second_downs, up_came
        )
        dense_came = swap_expert(dense[0], 0)
        third = third_parts([downs[1]], *second_downs)
        ups = cut([ups[0], up_came], LINE)
        up_outer = low(ups[3])
        third, up_outer, dense_came, attn_proj = sync(third, up_outer, dense_came, attn_proj)
        third_downs = line_third(*third)
        up_first = line_first(up_outer)
        first, second = cut([dense[1], dense_came], 2)
        first, second = cut(first, 2), cut(second, 2)
        aways = low(first[1]), low(second[1])
        aways, attn_proj = sync(aways, attn_proj)
        first_came = swap_expert(aways[0], 1)
        second_came = swap_pair(aways[1])

    backward = attn_backward(
        patches, mod, attn_proj, qkv_all, log_total, cotangent, out_weight,
        [grad_second, near[0], near_came, *far_sum],
    )
    grad_qkv_rows, grad_attn, grad_middle, grad_mod_early = backward
    if fast:
        tail_shapes = [(4 * width, width // 2)] * 2
        tail = weight_grad(
            first_in, grad_qkv_rows, table, tail_plan(width, 0, 3), tail_shapes, [], "grad_qkv"
        )
        tail = weight_grad(
            attended, grad_attn, table, tail_plan(width, 3, 1), tail_shapes, tail, "grad_out"
        )
        tail, third_downs, first_came, second_came, grad_middle = sync(
            tail, third_downs, first_came, second_came, grad_middle
        )
        tail_came = swap_expert(tail[0], 0)
        second = cut([*second[0], second_came], 2)
        first = cut([*first[0], first_came], 2)
        aways = sum_many([[first[1]], [second[1]]])
        aways, grad_middle = sync(aways, grad_middle)
        first_came = swap_pair(aways[0])
        second_came = swap_expert(aways[1], 1)
        tail_came, grad_middle = sync(tail_came, grad_middle)
        tail_base, *away = cut([tail[1], tail_came], 4)
        away = sum_many([[addends] for addends in away])
        away, grad_middle = sync(away, grad_middle)
    inner = input_backward(patches, mod, grad_qkv_rows, grad_middle, qkv_weight)
    if fast:
        away, inner, mix, first_came, second_came = sync(away, inner, mix, first_came, second_came)
        third_cames = swap_plane(away)
        first = cut([*first[0], first_came], LINE)
        second = cut([*second[0], second_came], LINE)
        aways = sum_many([[f, s] for f, s in zip(first[1:], second[1:])])
        own, away = cut(line_last([downs[0]], first_downs, *third_downs), 2)
        away = low(away)
        aways, away, mix, up_first = sync(aways, away, mix, up_first)
        up_second = sum_many([[ups[2]], [[*ups[2], up_first]]])
        up_second, mix = sync(up_second, mix)
        up_cames = line_second(*up_second)
    grad_input, grad_mod_late = inner

    middle = patches.astype(jnp.float32).reshape(latents, seq_len, width) + mod[
        :, 2:3
    ] * attn_proj.reshape(latents, seq_len, width)
    branch = (shared_out + added(mix)).reshape(latents, seq_len, width)
    block_out = (middle + mod[:, 5:6] * branch).reshape(tokens, width).astype(jnp.bfloat16)
    grad_gate_two = jnp.sum(
        cotangent.astype(jnp.float32).reshape(latents, seq_len, width) * branch, axis=1
    )
    local_counts = jnp.sum(
        (routes[:, :, None] == jnp.arange(experts, dtype=jnp.int32)).astype(jnp.int32),
        axis=(0, 1),
    )
    count_parts = jnp.concatenate([local_counts // 128, local_counts % 128]).astype(jnp.bfloat16)
    count_rows = jnp.zeros((latents, 128), jnp.bfloat16).at[0, : 2 * experts].set(count_parts)
    mods = jnp.concatenate(
        [
            grad_mod_late.reshape(latents, 2 * width).astype(jnp.bfloat16),
            grad_mod_early.reshape(latents, 3 * width).astype(jnp.bfloat16),
            grad_gate_two.astype(jnp.bfloat16),
            cond,
            count_rows,
        ],
        axis=1,
    )

    if fast:
        line_cames = line_direct(aways)
        third_cames, mods, block_out, up_cames = sync(third_cames, mods, block_out, up_cames)
        third = cut([*tail_base, *third_cames], LINE)
        tail_aways = sum_many([[addends] for addends in third[1:]])
        up_third = third_parts(ups[1], *up_cames)
        tail_aways, line_cames[0], mods = sync(tail_aways, line_cames[0], mods)
        third_cames = line_direct(tail_aways)
        mods_all = gather_ordered(mods)
        up_cames = line_third(*up_third)
        third_cames, line_cames, away, mods_all = sync(third_cames, line_cames, away, mods_all)
        down_came = swap_pair(away)
        dense_total = low([jnp.concatenate([added(first[0]), added(second[0])]), *line_cames])
        tail_total = low([*third[0], *third_cames])
        totals = jnp.concatenate([dense_total, tail_total], axis=0)
        totals, mods_all = sync(totals, mods_all)
        cames = share_quarters(totals)
        for bit in range(bits_of(dp_size)):
            mods_all = gather_dp_step(mods_all, bit)
        quarters = order_quarters(totals, cames)
        sum_e_up = rows_to_columns(added(line_last(ups[0], up_first, *up_cames)), hidden // width)
        sum_e_down = added([*own, down_came])
        rows = dense_total.shape[0]
        dense_sums = [jnp.concatenate([q[:rows] for q in chips]) for chips in quarters]
        tail_sums = [jnp.concatenate([q[rows:] for q in chips]) for chips in quarters]

        def columns(arrays):
            return jnp.concatenate(arrays, axis=1).astype(jnp.float32)

        half = hidden // 16
        sum_w_up, sum_w_down = [], []
        for chip in range(2):
            at = 2 * half * chip
            sum_w_up.append(
                columns([rows_to_columns(s[at : at + half], hidden // width) for s in dense_sums])
            )
            sum_w_down.append(columns([s[at + half : at + 2 * half] for s in dense_sums]))
        sum_w_up, sum_w_down = jnp.concatenate(sum_w_up), jnp.concatenate(sum_w_down)
        half = width // 16
        sum_w_qkv, sum_w_out = [], []
        for chip in range(2):
            at = 4 * half * chip
            sum_w_qkv.append(
                columns([rows_to_columns(s[at : at + 3 * half], 3) for s in tail_sums])
            )
            sum_w_out.append(columns([s[at + 3 * half : at + 4 * half] for s in tail_sums]))
        sum_w_qkv, sum_w_out = jnp.concatenate(sum_w_qkv), jnp.concatenate(sum_w_out)
    else:
        mods_all = gather_dp(gather_ordered(mods))

        def summed(left, right, axes):
            share = lax.psum_scatter(
                tn(left, right).astype(jnp.bfloat16), "dp", scatter_dimension=0, tiled=True
            )
            return (lax.psum(share, axes) if axes else share).astype(jnp.float32)

        sum_w_up = summed(second_in, grad_shared_pre, "expert")
        sum_w_down = summed(shared_act, grad_shared, "expert")
        sum_w_qkv = summed(first_in, grad_qkv_rows, "expert")
        sum_w_out = summed(attended, grad_attn, "expert")
        sum_e_up = summed(rows_in, grad_pre_rows, None)
        sum_e_down = summed(act_rows, grad_rows, None)

    grad_mod_all = mods_all[:, : 6 * width]
    count_sums = jnp.sum(mods_all[:, 7 * width :].astype(jnp.float32), axis=0).astype(jnp.int32)
    counts = count_sums[:experts] * 128 + count_sums[experts : 2 * experts]
    ada_rows = width // dp_size
    cond_mine = lax.dynamic_slice_in_dim(
        mods_all[:, 6 * width : 7 * width].T, dp_index * ada_rows, ada_rows, axis=0
    )
    sum_ada = jnp.dot(cond_mine, grad_mod_all, preferred_element_type=jnp.float32)
    bias_all = jnp.sum(grad_mod_all.astype(jnp.float32), axis=0)
    bias_size = bias_all.shape[0] // dp_size
    sum_bias = lax.dynamic_slice_in_dim(bias_all, dp_index * bias_size, bias_size)
    return (
        block_out,
        grad_input,
        sum_ada,
        sum_bias,
        sum_w_qkv,
        sum_w_out,
        sum_w_up,
        sum_w_down,
        sum_e_up[None],
        sum_e_down[None],
        counts,
    )


def solution(mesh):
    in_specs = (
        P(("dp", "expert"), None),
        P(("dp", "expert"), None),
        P(),
        P(),
        P(),
        P(),
        P(),
        P(),
        P("expert", None, None),
        P("expert", None, None),
        P(("dp", "expert"), None),
        P(("dp", "expert"), None),
        P(("dp", "expert"), None),
    )
    out_specs = (
        P(("dp", "expert"), None),
        P(("dp", "expert"), None),
        P("dp", None),
        P("dp"),
        P("dp", None),
        P("dp", None),
        P("dp", None),
        P("dp", None),
        P("expert", "dp", None),
        P("expert", "dp", None),
        P(),
    )
    return jax.shard_map(
        on_device, mesh=mesh, in_specs=in_specs, out_specs=out_specs, check_vma=False
    )
```
